32 devices in a mesh: seq: 16 (over z, y, x), head: 2 (over core).
Axes of the slice: x: 2, y: 2, z: 4, core: 2. Of those that a mesh axis runs over, the one named last changes fastest.
Arguments:
- latents: bfloat16 [2048, 1536], P('seq'), may hold values from -6 to 6
- caption: bfloat16 [512, 4096], P('seq'), may hold values from -6 to 6
- conditioning: bfloat16 [2, 1024], replicated, may hold values from -6 to 6
- clip_frames: int32 [2], replicated, may hold values from 4 to 16, as said below
- valid_patches: int32 [2], replicated, may hold values from 192 to 384, as said below
- query_proj: bfloat16 [1536, 1536], P('seq', 'head'), may hold values from -0.15625 to 0.15625
- key_proj: bfloat16 [1536, 1536], P('seq', 'head'), may hold values from -0.15625 to 0.15625
- value_proj: bfloat16 [1536, 1536], P('seq', 'head'), may hold values from -0.15625 to 0.15625
- output_proj: bfloat16 [1536, 1536], P('head', 'seq'), may hold values from -1.5 to 1.5
- caption_key: bfloat16 [4096, 1536], P('seq', 'head'), may hold values from -0.09375 to 0.09375
- caption_value: bfloat16 [4096, 1536], P('seq', 'head'), may hold values from -0.09375 to 0.09375
- gate_proj: bfloat16 [1536, 4096], P('seq', 'head'), may hold values from -0.15625 to 0.15625
- up_proj: bfloat16 [1536, 4096], P('seq', 'head'), may hold values from -0.15625 to 0.15625
- down_proj: bfloat16 [4096, 1536], P('head', 'seq'), may hold values from -0.09375 to 0.09375
- modulation: bfloat16 [1024, 6144], P('seq'), may hold values from -0.1875 to 0.1875
- query_gain: float32 [64], replicated, may hold values from 0.5 to 1.5
- key_gain: float32 [64], replicated, may hold values from 0.5 to 1.5
- caption_gain: float32 [64], replicated, may hold values from 0.5 to 1.5
- attn_gain: float32 [1536], replicated, may hold values from 0.5 to 1.5
- ffn_gain: float32 [1536], replicated, may hold values from 0.5 to 1.5
- cross_gate: float32 [24], P('head'), may hold values from 0.3 to 1.5
- cotangent: bfloat16 [2048, 1536], P('seq'), may hold values from -6 to 6
Outputs:
- output: bfloat16 [2048, 1536], P('seq')
- grad_latents: bfloat16 [2048, 1536], P('seq')
- grad_query_proj: float32 [1536, 1536], P('seq', 'head')
- grad_key_proj: float32 [1536, 1536], P('seq', 'head')
- grad_value_proj: float32 [1536, 1536], P('seq', 'head')
- grad_output_proj: float32 [1536, 1536], P('head', 'seq')
- grad_caption_key: float32 [4096, 1536], P('seq', 'head')
- grad_caption_value: float32 [4096, 1536], P('seq', 'head')
- grad_gate_proj: float32 [1536, 4096], P('seq', 'head')
- grad_up_proj: float32 [1536, 4096], P('seq', 'head')
- grad_down_proj: float32 [4096, 1536], P('head', 'seq')
- grad_modulation: float32 [1024, 6144], P('seq')
- grad_query_gain: float32 [64], replicated
- grad_key_gain: float32 [64], replicated
- grad_caption_gain: float32 [64], replicated
- grad_attn_gain: float32 [1536], replicated
- grad_ffn_gain: float32 [1536], replicated
- grad_cross_gate: float32 [24], P('head')
The draws below stay inside these ranges and needn't reach their ends.
Inputs may be any that keep to these rules, and one draw needn't show every extreme that they name: `clip_frames`: the clips lie end to end from the first token; their frames together cover more than all 2048 tokens, and the tokens of the last clips that lie past the end do not exist. One of the first two clips has 16 frames and the other 4. In every frame of a clip the first valid_patches of its 384 patch tokens are in use, the rest are padding; the frame's last token is the nextframe token. One of the first two clips uses all 384 and the other 192.
All inputs are finite; a program needn't handle non-finite values.
Results may differ from the reference program's by a relative error of at most 0.02.
Values may be sent and summed in bfloat16 or wider, within the bound.
No kernel may reach another device: no remote copies, remote signals or barrier semaphores. Data moves between devices by JAX's collectives and lax.ppermute only.
A program may use at most 256 MiB of HBM per device.

```python
import math
import jax
import jax.numpy as jnp
from jax import lax

D = 1536
HEADS = 24
HD = 64
FF = 4096
TEXTW = 4096
CONDW = 1024
TEXT = 256
FRAME = 385
FMIN = 4
FMAX = 16
PATCHES = 384
TOKENS = 2048
CLIPS = 2


def draw_clip_frames(key, part):
    base = jax.random.fold_in(key, part)
    pick = jax.random.randint(jax.random.fold_in(base, 101), (), 0, 2)
    frames = jax.random.randint(jax.random.fold_in(base, 102), (CLIPS,), FMIN, FMAX + 1)
    places = jnp.arange(CLIPS)
    frames = jnp.where(places == pick, FMAX, jnp.where(places == 1 - pick, FMIN, frames))
    return frames.astype(jnp.int32)


def draw_valid_patches(key, part):
    base = jax.random.fold_in(key, part)
    pick = jax.random.randint(jax.random.fold_in(base, 201), (), 0, 2)
    counts = jax.random.randint(jax.random.fold_in(base, 202), (CLIPS,), PATCHES // 2, PATCHES + 1)
    places = jnp.arange(CLIPS)
    counts = jnp.where(places == pick, PATCHES, jnp.where(places == 1 - pick, PATCHES // 2, counts))
    return counts.astype(jnp.int32)


def block_levels(rng, dims, cuts, low, largest):
    factor_of = 1.0
    for dim, parts in cuts:
        steps = jax.random.uniform(jax.random.fold_in(jax.random.fold_in(rng, 6), dim), (parts,), jnp.float32, low / len(cuts), largest / len(cuts))
        factor_of = factor_of * jnp.repeat(jnp.exp(steps), dims[dim] // parts).reshape((-1,) + (1,) * (len(dims) - 1 - dim))
    return factor_of


def normal_values(own_key, shape, spread, bound, pieces=(), held_as=jnp.bfloat16):
    values = jax.random.normal(own_key, shape, jnp.float32) * spread
    if len(pieces) > 0:
        values = block_levels(own_key, shape, pieces, -0.22, 0.18) * values
    return jnp.clip(values, min=-bound, max=bound).astype(held_as)


def setup_inputs(seed: int = 0) -> dict:
    seeds = jax.random.split(jax.random.key(seed), 23)
    latents = normal_values(seeds[0], (TOKENS, D), 1.0, 6.0, ((0, 16),))
    caption = normal_values(seeds[1], (CLIPS * TEXT, TEXTW), 1.0, 6.0, ((0, 16),))
    conditioning = normal_values(seeds[2], (CLIPS, CONDW), 1.0, 6.0)
    clip_frames = draw_clip_frames(jax.random.fold_in(seeds[22], 71), 0)
    valid_patches = draw_valid_patches(jax.random.fold_in(seeds[22], 71), 0)
    query_proj = normal_values(seeds[5], (D, D), D ** -0.5, 0.15625, ((0, 16), (1, 2)))
    key_proj = normal_values(seeds[6], (D, D), D ** -0.5, 0.15625, ((0, 16), (1, 2)))
    value_proj = normal_values(seeds[7], (D, D), D ** -0.5, 0.15625, ((0, 16), (1, 2)))
    output_proj = normal_values(seeds[8], (D, D), 16 ** -0.5, 1.5, ((0, 2), (1, 16)))
    caption_key = normal_values(seeds[9], (TEXTW, D), TEXTW ** -0.5, 0.09375, ((0, 16), (1, 2)))
    caption_value = normal_values(seeds[10], (TEXTW, D), TEXTW ** -0.5, 0.09375, ((0, 16), (1, 2)))
    gate_proj = normal_values(seeds[11], (D, FF), D ** -0.5, 0.15625, ((0, 16), (1, 2)))
    up_proj = normal_values(seeds[12], (D, FF), D ** -0.5, 0.15625, ((0, 16), (1, 2)))
    down_proj = normal_values(seeds[13], (FF, D), FF ** -0.5, 0.09375, ((0, 2), (1, 16)))
    modulation = normal_values(seeds[14], (CONDW, 4 * D), CONDW ** -0.5, 0.1875, ((0, 16),))
    query_gain = jnp.clip(1.0 + 0.1 * jax.random.normal(seeds[15], (HD,), jnp.float32), 0.5, 1.5)
    key_gain = jnp.clip(1.0 + 0.1 * jax.random.normal(seeds[16], (HD,), jnp.float32), 0.5, 1.5)
    caption_gain = jnp.clip(1.0 + 0.1 * jax.random.normal(seeds[17], (HD,), jnp.float32), 0.5, 1.5)
    attn_gain = jnp.clip(1.0 + 0.1 * jax.random.normal(seeds[18], (D,), jnp.float32), 0.5, 1.5)
    ffn_gain = jnp.clip(1.0 + 0.1 * jax.random.normal(seeds[19], (D,), jnp.float32), 0.5, 1.5)
    cross_gate = jnp.clip(0.3 + 1.2 * jax.random.uniform(seeds[20], (HEADS,), jnp.float32) ** block_levels(seeds[20], (HEADS,), ((0, 2),), -0.2, 0.2), 0.3, 1.5)
    cotangent = normal_values(seeds[21], (TOKENS, D), 1.0, 6.0, ((0, 16),))
    return dict(latents=latents, caption=caption, conditioning=conditioning, clip_frames=clip_frames, valid_patches=valid_patches, query_proj=query_proj, key_proj=key_proj, value_proj=value_proj, output_proj=output_proj, caption_key=caption_key, caption_value=caption_value, gate_proj=gate_proj, up_proj=up_proj, down_proj=down_proj, modulation=modulation, query_gain=query_gain, key_gain=key_gain, caption_gain=caption_gain, attn_gain=attn_gain, ffn_gain=ffn_gain, cross_gate=cross_gate, cotangent=cotangent)


@jax.custom_vjp
def low(v):
    return lax.optimization_barrier(v.astype(jnp.bfloat16)).astype(jnp.float32)

@jax.custom_vjp
def low_back(v):
    return v

def low_keep(v):
    return (low(v), None)

def low_pass(kept, grad):
    return (grad,)

def back_keep(v):
    return (v, None)

def back_low(kept, grad):
    return (low(grad),)
low.defvjp(low_keep, low_pass)
low_back.defvjp(back_keep, back_low)
EPSILON = 1e-06
HIGHEST = lax.Precision.HIGHEST

def token_layout(clip_frames, valid_patches, first, count):
    clips = clip_frames.shape[0]
    frames = clip_frames.astype(jnp.int32)
    ends = FRAME * jnp.cumsum(frames)
    starts = ends - FRAME * frames
    places = first + jnp.arange(count, dtype=jnp.int32)
    clip_index = lax.optimization_barrier(jnp.sum((ends[None, :] <= places[:, None]).astype(jnp.int32), axis=1))
    chosen = (clip_index[:, None] == jnp.arange(clips, dtype=jnp.int32)[None, :]).astype(jnp.int32)
    position = places - lax.optimization_barrier(jnp.sum(chosen * starts[None, :], axis=1))
    within = position % FRAME
    limit = lax.optimization_barrier(jnp.sum(chosen * valid_patches.astype(jnp.int32)[None, :], axis=1))
    valid = (within < limit) | (within == FRAME - 1)
    tag = jnp.where(valid, clip_index, -1)
    return (clip_index, position, tag)

def rotate(values, position, sign):
    half = values.shape[-1] // 2
    rates = 10000.0 ** (-(jnp.arange(half, dtype=jnp.float32) * 2.0 / values.shape[-1]))
    angle = position.astype(jnp.float32)[:, None] * rates[None, :]
    cosine = jnp.cos(angle)[:, None, :]
    sine = sign * jnp.sin(angle)[:, None, :]
    first = values[..., :half]
    second = values[..., half:]
    return jnp.concatenate([first * cosine - second * sine, first * sine + second * cosine], axis=-1)

def head_norm(values, gain):
    return values * lax.rsqrt(lax.optimization_barrier(jnp.mean(values * values, axis=-1, keepdims=True)) + EPSILON) * gain

def reference(latents, caption, conditioning, clip_frames, valid_patches, query_proj, key_proj, value_proj, output_proj, caption_key, caption_value, gate_proj, up_proj, down_proj, modulation, query_gain, key_gain, caption_gain, attn_gain, ffn_gain, cross_gate, cotangent):
    tokens = latents.shape[0]
    clip_index, position, tag = token_layout(clip_frames, valid_patches, 0, tokens)
    caption_float = caption.astype(jnp.float32)
    silu_cond = low(jax.nn.silu(conditioning.astype(jnp.float32)))
    text_rows = caption.shape[0]
    text_clip = jnp.arange(text_rows, dtype=jnp.int32) // TEXT
    scale = 1.0 / math.sqrt(HD)
    query_block = 128
    blocks = tokens // query_block

    def layer(inputs, query_weight, key_weight, value_weight, output_weight, caption_key_weight, caption_value_weight, gate_weight, up_weight, down_weight, modulation_weight, query_scale, key_scale, caption_scale, attn_scale, ffn_scale, cross_weight):
        shifts = jnp.dot(silu_cond, modulation_weight, precision=HIGHEST)[clip_index]
        scale_attn = shifts[:, :D]
        gate_attn = shifts[:, D:2 * D]
        scale_ffn = shifts[:, 2 * D:3 * D]
        gate_ffn = shifts[:, 3 * D:]
        normed = low(inputs * lax.rsqrt(lax.optimization_barrier(jnp.mean(inputs * inputs, axis=-1, keepdims=True)) + EPSILON) * attn_scale * (1.0 + scale_attn))
        query_raw = low_back(jnp.dot(normed, query_weight, precision=HIGHEST)).reshape(tokens, HEADS, HD)
        key_raw = low_back(jnp.dot(normed, key_weight, precision=HIGHEST)).reshape(tokens, HEADS, HD)
        queries = low(rotate(head_norm(query_raw, query_scale), position, 1.0))
        keys = low(rotate(head_norm(key_raw, key_scale), position, 1.0))
        values = low(low_back(jnp.dot(normed, value_weight, precision=HIGHEST))).reshape(tokens, HEADS, HD)
        caption_raw = low_back(jnp.dot(caption_float, caption_key_weight, precision=HIGHEST)).reshape(text_rows, HEADS, HD)
        caption_keys = low(head_norm(caption_raw, caption_scale))
        caption_values = low(low_back(jnp.dot(caption_float, caption_value_weight, precision=HIGHEST))).reshape(text_rows, HEADS, HD)
        gates = jnp.tanh(cross_weight)[None, :, None]

        def attend(block):
            query_part, clip_part = block
            scores = low_back(jnp.einsum('qhd,khd->hqk', query_part, keys, precision=HIGHEST) * scale)
            weights = jnp.where((clip_part[:, None] == tag[None, :])[None], jnp.exp(scores), 0.0)
            self_out = jnp.einsum('hqk,khd->qhd', low(weights), values, precision=HIGHEST) / lax.optimization_barrier(jnp.sum(weights, axis=-1)).T[:, :, None]
            cross_scores = low_back(jnp.einsum('qhd,khd->hqk', query_part, caption_keys, precision=HIGHEST) * scale)
            cross_weights = jnp.where((clip_part[:, None] == text_clip[None, :])[None], jnp.exp(cross_scores), 0.0)
            cross_out = low_back(jnp.einsum('hqk,khd->qhd', low(cross_weights), caption_values, precision=HIGHEST) / lax.optimization_barrier(jnp.sum(cross_weights, axis=-1)).T[:, :, None])
            return self_out + gates * cross_out
        mixed = lax.map(jax.checkpoint(attend), (queries.reshape(blocks, query_block, HEADS, HD), clip_index.reshape(blocks, query_block)))
        mixed = low(low_back(mixed.reshape(tokens, D)))
        attended = low_back(jnp.dot(mixed, output_weight, precision=HIGHEST))
        hidden = inputs + jnp.tanh(gate_attn) * attended
        ffn_input = low(hidden * lax.rsqrt(lax.optimization_barrier(jnp.mean(hidden * hidden, axis=-1, keepdims=True)) + EPSILON) * ffn_scale * (1.0 + scale_ffn))
        gate_val = low_back(jnp.dot(ffn_input, gate_weight, precision=HIGHEST))
        up_val = low_back(jnp.dot(ffn_input, up_weight, precision=HIGHEST))
        activation = low(jax.nn.silu(gate_val) * up_val)
        ffn_out = low_back(jnp.dot(activation, down_weight, precision=HIGHEST))
        return hidden + jnp.tanh(gate_ffn) * ffn_out
    result, pullback = jax.vjp(layer, latents.astype(jnp.float32), query_proj.astype(jnp.float32), key_proj.astype(jnp.float32), value_proj.astype(jnp.float32), output_proj.astype(jnp.float32), caption_key.astype(jnp.float32), caption_value.astype(jnp.float32), gate_proj.astype(jnp.float32), up_proj.astype(jnp.float32), down_proj.astype(jnp.float32), modulation.astype(jnp.float32), query_gain.astype(jnp.float32), key_gain.astype(jnp.float32), caption_gain.astype(jnp.float32), attn_gain.astype(jnp.float32), ffn_gain.astype(jnp.float32), cross_gate.astype(jnp.float32))
    grads = pullback(cotangent.astype(jnp.float32))
    return (result.astype(jnp.bfloat16), grads[0].astype(jnp.bfloat16), grads[1], grads[2], grads[3], grads[4], grads[5], grads[6], grads[7], grads[8], grads[9], grads[10], grads[11], grads[12], grads[13], grads[14], grads[15], grads[16])
```

```python
import math

import jax
import jax.numpy as jnp
from jax import lax
from jax.sharding import PartitionSpec as P

TEXT = 256
FRAME = 385
GROUPS = 4
EPSILON = 1e-06
LOW = jnp.bfloat16
FULL = jnp.float32


def token_layout(clip_frames, valid_patches, ids):
    clips = clip_frames.shape[0]
    upto = jnp.arange(clips)[None, :] <= jnp.arange(clips)[:, None]
    ends = FRAME * jnp.sum(jnp.where(upto, clip_frames[None, :], 0), axis=1)
    starts = ends - FRAME * clip_frames
    clip = jnp.sum((ends[None, :] <= ids[:, None]).astype(jnp.int32), axis=1)
    chosen = (clip[:, None] == jnp.arange(clips, dtype=jnp.int32)[None, :]).astype(jnp.int32)
    position = ids - jnp.sum(chosen * starts[None, :], axis=1)
    within = position % FRAME
    limit = jnp.sum(chosen * valid_patches[None, :], axis=1)
    tag = jnp.where((within < limit) | (within == FRAME - 1), clip, -1)
    return clip, position, tag


def rotate(values, cosine, sine):
    half = values.shape[-1] // 2
    first, second = values[..., :half], values[..., half:]
    return jnp.concatenate([first * cosine - second * sine, first * sine + second * cosine], -1)


def inverse_rms(values):
    return lax.rsqrt(jnp.mean(values * values, axis=-1, keepdims=True) + EPSILON)


def norm_back(raw, gain, grad):
    inverse = inverse_rms(raw)
    unit = raw * inverse
    scaled = grad * gain
    back = inverse * (scaled - unit * jnp.mean(scaled * unit, axis=-1, keepdims=True))
    return back, grad * unit


def dot(left, right, contract=(1, 0)):
    dims = (((contract[0],), (contract[1],)), ((), ()))
    return lax.dot_general(left, right, dims, preferred_element_type=FULL)


def by_clip(table, clip):
    out = table[0][None]
    for k in range(1, table.shape[0]):
        out = jnp.where(clip[:, None] == k, table[k][None], out)
    return out


def clip_sums(values, clip, clips):
    return jnp.stack(
        [jnp.sum(jnp.where(clip[:, None] == k, values, 0.0), axis=0) for k in range(clips)]
    )


def xor_order(blocks, index):
    blocks = list(blocks)
    bit = 1
    while bit < len(blocks):
        on = (index & bit) != 0
        blocks = [jnp.where(on, blocks[j ^ bit], blocks[j]) for j in range(len(blocks))]
        bit *= 2
    return blocks


def pick(stack, index, axis=0):
    return lax.dynamic_index_in_dim(stack, index, axis, keepdims=False)


def make_body(seq_size):
    inner = seq_size // GROUPS

    def hop_outer(x, t):
        pairs = [(i, ((i // inner) ^ t) * inner + i % inner) for i in range(seq_size)]
        return lax.ppermute(x, "seq", pairs)

    def hop_inner(x, t):
        pairs = [(i, (i // inner) * inner + ((i % inner) ^ t)) for i in range(seq_size)]
        return lax.ppermute(x, "seq", pairs)

    def hop_core(x):
        return lax.ppermute(x, "head", [(0, 1), (1, 0)])

    def gather_outer(x):
        return [x] + [hop_outer(x, t) for t in range(1, GROUPS)]

    def gather_inner(x):
        return [x] + [hop_inner(x, t) for t in range(1, inner)]

    def gather_tokens(x):
        near = jnp.concatenate(gather_outer(x))
        return jnp.concatenate([near, hop_core(near)])

    def scatter_tokens(partial):
        half = partial.shape[0] // 2
        near = partial[:half] + hop_core(partial[half:].astype(LOW)).astype(FULL)
        parts = near.reshape(GROUPS, half // GROUPS, near.shape[-1])
        total = parts[0]
        for t in range(1, GROUPS):
            total = total + hop_outer(parts[t].astype(LOW), t).astype(FULL)
        return total

    def scatter_inner(parts):
        total = parts[0]
        for t in range(1, inner):
            total = total + hop_inner(parts[t].astype(LOW), t).astype(FULL)
        return total

    def body(
        latents,
        caption,
        conditioning,
        clip_frames,
        valid_patches,
        query_proj,
        key_proj,
        value_proj,
        output_proj,
        caption_key,
        caption_value,
        gate_proj,
        up_proj,
        down_proj,
        modulation,
        query_gain,
        key_gain,
        caption_gain,
        attn_gain,
        ffn_gain,
        cross_gate,
        cotangent,
    ):
        rows, width = latents.shape
        half = rows // 2
        hd = query_gain.shape[0]
        heads = cross_gate.shape[0] // GROUPS
        inner_width = heads * hd
        clips = conditioning.shape[0]
        scale = 1.0 / math.sqrt(hd)
        seq = lax.axis_index("seq")
        core = lax.axis_index("head")
        o, p = seq // inner, seq % inner
        group_rows = GROUPS * rows

        def token_ids(plane):
            c_at = core ^ jnp.arange(2)[:, None, None]
            o_at = o ^ jnp.arange(GROUPS)[None, :, None]
            at = jnp.arange(half)[None, None, :]
            return ((o_at * inner + plane) * rows + c_at * half + at).reshape(-1).astype(jnp.int32)

        ids = token_ids(p)
        key_ids = jnp.concatenate([token_ids(p ^ t) for t in range(inner)])
        clip, position, _ = token_layout(clip_frames, valid_patches, ids)
        _, _, tag = token_layout(clip_frames, valid_patches, key_ids)
        own_clip = clip[:half]

        own = lax.dynamic_slice_in_dim(latents, core * half, half, 0)
        own_cot = lax.dynamic_slice_in_dim(cotangent, core * half, half, 0)
        group_latents = gather_tokens(own).astype(FULL)

        silu_cond = jax.nn.silu(conditioning.astype(FULL)).astype(LOW)
        cond_rows = modulation.shape[0]
        silu_own = lax.dynamic_slice_in_dim(silu_cond, seq * cond_rows, cond_rows, 1)
        shifts = dot(silu_own, modulation)
        shifts = sum(gather_outer(shifts))
        shifts = sum(gather_inner(shifts))
        scale_attn, gate_attn, scale_ffn, gate_ffn = [
            shifts[:, k * width : (k + 1) * width] for k in range(4)
        ]
        first_table = attn_gain * (1.0 + scale_attn)
        second_table = ffn_gain * (1.0 + scale_ffn)
        attn_tanh_table = jnp.tanh(gate_attn)
        ffn_tanh_table = jnp.tanh(gate_ffn)

        def collect(parts):
            piece = parts[0].shape[0]
            send = jnp.concatenate([w.reshape(piece, GROUPS, -1) for w in parts], axis=-1)
            got = [pick(send, o, 1)]
            got += [hop_outer(pick(send, o ^ t, 1), t) for t in range(1, GROUPS)]
            mine = jnp.stack(xor_order(got, o))
            blocks = jnp.stack(xor_order(gather_inner(mine), p), axis=1)
            return blocks.reshape(seq_size * piece, -1)

        attn_weights = collect((query_proj, key_proj, value_proj, output_proj.T))
        ffn_weights = collect((gate_proj, up_proj, down_proj.T))
        qkv = attn_weights[:, : 3 * inner_width]
        out_t = attn_weights[:, 3 * inner_width :]
        hidden_width = ffn_weights.shape[1] // 3
        gate_up = ffn_weights[:, : 2 * hidden_width]
        down_t = ffn_weights[:, 2 * hidden_width :]

        text_own = caption.shape[0]
        cap_cols = caption.shape[1] // seq_size
        cap_split = caption.reshape(text_own, GROUPS, inner, cap_cols)
        cap = [pick(cap_split, o, 1)]
        cap += [hop_outer(pick(cap_split, o ^ t, 1), t) for t in range(1, GROUPS)]
        cap = jnp.concatenate(cap)
        got = [pick(cap, p, 1)]
        got += [hop_inner(pick(cap, p ^ t, 1), t) for t in range(1, inner)]
        cap_mine = jnp.concatenate(got)
        text_group = GROUPS * text_own
        cap_part = jnp.concatenate([dot(cap_mine, caption_key), dot(cap_mine, caption_value)], 1)
        cap_sum = scatter_inner(
            [cap_part[t * text_group : (t + 1) * text_group] for t in range(inner)]
        )
        cap_sum = cap_sum.reshape(GROUPS, text_own, 2, GROUPS, inner_width)
        cap_raw = pick(cap_sum, o, 3)
        for t in range(1, GROUPS):
            sent = jnp.stack([pick(cap_sum[j ^ t], o ^ t, 2) for j in range(GROUPS)])
            cap_raw = cap_raw + hop_outer(sent.astype(LOW), t).astype(FULL)
        cap_raw = cap_raw.reshape(text_group, 2, inner_width)
        cap_key_raw = cap_raw[:, 0].reshape(text_group, heads, hd)
        cap_keys_own = (cap_key_raw * inverse_rms(cap_key_raw) * caption_gain).astype(LOW)
        cap_both = jnp.concatenate(
            [cap_keys_own.reshape(text_group, inner_width), cap_raw[:, 1].astype(LOW)], axis=1
        )
        cap_both = jnp.concatenate(gather_inner(cap_both))
        text_rows = cap_both.shape[0]
        cap_keys = cap_both[:, :inner_width].reshape(text_rows, heads, hd)
        cap_values = cap_both[:, inner_width:].reshape(text_rows, heads, hd)
        p_at = p ^ jnp.arange(inner)[:, None, None]
        o_at = o ^ jnp.arange(GROUPS)[None, :, None]
        text_ids = (o_at * inner + p_at) * text_own + jnp.arange(text_own)[None, None, :]
        text_clip = (text_ids // TEXT).reshape(-1)

        first_mult = by_clip(first_table, clip)
        normed = (group_latents * inverse_rms(group_latents) * first_mult).astype(LOW)
        raw = dot(normed, qkv)
        query_raw = raw[:, :inner_width].reshape(group_rows, heads, hd)
        key_raw = raw[:, inner_width : 2 * inner_width].reshape(group_rows, heads, hd)
        values_own = raw[:, 2 * inner_width :].astype(LOW)
        rates = 10000.0 ** (-(jnp.arange(hd // 2, dtype=FULL) * 2.0 / hd))
        angle = position.astype(FULL)[:, None] * rates[None, :]
        cosine, sine = jnp.cos(angle)[:, None, :], jnp.sin(angle)[:, None, :]
        queries = rotate(query_raw * inverse_rms(query_raw) * query_gain, cosine, sine).astype(LOW)
        keys_own = rotate(key_raw * inverse_rms(key_raw) * key_gain, cosine, sine).astype(LOW)
        both = jnp.concatenate([keys_own.reshape(group_rows, inner_width), values_own], axis=1)
        both = jnp.concatenate(gather_inner(both))
        keys = both[:, :inner_width].reshape(-1, heads, hd)
        values = both[:, inner_width:].reshape(-1, heads, hd)

        gate_here = pick(cross_gate.reshape(GROUPS, heads), o)
        cross_tanh = jnp.tanh(gate_here)

        def weights_of(key_heads, allowed):
            scores = jnp.einsum("qhd,khd->hqk", queries, key_heads, preferred_element_type=FULL)
            return jnp.where(allowed[None], jnp.exp(scores * scale), 0.0)

        def average(weights, value_heads):
            total = jnp.sum(weights, axis=-1)
            out = jnp.einsum(
                "hqk,khd->qhd", weights.astype(LOW), value_heads, preferred_element_type=FULL
            )
            return out / total.T[:, :, None], total

        self_weights = weights_of(keys, clip[:, None] == tag[None, :])
        cross_weights = weights_of(cap_keys, clip[:, None] == text_clip[None, :])
        self_out, self_total = average(self_weights, values)
        cross_out, cross_total = average(cross_weights, cap_values)
        gates = cross_tanh[None, :, None]
        mixed = (self_out + gates * cross_out).astype(LOW).reshape(group_rows, inner_width)
        attended = scatter_tokens(dot(mixed, out_t, (1, 1)))

        inputs = own.astype(FULL)
        upstream = own_cot.astype(FULL)
        attn_tanh = by_clip(attn_tanh_table, own_clip)
        hidden = inputs + attn_tanh * attended
        second_mult = by_clip(second_table, own_clip)
        ffn_own = (hidden * inverse_rms(hidden) * second_mult).astype(LOW)
        ffn_tanh = by_clip(ffn_tanh_table, own_clip)
        d_ffn = gather_tokens((ffn_tanh * upstream).astype(LOW))
        ffn_input = gather_tokens(ffn_own)
        gate_up_val = dot(ffn_input, gate_up)
        gate_val, up_val = gate_up_val[:, :hidden_width], gate_up_val[:, hidden_width:]
        sigma = jax.nn.sigmoid(gate_val)
        activation = (gate_val * sigma * up_val).astype(LOW)
        d_act = dot(d_ffn, down_t)
        d_gate = (d_act * up_val * sigma * (1.0 + gate_val * (1.0 - sigma))).astype(LOW)
        d_up = (d_act * gate_val * sigma).astype(LOW)
        d_gate_up = jnp.concatenate([d_gate, d_up], axis=1)
        d_ffn_input = scatter_tokens(dot(d_gate_up, gate_up, (1, 1)))
        ffn_out = scatter_tokens(dot(activation, down_t, (1, 1)))
        output = (hidden + ffn_tanh * ffn_out).astype(LOW)

        def reduce_matrix(partial, out_widths):
            columns = partial.shape[1]
            parts = partial.reshape(GROUPS, inner, -1, columns)
            total = scatter_inner([pick(parts, p ^ t if t else p, 1) for t in range(inner)])
            got = [pick(total, o)]
            got += [
                hop_outer(pick(total, o ^ t).astype(LOW), t).astype(FULL) for t in range(1, GROUPS)
            ]
            stacked = jnp.stack(xor_order(got, o), axis=1)
            outs, at = [], 0
            for w in out_widths:
                outs.append(stacked[:, :, at : at + w].reshape(stacked.shape[0], -1))
                at += w
            return outs

        ffn_grads = jnp.concatenate(
            [dot(ffn_input, d_gate_up, (0, 0)), dot(d_ffn, activation, (0, 0))], axis=1
        )
        grad_gate, grad_up, grad_down_t = reduce_matrix(ffn_grads, (hidden_width,) * 3)

        second_back, second_terms = norm_back(hidden, second_mult, d_ffn_input)
        ffn_gain_part = jnp.sum(second_terms * (1.0 + by_clip(scale_ffn, own_clip)), axis=0)
        d_hidden = upstream + second_back
        d_attended_own = (attn_tanh * d_hidden).astype(LOW)
        d_attended = gather_tokens(d_attended_own)

        d_mixed = dot(d_attended, out_t).astype(LOW).reshape(group_rows, heads, hd)
        grad_out_t = dot(d_attended, mixed, (0, 0))
        d_mixed_f = d_mixed.astype(FULL)
        cross_gate_part = jnp.sum(d_mixed_f * cross_out, axis=(0, 2)) * (1 - cross_tanh**2)
        d_cross = (gates * d_mixed_f).astype(LOW)

        def attend_back(weights, total, grad, out, key_heads, value_heads):
            prob = weights / total[:, :, None]
            delta = jnp.sum(grad.astype(FULL) * out, axis=-1).T
            d_prob = jnp.einsum("qhd,khd->hqk", grad, value_heads, preferred_element_type=FULL)
            ds = (prob * (d_prob - delta[:, :, None])).astype(LOW)
            dq = jnp.einsum("hqk,khd->qhd", ds, key_heads, preferred_element_type=FULL) * scale
            dk = jnp.einsum("hqk,qhd->khd", ds, queries, preferred_element_type=FULL) * scale
            dv = jnp.einsum("hqk,qhd->khd", prob.astype(LOW), grad, preferred_element_type=FULL)
            flat = lambda x: x.reshape(x.shape[0], inner_width)
            return dq, jnp.concatenate([flat(dk), flat(dv)], axis=1)

        dq_cross, cap_back = attend_back(
            cross_weights, cross_total, d_cross, cross_out, cap_keys, cap_values
        )
        dq_self, kv_back = attend_back(self_weights, self_total, d_mixed, self_out, keys, values)
        kv_back = scatter_inner(
            [kv_back[t * group_rows : (t + 1) * group_rows] for t in range(inner)]
        )
        cap_back = scatter_inner(
            [cap_back[t * text_group : (t + 1) * text_group] for t in range(inner)]
        )

        d_cap_raw, cap_terms = norm_back(
            cap_key_raw, caption_gain, cap_back[:, :inner_width].reshape(text_group, heads, hd)
        )
        d_cap = jnp.concatenate(
            [d_cap_raw.reshape(text_group, inner_width), cap_back[:, inner_width:]], axis=1
        ).astype(LOW)
        got = [d_cap]
        for t in range(1, GROUPS):
            other = hop_outer(d_cap, t).reshape(GROUPS, text_own, -1)
            got.append(jnp.concatenate([other[j ^ t] for j in range(GROUPS)]))
        d_cap = jnp.stack(xor_order(got, o), axis=1)
        d_cap = jnp.concatenate(
            [d_cap[:, :, :inner_width].reshape(text_group, -1), d_cap[:, :, inner_width:].reshape(text_group, -1)],
            axis=1,
        )
        d_cap = jnp.concatenate(gather_inner(d_cap))
        grad_cap = dot(cap_mine, d_cap, (0, 0))
        cap_width = caption_key.shape[1]

        d_query_raw, query_terms = norm_back(
            query_raw, query_gain, rotate(dq_self + dq_cross, cosine, -sine)
        )
        d_key = kv_back[:, :inner_width].reshape(group_rows, heads, hd)
        d_key_raw, key_terms = norm_back(key_raw, key_gain, rotate(d_key, cosine, -sine))
        d_qkv = jnp.concatenate(
            [
                d_query_raw.reshape(group_rows, inner_width),
                d_key_raw.reshape(group_rows, inner_width),
                kv_back[:, inner_width:],
            ],
            axis=1,
        ).astype(LOW)
        d_normed = scatter_tokens(dot(d_qkv, qkv, (1, 1)))
        attn_grads = jnp.concatenate([dot(normed, d_qkv, (0, 0)), grad_out_t], axis=1)
        grad_query, grad_key, grad_value, grad_output_t = reduce_matrix(
            attn_grads, (inner_width,) * 4
        )

        own_mult = by_clip(first_table, own_clip)
        first_back, first_terms = norm_back(inputs, own_mult, d_normed)
        grad_latents = (d_hidden + first_back).astype(LOW)
        attn_gain_part = jnp.sum(first_terms * (1.0 + by_clip(scale_attn, own_clip)), axis=0)

        token_grads = jnp.concatenate(
            [
                first_terms * attn_gain,
                d_hidden * attended * (1.0 - attn_tanh * attn_tanh),
                second_terms * ffn_gain,
                upstream * ffn_out * (1.0 - ffn_tanh * ffn_tanh),
            ],
            axis=1,
        )
        gate_slots = jnp.arange(2 * GROUPS) == core * GROUPS + o
        small = [
            clip_sums(token_grads, own_clip, clips).reshape(-1),
            attn_gain_part,
            ffn_gain_part,
            jnp.sum(query_terms, axis=(0, 1)),
            jnp.sum(key_terms, axis=(0, 1)),
            jnp.sum(cap_terms, axis=(0, 1)),
            jnp.where(gate_slots[:, None], cross_gate_part[None, :], 0.0).reshape(-1),
        ]
        sizes = [x.shape[0] for x in small]
        small = jnp.concatenate(small)
        small = small + hop_core(small)
        small = sum(xor_order(gather_outer(small), o))
        small = sum(xor_order(gather_inner(small), p))
        pieces, at = [], 0
        for n in sizes:
            pieces.append(small[at : at + n])
            at += n
        shift_grad, g_attn, g_ffn, g_query, g_key, g_cap, g_cross = pieces
        shift_grad = shift_grad.reshape(clips, 4 * width)
        g_cross = pick(g_cross.reshape(2, -1), core)
        silu_f = silu_own.astype(FULL)
        grad_modulation = sum(silu_f[k][:, None] * shift_grad[k][None, :] for k in range(clips))

        def whole_rows(x):
            both = jnp.stack([x, hop_core(x)])
            return jnp.concatenate([pick(both, core), pick(both, 1 - core)])

        return (
            whole_rows(output),
            whole_rows(grad_latents),
            grad_query,
            grad_key,
            grad_value,
            grad_output_t.T,
            grad_cap[:, :cap_width],
            grad_cap[:, cap_width:],
            grad_gate,
            grad_up,
            grad_down_t.T,
            grad_modulation,
            g_query,
            g_key,
            g_cap,
            g_attn,
            g_ffn,
            g_cross,
        )

    return body


def solution(mesh):
    rows, cols, turned = P("seq", None), P("seq", "head"), P("head", "seq")
    one = P()
    placed = (rows, rows, one, one, one, cols, cols, cols, turned, cols, cols, cols, cols, turned)
    placed += (rows, one, one, one, one, one, P("head"), rows)
    given = (rows, rows, cols, cols, cols, turned, cols, cols, cols, cols, turned, rows)
    given += (one, one, one, one, one, P("head"))
    return jax.shard_map(
        make_body(mesh.shape["seq"]), mesh=mesh, in_specs=placed, out_specs=given, check_vma=False
    )
```

```python
import math

import jax
import jax.numpy as jnp
from jax import lax
from jax.experimental import pallas as pl
from jax.experimental.pallas import tpu as pltpu
from jax.sharding import PartitionSpec as P

TEXT = 256
FRAME = 385
GROUPS = 4
EPSILON = 1e-06
LOW = jnp.bfloat16
FULL = jnp.float32


def token_layout(clip_frames, valid_patches, ids):
    clips = clip_frames.shape[0]
    upto = jnp.arange(clips)[None, :] <= jnp.arange(clips)[:, None]
    ends = FRAME * jnp.sum(jnp.where(upto, clip_frames[None, :], 0), axis=1)
    starts = ends - FRAME * clip_frames
    clip = jnp.sum((ends[None, :] <= ids[:, None]).astype(jnp.int32), axis=1)
    chosen = (clip[:, None] == jnp.arange(clips, dtype=jnp.int32)[None, :]).astype(jnp.int32)
    position = ids - jnp.sum(chosen * starts[None, :], axis=1)
    within = position % FRAME
    limit = jnp.sum(chosen * valid_patches[None, :], axis=1)
    tag = jnp.where((within < limit) | (within == FRAME - 1), clip, -1)
    return clip, position, tag


def inverse_rms(values, axis=-1):
    return lax.rsqrt(jnp.mean(values * values, axis=axis, keepdims=True) + EPSILON)


def norm_back(raw, gain, grad, axis=-1):
    inverse = inverse_rms(raw, axis)
    unit = raw * inverse
    scaled = grad * gain
    back = inverse * (scaled - unit * jnp.mean(scaled * unit, axis=axis, keepdims=True))
    return back, grad * unit


def dot(left, right, contract=(1, 0)):
    dims = (((contract[0],), (contract[1],)), ((), ()))
    return lax.dot_general(left, right, dims, preferred_element_type=FULL)


def by_clip(table, clip):
    out = table[0][None]
    for k in range(1, table.shape[0]):
        out = jnp.where(clip[:, None] == k, table[k][None], out)
    return out


def clip_sums(values, clip, clips):
    return jnp.stack(
        [jnp.sum(jnp.where(clip[:, None] == k, values, 0.0), axis=0) for k in range(clips)]
    )


def xor_order(blocks, index):
    blocks = list(blocks)
    bit = 1
    while bit < len(blocks):
        on = (index & bit) != 0
        blocks = [jnp.where(on, blocks[j ^ bit], blocks[j]) for j in range(len(blocks))]
        bit *= 2
    return blocks


def pick(stack, index, axis=0):
    return lax.dynamic_index_in_dim(stack, index, axis, keepdims=False)


def low_round(x):
    return lax.reduce_precision(x, 8, 7)


def two_parts(x):
    upper = low_round(x)
    return jnp.stack([upper, low_round(x - upper)]).astype(LOW)


def one_part(x):
    return x[0].astype(FULL) + x[1].astype(FULL)


def chunk_of(keys):
    return 512 if keys % 512 == 0 else keys


def kernel_call(body, ins, outs, flops, scratch=()):
    space = pl.BlockSpec(memory_space=pltpu.VMEM)
    size = sum(x.size * x.dtype.itemsize for x in ins)
    return pl.pallas_call(
        body,
        out_shape=outs,
        in_specs=[space] * len(ins),
        out_specs=[space] * len(outs),
        scratch_shapes=list(scratch),
        compiler_params=pltpu.CompilerParams(vmem_limit_bytes=56 << 20),
        cost_estimate=pl.CostEstimate(flops=flops, bytes_accessed=size, transcendentals=flops // 256),
    )(*ins)


def project(raw, gain_q, gain_k, cosine, sine, heads):
    hd = gain_q.shape[0]
    half, width, rows = hd // 2, heads * hd, raw.shape[1]
    scale = 1.0 / math.sqrt(hd)

    def body(raw_ref, gq_ref, gk_ref, cos_ref, sin_ref, q_ref, kv_ref):
        c, s = cos_ref[...], sin_ref[...]
        for part, gain_ref, out_ref in ((0, gq_ref, q_ref), (1, gk_ref, kv_ref)):
            for h in range(heads):
                u = raw_ref[pl.ds(part * width + h * hd, hd), :]
                n = u * inverse_rms(u, 0) * gain_ref[...]
                a, b = n[:half], n[half:]
                turned = jnp.concatenate([a * c - b * s, a * s + b * c], axis=0).astype(LOW)
                if part == 0:
                    turned = (turned.astype(FULL) * scale).astype(LOW)
                out_ref[pl.ds(h * hd, hd), :] = turned
        kv_ref[pl.ds(width, width), :] = raw_ref[pl.ds(2 * width, width), :].astype(LOW)

    outs = (jax.ShapeDtypeStruct((width, rows), LOW), jax.ShapeDtypeStruct((2 * width, rows), LOW))
    return kernel_call(body, (raw, gain_q, gain_k, cosine, sine), outs, raw.size * 16)


def project_back(raw, gain_q, gain_k, cosine, sine, heads, dq_self, dq_cross, kv_near, kv_far):
    hd = gain_q.shape[0]
    half, width, rows = hd // 2, heads * hd, raw.shape[1]

    def body(raw_ref, gq_ref, gk_ref, cos_ref, sin_ref, a_ref, b_ref, n_ref, f_ref, out_ref, tq, tk):
        c, s = cos_ref[...], sin_ref[...]
        for part, gain_ref, term_ref in ((0, gq_ref, tq), (1, gk_ref, tk)):
            terms = jnp.zeros((hd, rows), FULL)
            for h in range(heads):
                at = pl.ds(h * hd, hd)
                if part == 0:
                    grad = a_ref[at, :] + b_ref[at, :]
                else:
                    grad = n_ref[at, :] + f_ref[at, :].astype(FULL)
                x, y = grad[:half], grad[half:]
                grad = jnp.concatenate([x * c + y * s, y * c - x * s], axis=0)
                where = pl.ds(part * width + h * hd, hd)
                back, term = norm_back(raw_ref[where, :], gain_ref[...], grad, 0)
                out_ref[where, :] = back.astype(LOW)
                terms = terms + term
            term_ref[...] = jnp.sum(terms, axis=1, keepdims=True)
        at = pl.ds(width, width)
        out_ref[pl.ds(2 * width, width), :] = (n_ref[at, :] + f_ref[at, :].astype(FULL)).astype(LOW)

    one = jax.ShapeDtypeStruct((hd, 1), FULL)
    outs = (jax.ShapeDtypeStruct((3 * width, rows), LOW), one, one)
    ins = (raw, gain_q, gain_k, cosine, sine, dq_self, dq_cross, kv_near, kv_far)
    return kernel_call(body, ins, outs, raw.size * 32)


def project_caption(parts, gain, heads):
    hd = gain.shape[0]
    width, rows = heads * hd, parts[0].shape[1]

    def body(*refs):
        part_refs, gain_ref, out_ref, raw_ref = refs[:-3], refs[-3], refs[-2], refs[-1]
        total = part_refs[0][...]
        for ref in part_refs[1:]:
            total = total + ref[...].astype(FULL)
        raw_ref[...] = total[:width]
        for h in range(heads):
            u = total[h * hd : (h + 1) * hd]
            out_ref[pl.ds(h * hd, hd), :] = (u * inverse_rms(u, 0) * gain_ref[...]).astype(LOW)
        out_ref[pl.ds(width, width), :] = total[width:].astype(LOW)

    outs = (jax.ShapeDtypeStruct((2 * width, rows), LOW), jax.ShapeDtypeStruct((width, rows), FULL))
    return kernel_call(body, (*parts, gain), outs, parts[0].size * 16)


def project_caption_back(raw, gain, heads, near, far):
    hd = gain.shape[0]
    width, rows = raw.shape

    def body(raw_ref, gain_ref, n_ref, f_ref, out_ref, term_ref):
        total = n_ref[...] + f_ref[...].astype(FULL)
        terms = jnp.zeros((hd, rows), FULL)
        for h in range(heads):
            at = slice(h * hd, (h + 1) * hd)
            back, term = norm_back(raw_ref[at, :], gain_ref[...], total[at], 0)
            out_ref[at, :] = back.astype(LOW)
            terms = terms + term
        term_ref[...] = jnp.sum(terms, axis=1, keepdims=True)
        out_ref[width:, :] = total[width:].astype(LOW)

    outs = (jax.ShapeDtypeStruct((2 * width, rows), LOW), jax.ShapeDtypeStruct((hd, 1), FULL))
    return kernel_call(body, (raw, gain, near, far), outs, raw.size * 32)


def attend(query, clip, kvs, tags, heads, gates=None, other=None):
    width, rows = query.shape
    hd = width // heads
    n = len(kvs)

    def body(*refs):
        q_ref, clip_ref = refs[:2]
        kv_refs, tag_refs = refs[2 : 2 + n], refs[2 + n : 2 + 2 * n]
        rest = refs[2 + 2 * n :]
        if gates is not None:
            gate_ref, other_ref, out_ref, inv_ref, mix_ref = rest
        else:
            out_ref, inv_ref = rest
        here = clip_ref[...]
        sums = [(jnp.zeros((1, rows), FULL), jnp.zeros((hd, rows), FULL)) for _ in range(heads)]
        for kv_ref, tag_ref in zip(kv_refs, tag_refs):
            count = chunk_of(kv_ref.shape[1])

            def chunk(i, carry):
                at = pl.ds(pl.multiple_of(i * count, count), count)
                allowed = tag_ref[at, :] == here
                out = []
                for h in range(heads):
                    total, acc = carry[h]
                    key = kv_ref[pl.ds(h * hd, hd), at]
                    value = kv_ref[pl.ds(width + h * hd, hd), at]
                    scores = dot(key, q_ref[pl.ds(h * hd, hd), :], (0, 0))
                    weights = jnp.where(allowed, jnp.exp(scores), 0.0)
                    total = total + jnp.sum(weights, axis=0, keepdims=True)
                    out.append((total, acc + dot(value, weights.astype(LOW))))
                return out

            sums = lax.fori_loop(0, kv_ref.shape[1] // count, chunk, sums)
        for h in range(heads):
            total, acc = sums[h]
            inverse = 1.0 / total
            inv_ref[pl.ds(h, 1), :] = inverse
            out_ref[pl.ds(h * hd, hd), :] = acc * inverse
            if gates is not None:
                own = pl.ds(h * hd, hd)
                mix_ref[own, :] = (other_ref[own, :] + gate_ref[own, :] * (acc * inverse)).astype(LOW)

    keys = sum(x.shape[1] for x in kvs)
    ins = (query, clip, *kvs, *tags)
    outs = (jax.ShapeDtypeStruct((width, rows), FULL), jax.ShapeDtypeStruct((heads, rows), FULL))
    if gates is not None:
        ins += (gates, other)
        outs += (jax.ShapeDtypeStruct((width, rows), LOW),)
    return kernel_call(body, ins, outs, 4 * width * rows * keys)


def attend_back(query, clip, kvs, tags, heads, inverse, grad, out, gates=None):
    width, rows = query.shape
    hd = width // heads
    n = len(kvs)
    scale = 1.0 / math.sqrt(hd)

    def body(*refs):
        q_ref, clip_ref, inv_ref, given_ref, o_ref = refs[:5]
        kv_refs, tag_refs = refs[5 : 5 + n], refs[5 + n : 5 + 2 * n]
        here = clip_ref[...]
        if gates is None:
            dq_ref, back_refs = refs[5 + 2 * n], refs[6 + 2 * n :]
            grad_ref = given_ref
        else:
            gate_ref, dq_ref, back_refs = refs[5 + 2 * n], refs[6 + 2 * n], refs[7 + 2 * n :]
            back_refs, sum_ref, grad_ref = back_refs[:n], back_refs[n], back_refs[n + 1]
        deltas = []
        for h in range(heads):
            own = pl.ds(h * hd, hd)
            if gates is not None:
                given = given_ref[own, :].astype(FULL)
                grad_ref[own, :] = (gate_ref[own, :] * given).astype(LOW)
                sum_ref[pl.ds(h, 1), :] = jnp.sum(given * o_ref[own, :], axis=0, keepdims=True)
            terms = grad_ref[own, :].astype(FULL) * o_ref[own, :]
            deltas.append(jnp.sum(terms, axis=0, keepdims=True))
        sums = [jnp.zeros((hd, rows), FULL) for _ in range(heads)]
        for kv_ref, tag_ref, back_ref in zip(kv_refs, tag_refs, back_refs):
            count = chunk_of(kv_ref.shape[1])

            def chunk(i, carry):
                at = pl.ds(pl.multiple_of(i * count, count), count)
                allowed = tag_ref[at, :] == here
                out = []
                for h in range(heads):
                    own = pl.ds(h * hd, hd)
                    key = kv_ref[own, at]
                    value = kv_ref[pl.ds(width + h * hd, hd), at]
                    scores = dot(key, q_ref[own, :], (0, 0))
                    prob = jnp.where(allowed, jnp.exp(scores), 0.0) * inv_ref[pl.ds(h, 1), :]
                    d_prob = dot(value, grad_ref[own, :], (0, 0))
                    ds = (prob * (d_prob - deltas[h])).astype(LOW)
                    back_ref[own, at] = dot(q_ref[own, :], ds, (1, 1)).astype(back_ref.dtype)
                    back_ref[pl.ds(width + h * hd, hd), at] = dot(
                        grad_ref[own, :], prob.astype(LOW), (1, 1)
                    ).astype(back_ref.dtype)
                    out.append(carry[h] + dot(key, ds))
                return out

            sums = lax.fori_loop(0, kv_ref.shape[1] // count, chunk, sums)
        for h in range(heads):
            dq_ref[pl.ds(h * hd, hd), :] = sums[h] * scale

    keys = sum(x.shape[1] for x in kvs)
    outs = [jax.ShapeDtypeStruct((width, rows), FULL)]
    outs += [jax.ShapeDtypeStruct(x.shape, FULL if i == 0 else LOW) for i, x in enumerate(kvs)]
    ins = (query, clip, inverse, grad, out, *kvs, *tags)
    scratch = []
    if gates is not None:
        ins += (gates,)
        outs.append(jax.ShapeDtypeStruct((heads, rows), FULL))
        scratch = [pltpu.VMEM((width, rows), LOW)]
    return kernel_call(body, ins, outs, 10 * width * rows * keys, scratch)


def make_body(seq_size):
    inner = seq_size // GROUPS
    steps = inner.bit_length() - 1

    def turned(j):
        return sum(((j >> i) & 1) << (steps - 1 - i) for i in range(steps))

    def hop_outer(x, t):
        pairs = [(i, ((i // inner) ^ t) * inner + i % inner) for i in range(seq_size)]
        return lax.ppermute(x, "seq", pairs)

    def hop_core(x):
        return lax.ppermute(x, "head", [(0, 1), (1, 0)])

    def hop_slot(x, j):
        pairs = []
        for at in range(seq_size):
            for head in range(2):
                to = (at // inner) * inner + ((at % inner) ^ (j if head == 0 else turned(j)))
                pairs.append((at * 2 + head, to * 2 + head))
        return lax.ppermute(x, ("seq", "head"), pairs)

    def hop_step(x, i):
        return hop_slot(x, 1 << i)

    def gather_outer(x):
        return [x] + [hop_outer(x, t) for t in range(1, GROUPS)]

    def body(
        latents,
        caption,
        conditioning,
        clip_frames,
        valid_patches,
        query_proj,
        key_proj,
        value_proj,
        output_proj,
        caption_key,
        caption_value,
        gate_proj,
        up_proj,
        down_proj,
        modulation,
        query_gain,
        key_gain,
        caption_gain,
        attn_gain,
        ffn_gain,
        cross_gate,
        cotangent,
    ):
        rows, width = latents.shape
        half = rows // 2
        hd = query_gain.shape[0]
        heads = cross_gate.shape[0] // GROUPS
        inner_width = heads * hd
        clips = conditioning.shape[0]
        scale = 1.0 / math.sqrt(hd)
        seq = lax.axis_index("seq")
        core = lax.axis_index("head")
        o, p = seq // inner, seq % inner
        group_rows = GROUPS * rows
        piece = query_proj.shape[0]
        planes = [p ^ jnp.where(core == 0, j, turned(j)) for j in range(inner)]
        last = [()]

        def step(*xs):
            xs, _ = lax.optimization_barrier((xs, last[0]))
            return xs

        def ended(*xs):
            last[0] = xs

        def plane_order(blocks):
            index = jnp.where(
                core == 0, p, sum(((p >> i) & 1) << (steps - 1 - i) for i in range(steps))
            )
            blocks = xor_order(blocks, index)
            return [
                b if turned(j) == j else jnp.where(core == 0, b, blocks[turned(j)])
                for j, b in enumerate(blocks)
            ]

        def token_ids(plane):
            c_at = core ^ jnp.arange(2)[:, None, None]
            o_at = o ^ jnp.arange(GROUPS)[None, :, None]
            at = jnp.arange(half)[None, None, :]
            return ((o_at * inner + plane) * rows + c_at * half + at).reshape(-1).astype(jnp.int32)

        ids = token_ids(p)
        key_ids = jnp.concatenate([token_ids(q) for q in planes])
        clip, position, _ = token_layout(clip_frames, valid_patches, ids)
        _, _, tag = token_layout(clip_frames, valid_patches, key_ids)
        own_clip = clip[:half]
        clip_row = clip[None, :]
        rates = 10000.0 ** (-(jnp.arange(hd // 2, dtype=FULL) * 2.0 / hd))
        angle = position.astype(FULL)[None, :] * rates[:, None]
        cosine, sine = jnp.cos(angle), jnp.sin(angle)

        own = lax.dynamic_slice_in_dim(latents, core * half, half, 0)
        own_cot = lax.dynamic_slice_in_dim(cotangent, core * half, half, 0)

        silu_cond = jax.nn.silu(conditioning.astype(FULL)).astype(LOW)
        cond_rows = modulation.shape[0]
        silu_own = lax.dynamic_slice_in_dim(silu_cond, seq * cond_rows, cond_rows, 1)
        shift_part = dot(silu_own, modulation)
        qkv_width = 3 * inner_width
        first_width = 4 * inner_width
        extra = two_parts(shift_part).reshape(piece, -1)
        got = []
        for t in range(GROUPS):
            cols = [
                lax.dynamic_slice_in_dim(w, (o ^ t) * inner_width, inner_width, 1)
                for w in (query_proj, key_proj, value_proj)
            ]
            cols.append(lax.dynamic_slice_in_dim(output_proj, (o ^ t) * inner_width, inner_width, 0).T)
            block = jnp.concatenate(cols + [extra], axis=1)
            got.append(hop_outer(block, t) if t else block)
        text_own = caption.shape[0]
        text_group = GROUPS * text_own
        cap_cols = caption.shape[1] // seq_size
        cap_split = caption.reshape(text_own, GROUPS, inner, cap_cols)
        cap = []
        for j in range(inner):
            block = pick(cap_split, planes[j], 2).reshape(text_own, GROUPS * cap_cols)
            cap.append(hop_slot(block, j) if j else block)
        ended(got, cap)

        shift_parts = [one_part(x[:, first_width:].reshape((2,) + shift_part.shape)) for x in got]
        shift_part = sum(xor_order(shift_parts, o))
        qkv_near = jnp.stack(xor_order([x[:, :first_width] for x in got], o))
        extra = two_parts(shift_part).reshape(GROUPS, piece, -1)
        qkv_stack = jnp.concatenate([qkv_near, extra], axis=2)[None]
        cap = jnp.concatenate(cap)
        cap_send = [
            lax.dynamic_slice_in_dim(cap, (o ^ t) * cap_cols, cap_cols, 1) for t in range(GROUPS)
        ]
        own_latents = own
        own, qkv_stack, cap_send = step(own, qkv_stack, cap_send)
        qkv_far = hop_step(qkv_stack, 0)
        cap = [cap_send[0]] + [hop_outer(cap_send[t], t) for t in range(1, GROUPS)]
        near_latents = gather_outer(own)
        for i in range(1, steps):
            qkv_stack = jnp.concatenate([qkv_stack, qkv_far])
            qkv_far = hop_step(qkv_stack, i)
        late_in, near_latents = lax.optimization_barrier(
            ((gate_proj, up_proj, down_proj), near_latents)
        )
        hidden_width = gate_proj.shape[1] // GROUPS
        late = []
        for t in range(GROUPS):
            wide = (o ^ t) * hidden_width
            block = jnp.concatenate(
                [
                    lax.dynamic_slice_in_dim(late_in[0], wide, hidden_width, 1),
                    lax.dynamic_slice_in_dim(late_in[1], wide, hidden_width, 1),
                    lax.dynamic_slice_in_dim(late_in[2], wide, hidden_width, 0).T,
                ],
                axis=1,
            )
            late.append(hop_outer(block, t) if t else block)
        ended(near_latents, qkv_far, cap)

        qkv_stack = jnp.concatenate([qkv_stack, qkv_far])
        near_latents = jnp.concatenate(near_latents)
        cap = [x.reshape(inner, text_own, cap_cols) for x in xor_order(cap, o)]
        cap_mine = jnp.stack(cap, axis=1).reshape(inner * text_group, cap_cols)
        cap_part = jnp.concatenate([dot(cap_mine, caption_key), dot(cap_mine, caption_value)], 1)
        far_latents = hop_core(near_latents)
        group_latents = jnp.concatenate([near_latents, far_latents]).astype(FULL)
        qkv = plane_order([qkv_stack[j, ..., :first_width] for j in range(inner)])
        first_weights = jnp.stack(qkv, axis=1).reshape(seq_size * piece, -1)
        qkv, out_t = first_weights[:, :qkv_width], first_weights[:, qkv_width:]
        shift_parts = [
            one_part(qkv_stack[j, ..., first_width:].reshape((2,) + shift_part.shape))
            for j in range(inner)
        ]
        shifts = sum(plane_order(shift_parts))
        scale_attn, gate_attn, scale_ffn, gate_ffn = [
            shifts[:, k * width : (k + 1) * width] for k in range(4)
        ]
        first_table = attn_gain * (1.0 + scale_attn)
        second_table = ffn_gain * (1.0 + scale_ffn)
        attn_tanh_table = jnp.tanh(gate_attn)
        ffn_tanh_table = jnp.tanh(gate_ffn)

        first_mult = by_clip(first_table, clip)
        normed = (group_latents * inverse_rms(group_latents) * first_mult).astype(LOW)
        raw = dot(qkv, normed, (0, 1))
        gain_q, gain_k, gain_c = query_gain[:, None], key_gain[:, None], caption_gain[:, None]
        queries, both = project(raw, gain_q, gain_k, cosine, sine, heads)

        both, cap_part, near_cot, late = step(both, cap_part, own_cot, late)
        for i in range(steps):
            if i:
                both, cap_part = step(both, cap_part)
            far = hop_step(both, i)
            keep = cap_part.shape[0] // 2
            cap_far = hop_step(cap_part[keep:].astype(LOW), steps - 1 - i)
            if i == 0:
                near_cot = gather_outer(near_cot)
            if i == steps - 1:
                ended(far, cap_far, near_cot)
            else:
                ended(far, cap_far)
            cap_part = cap_part[:keep] + cap_far.astype(FULL)
            if i < steps - 1:
                both = jnp.concatenate([both, far], axis=1)

        cap_part = cap_part.T.reshape(2, GROUPS, inner_width, text_group)
        cap_sent = [
            pick(cap_part, o ^ t, 1).reshape(2 * inner_width, text_group) for t in range(GROUPS)
        ]
        cap_first = cap_sent[0]
        late = jnp.stack(xor_order(late, o))[None]
        cap_sent, late = step([x.astype(LOW) for x in cap_sent[1:]], late)
        cap_z = [hop_outer(x, t + 1) for t, x in enumerate(cap_sent)]
        late_far = hop_step(late, 0)
        ended(cap_z)
        kvs = (both, far)
        tags = (tag[: both.shape[1]][:, None], tag[both.shape[1] :][:, None])
        cap_both, cap_key_raw = project_caption([cap_first] + cap_z, gain_c, heads)

        self_out, self_inv = attend(queries, clip_row, kvs, tags, heads)
        cap_both, self_out = step(cap_both, self_out)
        cap_both = [cap_both] + [hop_slot(cap_both, j) for j in range(1, inner)]
        ended(cap_both)
        cap_both = jnp.concatenate(cap_both, axis=1)
        text_rows = cap_both.shape[1]
        p_at = jnp.stack(planes)[:, None, None]
        o_at = jnp.arange(GROUPS)[None, :, None]
        text_ids = (o_at * inner + p_at) * text_own + jnp.arange(text_own)[None, None, :]
        text_clip = (text_ids // TEXT).reshape(-1, 1).astype(jnp.int32)

        gate_here = pick(cross_gate.reshape(GROUPS, heads), o)
        cross_tanh = jnp.tanh(gate_here)
        gates = jnp.broadcast_to(cross_tanh[:, None, None], (heads, hd, 1)).reshape(inner_width, 1)
        cross_out, cross_inv, mixed = attend(
            queries, clip_row, (cap_both,), (text_clip,), heads, gates, self_out
        )

        def send_core(partial):
            split = partial.shape[0] // 2
            return partial[:split], hop_core(partial[split:].astype(LOW))

        def send_outer(near, far):
            total = near + far.astype(FULL)
            parts = total.reshape(GROUPS, half, width)
            return [parts[0]] + [hop_outer(parts[t].astype(LOW), t) for t in range(1, GROUPS)]

        def summed(parts):
            total = parts[0]
            for x in parts[1:]:
                total = total + x.astype(FULL)
            return total

        near, far = send_core(dot(mixed, out_t, (0, 1)))
        late, _ = step(jnp.concatenate([late, late_far]), mixed)
        for i in range(1, steps):
            late = jnp.concatenate([late, hop_step(late, i)])
        attended_parts = send_outer(near, far)
        ended(attended_parts)

        attended = summed(attended_parts)
        inputs = own_latents.astype(FULL)
        upstream = own_cot.astype(FULL)
        attn_tanh = by_clip(attn_tanh_table, own_clip)
        hidden = inputs + attn_tanh * attended
        second_mult = by_clip(second_table, own_clip)
        ffn_own = (hidden * inverse_rms(hidden) * second_mult).astype(LOW)
        ffn_near = jnp.concatenate(gather_outer(ffn_own))
        ffn_input = jnp.concatenate([ffn_near, hop_core(ffn_near)])

        late = plane_order([late[j] for j in range(inner)])
        late = jnp.stack(late, axis=1).reshape(seq_size * piece, -1)
        gate_up, down_t = late[:, : 2 * hidden_width], late[:, 2 * hidden_width :]
        ffn_tanh = by_clip(ffn_tanh_table, own_clip)
        near_cot = jnp.concatenate(near_cot)
        group_cot = jnp.concatenate([near_cot, hop_core(near_cot)]).astype(FULL)
        d_ffn = (by_clip(ffn_tanh_table, clip) * group_cot).astype(LOW)
        d_act = dot(d_ffn, down_t)

        gate_up_val = dot(ffn_input, gate_up)
        gate_val, up_val = gate_up_val[:, :hidden_width], gate_up_val[:, hidden_width:]
        sigma = jax.nn.sigmoid(gate_val)
        activation = (gate_val * sigma * up_val).astype(LOW)
        d_gate = (d_act * up_val * sigma * (1.0 + gate_val * (1.0 - sigma))).astype(LOW)
        d_up = (d_act * gate_val * sigma).astype(LOW)
        d_gate_up = jnp.concatenate([d_gate, d_up], axis=1)
        near, far = send_core(dot(d_gate_up, gate_up, (1, 1)))
        d_ffn_parts = send_outer(near, far)

        def grad_slots(partial):
            parts = partial.astype(LOW).reshape(GROUPS, inner, piece, partial.shape[1])
            parts = jnp.concatenate([pick(parts, q, 1) for q in planes])
            return parts.reshape(inner * GROUPS * piece, partial.shape[1])

        def slots_hop(parts, i):
            near = parts.shape[0] // 2
            back = hop_step(parts[near:].astype(LOW), i)
            return parts[:near].astype(FULL) + back.astype(FULL)

        def slots_outer(parts):
            parts = parts.reshape(GROUPS, piece, -1)
            got = [
                hop_outer(pick(parts, o ^ t).astype(LOW), t).astype(FULL) for t in range(1, GROUPS)
            ]
            return [pick(parts, o)] + got

        def placed_columns(blocks, w, count):
            stacked = jnp.stack(xor_order(blocks, o), axis=1)
            return [stacked[:, :, i * w : (i + 1) * w].reshape(piece, -1) for i in range(count)]

        ffn_grads = jnp.concatenate(
            [dot(ffn_input, d_gate_up, (0, 0)), dot(d_ffn, activation, (0, 0))], axis=1
        )
        ffn_grads = grad_slots(ffn_grads)
        for i in reversed(range(1, steps)):
            ffn_grads = slots_hop(ffn_grads, i)
        ended(ffn_grads, d_ffn_parts)
        d_ffn_input = summed(d_ffn_parts)
        second_back, second_terms = norm_back(hidden, second_mult, d_ffn_input)
        d_hidden = upstream + second_back
        d_attended_own = (attn_tanh * d_hidden).astype(LOW)
        d_attended_own, ffn_grads = step(d_attended_own, ffn_grads)
        near = jnp.concatenate(gather_outer(d_attended_own))
        ffn_grads = slots_hop(ffn_grads, 0)
        d_attended = jnp.concatenate([near, hop_core(near)])
        ended(d_attended)

        d_mixed = dot(out_t, d_attended, (0, 1)).astype(LOW)
        ffn_out_sent = send_core(dot(activation, down_t, (1, 1)))
        d_mixed, ffn_out_sent = step(d_mixed, ffn_out_sent)
        ffn_out_parts = send_outer(*ffn_out_sent)
        dq_cross, cap_back, gate_terms = attend_back(
            queries, clip_row, (cap_both,), (text_clip,), heads, cross_inv, d_mixed, cross_out, gates
        )
        cap_keep = cap_back.shape[1] // 2
        cap_far = hop_step(cap_back[:, cap_keep:].astype(LOW), steps - 1)
        dq_self, kv_near, kv_far = attend_back(
            queries, clip_row, kvs, tags, heads, self_inv, d_mixed, self_out
        )
        ended(kv_far, cap_far, ffn_out_parts)
        cap_back = cap_back[:, :cap_keep] + cap_far.astype(FULL)
        for i in reversed(range(steps)):
            if i == steps - 1:
                kv_near, kv_far, cap_back, ffn_grads = step(kv_near, kv_far, cap_back, ffn_grads)
                ffn_blocks = slots_outer(ffn_grads)
                keep = kv_near.shape[1]
                far = hop_step(kv_far, i)
            else:
                kv_near, cap_back = step(kv_near, cap_back)
                keep = kv_near.shape[1] // 2
                far = hop_step(kv_near[:, keep:].astype(LOW), i)
            if i:
                cap_keep = cap_back.shape[1] // 2
                cap_far = hop_step(cap_back[:, cap_keep:].astype(LOW), i - 1)
                ended(far, cap_far)
                if i > 1:
                    cap_back = cap_back[:, :cap_keep] + cap_far.astype(FULL)
                kv_near = kv_near[:, :keep] + far.astype(FULL)
        kv_near = kv_near[:, :keep]

        d_qkv, query_terms, key_terms = project_back(
            raw, gain_q, gain_k, cosine, sine, heads, dq_self, dq_cross, kv_near, far
        )
        d_normed_part = dot(d_qkv, qkv, (0, 1))
        near, far = send_core(d_normed_part)
        near, far, d_qkv, normed, d_normed_part, cap_back, cap_far = step(
            near, far, d_qkv, normed, d_normed_part, cap_back, cap_far
        )
        d_normed_parts = send_outer(near, far)
        d_cap, cap_terms = project_caption_back(
            cap_key_raw, gain_c, heads, cap_back[:, :cap_keep], cap_far
        )
        grad_out_t = dot(d_attended, lax.optimization_barrier(mixed.T), (0, 0))
        cross_gate_part = jnp.sum(gate_terms, axis=1) * (1.0 - cross_tanh * cross_tanh)

        first_unit = group_latents * inverse_rms(group_latents)
        ffn_out = summed(ffn_out_parts)
        output = (hidden + ffn_tanh * ffn_out).astype(LOW)
        gate_slots = jnp.arange(2 * GROUPS) == core * GROUPS + o
        small = [
            clip_sums(d_normed_part * first_unit, clip, clips).reshape(-1),
            clip_sums(d_hidden * attended, own_clip, clips).reshape(-1),
            clip_sums(second_terms, own_clip, clips).reshape(-1),
            clip_sums(upstream * ffn_out, own_clip, clips).reshape(-1),
            query_terms[:, 0],
            key_terms[:, 0],
            cap_terms[:, 0],
            jnp.where(gate_slots[:, None], cross_gate_part[None, :], 0.0).reshape(-1),
        ]
        sizes = [x.shape[0] for x in small]
        small = jnp.concatenate(small)
        attn_grads = grad_slots(
            jnp.concatenate(
                [dot(normed, lax.optimization_barrier(d_qkv.T), (0, 0)), grad_out_t], axis=1
            )
        )
        attn_grads, small, d_cap = lax.optimization_barrier((attn_grads, small, d_cap))
        for k, i in enumerate(reversed(range(steps))):
            if k:
                attn_grads, small, d_cap = step(attn_grads, small, d_cap)
            attn_grads = slots_hop(attn_grads, i)
            small = small + hop_step(small, k)
            if k == 1:
                d_cap_parts = gather_outer(d_cap)
            ended(attn_grads, small)
        attn_grads, small, d_cap_parts = step(attn_grads, small, d_cap_parts)
        attn_blocks = slots_outer(attn_grads)
        bit = 1
        while bit < GROUPS:
            small = small + hop_outer(small, bit)
            bit *= 2
        small = small + hop_core(small)

        d_cap = jnp.stack(xor_order(d_cap_parts, o)).reshape(GROUPS, 2, inner_width, text_group)
        d_cap = jnp.swapaxes(d_cap, 0, 1).reshape(2 * GROUPS * inner_width, text_group)
        d_cap = jnp.concatenate(
            [d_cap] + [hop_slot(d_cap, j) for j in range(1, inner)], axis=1
        )
        cap_width = caption_key.shape[1]
        grad_cap_key = dot(cap_mine, d_cap[:cap_width], (0, 1))
        grad_cap_value = dot(cap_mine, d_cap[cap_width:], (0, 1))

        grad_gate, grad_up, grad_down_t = placed_columns(ffn_blocks, hidden_width, 3)
        grad_query, grad_key, grad_value, grad_output_t = placed_columns(attn_blocks, inner_width, 4)
        d_normed = summed(d_normed_parts)
        own_mult = by_clip(first_table, own_clip)
        first_back, _ = norm_back(inputs, own_mult, d_normed)
        grad_latents = (d_hidden + first_back).astype(LOW)

        pieces, at = [], 0
        for n in sizes:
            pieces.append(small[at : at + n])
            at += n
        first_sum, attended_sum, second_sum, out_sum = [x.reshape(clips, width) for x in pieces[:4]]
        g_query, g_key, g_cap, g_cross = pieces[4:]
        g_attn = jnp.sum(first_sum * (1.0 + scale_attn), axis=0)
        g_ffn = jnp.sum(second_sum * (1.0 + scale_ffn), axis=0)
        shift_grad = jnp.concatenate(
            [
                first_sum * attn_gain,
                attended_sum * (1.0 - attn_tanh_table**2),
                second_sum * ffn_gain,
                out_sum * (1.0 - ffn_tanh_table**2),
            ],
            axis=1,
        )
        g_cross = pick(g_cross.reshape(2, -1), core)
        silu_f = silu_own.astype(FULL)
        grad_modulation = sum(silu_f[k][:, None] * shift_grad[k][None, :] for k in range(clips))

        def whole_rows(x):
            both = jnp.stack([x, hop_core(x)])
            return jnp.concatenate([pick(both, core), pick(both, 1 - core)])

        return (
            whole_rows(output),
            whole_rows(grad_latents),
            grad_query,
            grad_key,
            grad_value,
            grad_output_t.T,
            grad_cap_key,
            grad_cap_value,
            grad_gate,
            grad_up,
            grad_down_t.T,
            grad_modulation,
            g_query,
            g_key,
            g_cap,
            g_attn,
            g_ffn,
            g_cross,
        )

    return body


def solution(mesh):
    rows, cols, turned = P("seq", None), P("seq", "head"), P("head", "seq")
    one = P()
    placed = (rows, rows, one, one, one, cols, cols, cols, turned, cols, cols, cols, cols, turned)
    placed += (rows, one, one, one, one, one, P("head"), rows)
    given = (rows, rows, cols, cols, cols, turned, cols, cols, cols, cols, turned, rows)
    given += (one, one, one, one, one, P("head"))
    return jax.shard_map(
        make_body(mesh.shape["seq"]), mesh=mesh, in_specs=placed, out_specs=given, check_vma=False
    )
```

```python
import math

import jax
import jax.numpy as jnp
from jax import lax
from jax.experimental import pallas as pl
from jax.experimental.pallas import tpu as pltpu
from jax.sharding import PartitionSpec as P

TEXT = 256
FRAME = 385
GROUPS = 4
EPSILON = 1e-06
LOW = jnp.bfloat16
FULL = jnp.float32


def token_layout(clip_frames, valid_patches, ids):
    clips = clip_frames.shape[0]
    upto = jnp.arange(clips)[None, :] <= jnp.arange(clips)[:, None]
    ends = FRAME * jnp.sum(jnp.where(upto, clip_frames[None, :], 0), axis=1)
    starts = ends - FRAME * clip_frames
    clip = jnp.sum((ends[None, :] <= ids[:, None]).astype(jnp.int32), axis=1)
    chosen = (clip[:, None] == jnp.arange(clips, dtype=jnp.int32)[None, :]).astype(jnp.int32)
    position = ids - jnp.sum(chosen * starts[None, :], axis=1)
    within = position % FRAME
    limit = jnp.sum(chosen * valid_patches[None, :], axis=1)
    tag = jnp.where((within < limit) | (within == FRAME - 1), clip, -1)
    return clip, position, tag


def inverse_rms(values, axis=-1):
    return lax.rsqrt(jnp.mean(values * values, axis=axis, keepdims=True) + EPSILON)


def norm_back(raw, gain, grad, axis=-1):
    inverse = inverse_rms(raw, axis)
    unit = raw * inverse
    scaled = grad * gain
    back = inverse * (scaled - unit * jnp.mean(scaled * unit, axis=axis, keepdims=True))
    return back, grad * unit


def dot(left, right, contract=(1, 0)):
    dims = (((contract[0],), (contract[1],)), ((), ()))
    return lax.dot_general(left, right, dims, preferred_element_type=FULL)


def by_clip(table, clip):
    out = table[0][None]
    for k in range(1, table.shape[0]):
        out = jnp.where(clip[:, None] == k, table[k][None], out)
    return out


def clip_sums(values, clip, clips):
    return jnp.stack(
        [jnp.sum(jnp.where(clip[:, None] == k, values, 0.0), axis=0) for k in range(clips)]
    )


def xor_order(blocks, index):
    blocks = list(blocks)
    bit = 1
    while bit < len(blocks):
        on = (index & bit) != 0
        blocks = [jnp.where(on, blocks[j ^ bit], blocks[j]) for j in range(len(blocks))]
        bit *= 2
    return blocks


def pick(stack, index, axis=0):
    return lax.dynamic_index_in_dim(stack, index, axis, keepdims=False)


def low_round(x):
    return lax.reduce_precision(x, 8, 7)


def two_parts(x):
    upper = low_round(x)
    return jnp.stack([upper, low_round(x - upper)]).astype(LOW)


def two_round(x):
    upper = low_round(x)
    return upper + low_round(x - upper)


def one_part(x):
    return x[0].astype(FULL) + x[1].astype(FULL)


def chunk_of(keys):
    return 512 if keys % 512 == 0 else keys


def kernel_call(body, ins, outs, scratch=(), scalars=-1):
    space, small = [pl.BlockSpec(memory_space=m) for m in (pltpu.VMEM, pltpu.SMEM)]
    return pl.pallas_call(
        body,
        out_shape=outs,
        in_specs=[small if i == scalars else space for i in range(len(ins))],
        out_specs=[space] * len(outs),
        scratch_shapes=list(scratch),
        compiler_params=pltpu.CompilerParams(vmem_limit_bytes=56 << 20),
        cost_estimate=pl.CostEstimate(flops=1000, bytes_accessed=1000, transcendentals=0),
    )(*ins)


def project(raw, gain_q, gain_k, cosine, sine, heads):
    hd = gain_q.shape[0]
    half, width, rows = hd // 2, heads * hd, raw.shape[1]
    scale = 1.0 / math.sqrt(hd)

    def body(raw_ref, gq_ref, gk_ref, cos_ref, sin_ref, q_ref, kv_ref):
        c, s = cos_ref[...], sin_ref[...]
        for part, gain_ref, out_ref in ((0, gq_ref, q_ref), (1, gk_ref, kv_ref)):
            for h in range(heads):
                u = raw_ref[pl.ds(part * width + h * hd, hd), :]
                n = u * inverse_rms(u, 0) * gain_ref[...]
                a, b = n[:half], n[half:]
                turned = jnp.concatenate([a * c - b * s, a * s + b * c], axis=0).astype(LOW)
                if part == 0:
                    turned = (turned.astype(FULL) * scale).astype(LOW)
                out_ref[pl.ds(h * hd, hd), :] = turned
        kv_ref[pl.ds(width, width), :] = raw_ref[pl.ds(2 * width, width), :].astype(LOW)

    outs = (jax.ShapeDtypeStruct((width, rows), LOW), jax.ShapeDtypeStruct((2 * width, rows), LOW))
    return kernel_call(body, (raw, gain_q, gain_k, cosine, sine), outs)


def row_sums(terms):
    wide = terms[:, :128]
    for at in range(128, terms.shape[1], 128):
        wide = wide + terms[:, at : at + 128]
    return jnp.sum(wide.T, axis=0, keepdims=True)


def project_back(raw, gain_q, gain_k, cosine, sine, heads, dqs, kv_near, kv_far, left, planes, groups):
    hd = gain_q.shape[0]
    half, width, rows = hd // 2, heads * hd, raw.shape[1]
    normed, mixed, d_attended = left
    inner, features = planes.shape[0], normed.shape[1]
    piece = features // (inner * groups)
    n = len(dqs)
    lanes = features // 4

    def body(*refs):
        raw_ref, gq_ref, gk_ref, cos_ref, sin_ref = refs[:5]
        dq_refs, rest = refs[5 : 5 + n], refs[5 + n :]
        n_ref, f_ref, x_ref, m_ref, a_ref, p_ref, out_ref, tq, tk, near_ref, far_ref, g_ref = rest
        c, s = cos_ref[...], sin_ref[...]
        for part, gain_ref, term_ref in ((0, gq_ref, tq), (1, gk_ref, tk)):
            terms = jnp.zeros((hd, rows), FULL)
            for h in range(heads):
                at = pl.ds(h * hd, hd)
                if part == 0:
                    grad = dq_refs[0][at, :]
                    for ref in dq_refs[1:]:
                        grad = grad + ref[at, :]
                else:
                    grad = n_ref[at, :] + f_ref[at, :].astype(FULL)
                x, y = grad[:half], grad[half:]
                grad = jnp.concatenate([x * c + y * s, y * c - x * s], axis=0)
                where = pl.ds(part * width + h * hd, hd)
                back, term = norm_back(raw_ref[where, :], gain_ref[...], grad, 0)
                out_ref[where, :] = back.astype(LOW)
                terms = terms + term
            term_ref[...] = row_sums(terms)
        at = pl.ds(width, width)
        out_ref[pl.ds(2 * width, width), :] = (n_ref[at, :] + f_ref[at, :].astype(FULL)).astype(LOW)
        turned = out_ref[...].T
        mix = m_ref[...].T
        for k in range(4):
            at = pl.ds(k * lanes, lanes)
            one = dot(x_ref[:, at], turned, (0, 0))
            two = dot(a_ref[:, at], mix, (0, 0))
            g_ref[at, :] = jnp.concatenate([one, two], axis=1)
        for j in range(inner):
            for g in range(groups):
                start = pl.multiple_of((g * inner + p_ref[j]) * piece, 8)
                block = g_ref[pl.ds(start, piece), :]
                if j < inner // 2:
                    near_ref[j * groups + g] = block
                else:
                    far_ref[(j - inner // 2) * groups + g] = block.astype(LOW)

    row = jax.ShapeDtypeStruct((1, hd), FULL)
    blocks = (inner * groups // 2, piece, 4 * width)
    outs = (jax.ShapeDtypeStruct((3 * width, rows), LOW), row, row)
    outs += (jax.ShapeDtypeStruct(blocks, FULL), jax.ShapeDtypeStruct(blocks, LOW))
    ins = (raw, gain_q, gain_k, cosine, sine, *dqs, kv_near, kv_far, normed, mixed, d_attended, planes)
    scratch = [pltpu.VMEM((features, 4 * width), FULL)]
    return kernel_call(body, ins, outs, scratch, len(ins) - 1)


def place_columns(blocks, index, count):
    groups = len(blocks)
    rows, w = blocks[0].shape[0], blocks[0].shape[1] // count

    def body(index_ref, *refs):
        here = index_ref[0]
        block_refs, out_refs = refs[:groups], refs[groups:]
        for g in range(groups):
            for k in range(count):
                at = pl.ds(k * w, w)
                x = block_refs[0][:, at].astype(FULL)
                for t in range(1, groups):
                    x = jnp.where(here == (g ^ t), block_refs[t][:, at].astype(FULL), x)
                out_refs[k][:, pl.ds(g * w, w)] = x

    outs = [jax.ShapeDtypeStruct((rows, groups * w), FULL)] * count
    return kernel_call(body, (index.reshape(1), *blocks), outs, (), 0)


def project_caption(parts, gain, heads):
    hd = gain.shape[0]
    width, rows = heads * hd, parts[0].shape[0]

    def body(*refs):
        part_refs, gain_ref, out_ref, raw_ref = refs[:-3], refs[-3], refs[-2], refs[-1]
        total = part_refs[0][...]
        for ref in part_refs[1:]:
            total = total + ref[...].astype(FULL)
        total = total.T
        raw_ref[...] = total[:width]
        for h in range(heads):
            u = total[h * hd : (h + 1) * hd]
            out_ref[pl.ds(h * hd, hd), :] = (u * inverse_rms(u, 0) * gain_ref[...]).astype(LOW)
        out_ref[pl.ds(width, width), :] = total[width:].astype(LOW)

    outs = (jax.ShapeDtypeStruct((2 * width, rows), LOW), jax.ShapeDtypeStruct((width, rows), FULL))
    return kernel_call(body, (*parts, gain), outs)


def project_caption_back(raw, gain, heads, near, far):
    hd = gain.shape[0]
    width, rows = raw.shape

    def body(raw_ref, gain_ref, n_ref, f_ref, out_ref, term_ref):
        total = n_ref[...] + f_ref[...].astype(FULL)
        terms = jnp.zeros((hd, rows), FULL)
        for h in range(heads):
            at = slice(h * hd, (h + 1) * hd)
            back, term = norm_back(raw_ref[at, :], gain_ref[...], total[at], 0)
            out_ref[at, :] = back.astype(LOW)
            terms = terms + term
        term_ref[...] = (row_sums(terms) if rows % 128 == 0 else jnp.sum(terms.T, axis=0, keepdims=True))
        out_ref[width:, :] = total[width:].astype(LOW)

    outs = (jax.ShapeDtypeStruct((2 * width, rows), LOW), jax.ShapeDtypeStruct((1, hd), FULL))
    return kernel_call(body, (raw, gain, near, far), outs)


def attend(query, clip, kvs, tags, heads, gates=None, other=None):
    width, rows = query.shape
    hd = width // heads
    n = len(kvs)

    def body(*refs):
        q_ref, clip_ref = refs[:2]
        kv_refs, tag_refs = refs[2 : 2 + n], refs[2 + n : 2 + 2 * n]
        rest = refs[2 + 2 * n :]
        if gates is not None:
            gate_ref, other_ref, out_ref, inv_ref, mix_ref = rest
        else:
            out_ref, inv_ref = rest
        here = clip_ref[...]
        sums = [(jnp.zeros((1, rows), FULL), jnp.zeros((hd, rows), FULL)) for _ in range(heads)]
        for kv_ref, tag_ref in zip(kv_refs, tag_refs):
            count = chunk_of(kv_ref.shape[1])

            def chunk(i, carry):
                at = pl.ds(pl.multiple_of(i * count, count), count)
                allowed = tag_ref[at, :] == here
                out = []
                for h in range(heads):
                    total, acc = carry[h]
                    key = kv_ref[pl.ds(h * hd, hd), at]
                    value = kv_ref[pl.ds(width + h * hd, hd), at]
                    scores = dot(key, q_ref[pl.ds(h * hd, hd), :], (0, 0))
                    weights = jnp.where(allowed, jnp.exp(scores), 0.0)
                    total = total + jnp.sum(weights, axis=0, keepdims=True)
                    out.append((total, acc + dot(value, weights.astype(LOW))))
                return out

            sums = lax.fori_loop(0, kv_ref.shape[1] // count, chunk, sums)
        for h in range(heads):
            total, acc = sums[h]
            inverse = 1.0 / total
            inv_ref[pl.ds(h, 1), :] = inverse
            out_ref[pl.ds(h * hd, hd), :] = acc * inverse
            if gates is not None:
                own = pl.ds(h * hd, hd)
                mix_ref[own, :] = (other_ref[own, :] + gate_ref[own, :] * (acc * inverse)).astype(LOW)

    ins = (query, clip, *kvs, *tags)
    outs = (jax.ShapeDtypeStruct((width, rows), FULL), jax.ShapeDtypeStruct((heads, rows), FULL))
    if gates is not None:
        ins += (gates, other)
        outs += (jax.ShapeDtypeStruct((width, rows), LOW),)
    return kernel_call(body, ins, outs)


def attend_back(query, clip, kvs, tags, heads, inverse, grad, out, kind, gates=None):
    width, rows = query.shape
    hd = width // heads
    n = len(kvs)
    scale = 1.0 / math.sqrt(hd)

    def body(*refs):
        q_ref, clip_ref, inv_ref, given_ref, o_ref = refs[:5]
        kv_refs, tag_refs = refs[5 : 5 + n], refs[5 + n : 5 + 2 * n]
        here = clip_ref[...]
        if gates is None:
            dq_ref, back_refs = refs[5 + 2 * n], refs[6 + 2 * n :]
            grad_ref = given_ref
        else:
            gate_ref, dq_ref, back_refs = refs[5 + 2 * n], refs[6 + 2 * n], refs[7 + 2 * n :]
            back_refs, sum_ref, grad_ref = back_refs[:n], back_refs[n], back_refs[n + 1]
        deltas = []
        for h in range(heads):
            own = pl.ds(h * hd, hd)
            if gates is not None:
                given = given_ref[own, :].astype(FULL)
                grad_ref[own, :] = (gate_ref[own, :] * given).astype(LOW)
                sum_ref[pl.ds(h, 1), :] = jnp.sum(given * o_ref[own, :], axis=0, keepdims=True)
            terms = grad_ref[own, :].astype(FULL) * o_ref[own, :]
            deltas.append(jnp.sum(terms, axis=0, keepdims=True))
        sums = [jnp.zeros((hd, rows), FULL) for _ in range(heads)]
        for kv_ref, tag_ref, back_ref in zip(kv_refs, tag_refs, back_refs):
            count = chunk_of(kv_ref.shape[1])

            def chunk(i, carry):
                at = pl.ds(pl.multiple_of(i * count, count), count)
                allowed = tag_ref[at, :] == here
                out = []
                for h in range(heads):
                    own = pl.ds(h * hd, hd)
                    key = kv_ref[own, at]
                    value = kv_ref[pl.ds(width + h * hd, hd), at]
                    scores = dot(key, q_ref[own, :], (0, 0))
                    prob = jnp.where(allowed, jnp.exp(scores), 0.0) * inv_ref[pl.ds(h, 1), :]
                    d_prob = dot(value, grad_ref[own, :], (0, 0))
                    ds = (prob * (d_prob - deltas[h])).astype(LOW)
                    back_ref[own, at] = dot(q_ref[own, :], ds, (1, 1)).astype(back_ref.dtype)
                    back_ref[pl.ds(width + h * hd, hd), at] = dot(
                        grad_ref[own, :], prob.astype(LOW), (1, 1)
                    ).astype(back_ref.dtype)
                    out.append(carry[h] + dot(key, ds))
                return out

            sums = lax.fori_loop(0, kv_ref.shape[1] // count, chunk, sums)
        for h in range(heads):
            dq_ref[pl.ds(h * hd, hd), :] = sums[h] * scale

    outs = [jax.ShapeDtypeStruct((width, rows), FULL)]
    outs += [jax.ShapeDtypeStruct(x.shape, kind) for x in kvs]
    ins = (query, clip, inverse, grad, out, *kvs, *tags)
    scratch = []
    if gates is not None:
        ins += (gates,)
        outs.append(jax.ShapeDtypeStruct((heads, rows), FULL))
        scratch = [pltpu.VMEM((width, rows), LOW)]
    return kernel_call(body, ins, outs, scratch)


def assemble(near, far, slots):
    half, groups, piece, columns = near.shape

    def body(s_ref, a_ref, b_ref, out_ref):
        for q in range(2 * half):
            at = s_ref[q]

            @pl.when(at < half)
            def _():
                for g in range(groups):
                    out_ref[g, q] = a_ref[at, g]

            @pl.when(at >= half)
            def _():
                for g in range(groups):
                    out_ref[g, q] = b_ref[at - half, g]

    shape = (groups, 2 * half, piece, columns)
    (out,) = kernel_call(body, (slots, near, far), (jax.ShapeDtypeStruct(shape, near.dtype),), (), 0)
    return out.reshape(-1, columns)


def feed_forward(halves, d_ffn, weights):
    count, width = halves[0].shape
    hidden = weights.shape[1] // 3

    def body(a_ref, b_ref, d_ref, w_ref, act_ref, dgu_ref, near_ref, far_ref):
        for k, (x_ref, out_ref) in enumerate(((a_ref, near_ref), (b_ref, far_ref))):
            at = pl.ds(k * count, count)
            gate_up = w_ref[:, pl.ds(0, 2 * hidden)]
            both = dot(x_ref[...], gate_up)
            d_act = dot(d_ref[at, :], w_ref[:, pl.ds(2 * hidden, hidden)])
            gate, up = both[:, :hidden], both[:, hidden:]
            sigma = 1.0 / (1.0 + jnp.exp(-gate))
            act_ref[at, :] = (gate * sigma * up).astype(LOW)
            d_gate = (d_act * up * sigma * (1.0 + gate * (1.0 - sigma))).astype(LOW)
            dgu_ref[at, pl.ds(0, hidden)] = d_gate
            dgu_ref[at, pl.ds(hidden, hidden)] = (d_act * gate * sigma).astype(LOW)
            out_ref[...] = dot(dgu_ref[at, :], gate_up, (1, 1)).astype(out_ref.dtype)

    outs = (
        jax.ShapeDtypeStruct((2 * count, hidden), LOW),
        jax.ShapeDtypeStruct((2 * count, 2 * hidden), LOW),
        jax.ShapeDtypeStruct((count, width), FULL),
        jax.ShapeDtypeStruct((count, width), LOW),
    )
    return kernel_call(body, (*halves, d_ffn, weights), outs)


def feed_forward_grads(halves, d_ffn, weights, activation, d_gate_up, planes, groups):
    count, width = halves[0].shape
    hidden = activation.shape[1]
    inner = planes.shape[0]
    piece = width // (inner * groups)
    lanes = width // 4

    def body(a_ref, b_ref, d_ref, w_ref, act_ref, dgu_ref, p_ref, near_ref, far_ref, gn_ref, gf_ref, g_ref):
        for k, out_ref in enumerate((near_ref, far_ref)):
            at = pl.ds(k * count, count)
            out_ref[...] = dot(
                act_ref[at, :], w_ref[:, pl.ds(2 * hidden, hidden)], (1, 1)
            ).astype(out_ref.dtype)
        for k in range(4):
            at = pl.ds(k * lanes, lanes)
            x = jnp.concatenate([a_ref[:, at], b_ref[:, at]], axis=0)
            g_ref[at, pl.ds(0, 2 * hidden)] = dot(x, dgu_ref[...], (0, 0))
            g_ref[at, pl.ds(2 * hidden, hidden)] = dot(d_ref[:, at], act_ref[...], (0, 0))
        for j in range(inner):
            for g in range(groups):
                start = pl.multiple_of((g * inner + p_ref[j]) * piece, 8)
                block = g_ref[pl.ds(start, piece), :].astype(LOW)
                if j < inner // 2:
                    gn_ref[j * groups + g] = block
                else:
                    gf_ref[(j - inner // 2) * groups + g] = block

    blocks = jax.ShapeDtypeStruct((inner * groups // 2, piece, 3 * hidden), LOW)
    outs = (
        jax.ShapeDtypeStruct((count, width), FULL),
        jax.ShapeDtypeStruct((count, width), LOW),
        blocks,
        blocks,
    )
    ins = (*halves, d_ffn, weights, activation, d_gate_up, planes)
    return kernel_call(body, ins, outs, [pltpu.VMEM((width, 3 * hidden), FULL)], len(ins) - 1)


def normed_back(d_qkv, qkv, latents, clip, clips):
    rows, width = latents.shape
    half, lanes = rows // 2, width // 4

    def body(d_ref, w_ref, x_ref, c_ref, near_ref, far_ref, sum_ref):
        x = x_ref[...].astype(FULL)
        inverse = inverse_rms(x)
        turned = d_ref[...].T
        for k in range(4):
            at = pl.ds(k * lanes, lanes)
            part = dot(turned, w_ref[at, pl.ds(0, turned.shape[1])], (1, 1))
            near_ref[:, at] = part[:half]
            far_ref[:, at] = part[half:].astype(LOW)
            terms = part * (x_ref[:, at].astype(FULL) * inverse)
            for c in range(clips):
                picked = jnp.where(c_ref[...] == c, terms, 0.0)
                sum_ref[pl.ds(c, 1), at] = jnp.sum(picked, axis=0, keepdims=True)

    outs = (
        jax.ShapeDtypeStruct((half, width), FULL),
        jax.ShapeDtypeStruct((half, width), LOW),
        jax.ShapeDtypeStruct((clips, width), FULL),
    )
    return kernel_call(body, (d_qkv, qkv, latents, clip), outs)


def small_sums(first, terms, ffn_parts, upstream, hidden, ffn_tanh, clip, gains, gate_terms, gates, place, slots):
    clips, width = first.shape
    d_hidden, attended, second = terms
    heads = gate_terms.shape[0]
    hd = gates.shape[0] // heads
    n = len(ffn_parts)
    rows = 4 * clips + len(gains) + 1
    padded = -(-rows // 8) * 8

    def body(p_ref, first_ref, dh_ref, at_ref, s_ref, *refs):
        part_refs, refs = refs[:n], refs[n:]
        up_ref, h_ref, t_ref, c_ref, *gain_refs, gt_ref, gate_ref, out_ref, sum_ref = refs
        ffn_out = part_refs[0][...]
        for ref in part_refs[1:]:
            ffn_out = ffn_out + ref[...].astype(FULL)
        out_ref[...] = (h_ref[...] + t_ref[...] * ffn_out).astype(LOW)
        sum_ref[...] = jnp.zeros_like(sum_ref)
        sum_ref[pl.ds(0, clips), :] = first_ref[...]
        for k, x in enumerate((dh_ref[...] * at_ref[...], s_ref[...], up_ref[...] * ffn_out)):
            for c in range(clips):
                picked = jnp.where(c_ref[...] == c, x, 0.0)
                sum_ref[pl.ds((k + 1) * clips + c, 1), :] = jnp.sum(picked, axis=0, keepdims=True)
        for k, ref in enumerate(gain_refs):
            sum_ref[pl.ds(4 * clips + k, 1), pl.ds(0, ref.shape[1])] = ref[...]
        lane = lax.broadcasted_iota(jnp.int32, (1, 128), 1)
        row = jnp.zeros((1, 128), FULL)
        for h in range(heads):
            total = jnp.sum(gt_ref[pl.ds(h, 1), :], axis=1, keepdims=True)
            gate = gate_ref[pl.ds(h * hd, 1), :]
            row = jnp.where(lane == p_ref[0] * heads + h, total * (1.0 - gate * gate), row)
        sum_ref[pl.ds(rows - 1, 1), pl.ds(0, 128)] = row

    ins = (place, first, d_hidden, attended, second, *ffn_parts, upstream, hidden, ffn_tanh, clip)
    ins += (*gains, gate_terms, gates)
    outs = (jax.ShapeDtypeStruct(hidden.shape, LOW), jax.ShapeDtypeStruct((padded, width), FULL))
    return kernel_call(body, ins, outs, (), 0)


def make_body(seq_size):
    inner = seq_size // GROUPS
    steps = inner.bit_length() - 1

    def turned(j):
        return sum(((j >> i) & 1) << (steps - 1 - i) for i in range(steps))

    def hop_outer(x, t):
        pairs = [(i, ((i // inner) ^ t) * inner + i % inner) for i in range(seq_size)]
        return lax.ppermute(x, "seq", pairs)

    def hop_core(x):
        return lax.ppermute(x, "head", [(0, 1), (1, 0)])

    def hop_slot(x, j):
        pairs = []
        for at in range(seq_size):
            for head in range(2):
                to = (at // inner) * inner + ((at % inner) ^ (j if head == 0 else turned(j)))
                pairs.append((at * 2 + head, to * 2 + head))
        return lax.ppermute(x, ("seq", "head"), pairs)

    def hop_step(x, i):
        return hop_slot(x, 1 << i)

    def gather_outer(x):
        return [x] + [hop_outer(x, t) for t in range(1, GROUPS)]

    def body(
        latents,
        caption,
        conditioning,
        clip_frames,
        valid_patches,
        query_proj,
        key_proj,
        value_proj,
        output_proj,
        caption_key,
        caption_value,
        gate_proj,
        up_proj,
        down_proj,
        modulation,
        query_gain,
        key_gain,
        caption_gain,
        attn_gain,
        ffn_gain,
        cross_gate,
        cotangent,
    ):
        rows, width = latents.shape
        half = rows // 2
        hd = query_gain.shape[0]
        heads = cross_gate.shape[0] // GROUPS
        inner_width = heads * hd
        clips = conditioning.shape[0]
        scale = 1.0 / math.sqrt(hd)
        seq = lax.axis_index("seq")
        core = lax.axis_index("head")
        o, p = seq // inner, seq % inner
        group_rows = GROUPS * rows
        piece = query_proj.shape[0]
        planes = [p ^ jnp.where(core == 0, j, turned(j)) for j in range(inner)]
        fence = lax.optimization_barrier
        place_of = jnp.arange(inner)
        relative = p ^ place_of
        turned_relative = sum(((relative >> i) & 1) << (steps - 1 - i) for i in range(steps))
        slots = jnp.where(core == 0, relative, turned_relative).astype(jnp.int32)


        def plane_order(blocks):
            index = jnp.where(
                core == 0, p, sum(((p >> i) & 1) << (steps - 1 - i) for i in range(steps))
            )
            blocks = xor_order(blocks, index)
            return [
                b if turned(j) == j else jnp.where(core == 0, b, blocks[turned(j)])
                for j, b in enumerate(blocks)
            ]

        def token_ids(plane):
            c_at = core ^ jnp.arange(2)[:, None, None]
            o_at = o ^ jnp.arange(GROUPS)[None, :, None]
            at = jnp.arange(half)[None, None, :]
            return ((o_at * inner + plane) * rows + c_at * half + at).reshape(-1).astype(jnp.int32)

        ids = token_ids(p)
        key_ids = jnp.concatenate([token_ids(q) for q in planes])
        clip, position, _ = token_layout(clip_frames, valid_patches, ids)
        _, _, tag = token_layout(clip_frames, valid_patches, key_ids)
        own_clip = clip[:half]
        clip_row = clip[None, :]
        rates = 10000.0 ** (-(jnp.arange(hd // 2, dtype=FULL) * 2.0 / hd))
        angle = position.astype(FULL)[None, :] * rates[:, None]
        cosine, sine = jnp.cos(angle), jnp.sin(angle)

        own = lax.dynamic_slice_in_dim(latents, core * half, half, 0)
        own_cot = lax.dynamic_slice_in_dim(cotangent, core * half, half, 0)
        inputs = own.astype(FULL)
        upstream = own_cot.astype(FULL)

        def send_core(partial):
            split = partial.shape[0] // 2
            return partial[:split], hop_core(partial[split:].astype(LOW))

        def parts_of(near, far):
            parts = (near + far.astype(FULL)).reshape(GROUPS, half, width)
            return [parts[0]] + [parts[t].astype(LOW) for t in range(1, GROUPS)]

        def send_outer(near, far):
            return hops_outer(parts_of(near, far))

        def summed(parts):
            total = parts[0]
            for x in parts[1:]:
                total = total + x.astype(FULL)
            return total

        def hops_outer(blocks):
            return [hop_outer(x, t) if t else x for t, x in enumerate(blocks)]

        def hops_slot(blocks):
            return [hop_slot(x, t) if t else x for t, x in enumerate(blocks)]

        silu_cond = jax.nn.silu(conditioning.astype(FULL)).astype(LOW)
        cond_rows = modulation.shape[0]
        silu_own = lax.dynamic_slice_in_dim(silu_cond, seq * cond_rows, cond_rows, 1)
        shift_part = dot(silu_own, modulation)
        shift_shape = (2,) + shift_part.shape
        qkv_width = 3 * inner_width
        first_width = 4 * inner_width
        extra = two_parts(shift_part).reshape(piece, -1)
        sent = []
        for t in range(GROUPS):
            at = (o ^ t) * inner_width
            cols = [
                lax.dynamic_slice_in_dim(w, at, inner_width, 1)
                for w in (query_proj, key_proj, value_proj)
            ]
            cols.append(lax.dynamic_slice_in_dim(output_proj, at, inner_width, 0).T)
            sent.append(jnp.concatenate(cols + [extra], axis=1))
        text_own = caption.shape[0]
        text_group = GROUPS * text_own
        cap_cols = caption.shape[1] // seq_size
        sent, caption = fence((sent, caption))
        got = hops_outer(sent)
        cap_split = caption.reshape(text_own, GROUPS, inner, cap_cols)
        cap = hops_slot([pick(cap_split, q, 2).reshape(text_own, -1) for q in planes])
        split = key_ids.shape[0] // 2
        p_at = jnp.stack(planes)[:, None, None]
        o_at = jnp.arange(GROUPS)[None, :, None]
        text_ids = (o_at * inner + p_at) * text_own + jnp.arange(text_own)[None, None, :]
        columns = [
            tag[:split][:, None],
            tag[split:][:, None],
            (text_ids // TEXT).reshape(-1, 1).astype(jnp.int32),
            clip[:, None],
            own_clip[:, None],
            query_gain[:, None],
            key_gain[:, None],
            caption_gain[:, None],
        ]
        gate_here = pick(cross_gate.reshape(GROUPS, heads), o)
        gates = jnp.broadcast_to(jnp.tanh(gate_here)[:, None, None], (heads, hd, 1))
        gates = gates.reshape(inner_width, 1)
        got, cap, own, columns, gates, cosine, sine = fence(
            (got, cap, own, columns, gates, cosine, sine)
        )
        tag_columns, text_clip, clip_column, own_clip_column = columns[:2], *columns[2:5]
        gain_q, gain_k, gain_c = columns[5:]

        shift_parts = [one_part(x[:, first_width:].reshape(shift_shape)) for x in got]
        shift_part = sum(xor_order(shift_parts, o))
        extra = two_parts(shift_part).reshape(GROUPS, piece, -1)
        stack = jnp.stack(xor_order([x[:, :first_width] for x in got], o))
        stack = jnp.concatenate([stack, extra], axis=2)[None]
        cap = jnp.concatenate(cap)
        far = hop_step(stack, 0)
        cap = hops_outer(
            [lax.dynamic_slice_in_dim(cap, (o ^ t) * cap_cols, cap_cols, 1) for t in range(GROUPS)]
        )
        stack, far, cap, own = fence((stack, far, cap, own))

        for i in range(1, steps):
            stack = jnp.concatenate([stack, far])
            far = hop_step(stack, i)
        near_latents = gather_outer(own)
        cap = [x.reshape(inner, text_own, cap_cols) for x in xor_order(cap, o)]
        cap_mine = jnp.stack(cap, axis=1).reshape(inner * text_group, cap_cols)
        cap_part = jnp.concatenate([dot(cap_mine, caption_key), dot(cap_mine, caption_value)], 1)
        stack, far, near_latents, cap_part, cap_mine, own_cot = fence(
            (stack, far, near_latents, cap_part, cap_mine, own_cot)
        )

        near_cot = gather_outer(own_cot)
        near_latents = jnp.concatenate(near_latents)
        group_latents = fence(jnp.concatenate([near_latents, hop_core(near_latents)]))
        latents_f = group_latents.astype(FULL)
        stack = jnp.concatenate([stack, far])
        blocks = plane_order([stack[j, ..., :first_width] for j in range(inner)])
        first_weights = jnp.stack(blocks, axis=1).reshape(seq_size * piece, -1)
        qkv, out_t = first_weights[:, :qkv_width], first_weights[:, qkv_width:]
        shift_parts = [one_part(stack[j, ..., first_width:].reshape(shift_shape)) for j in range(inner)]
        shifts = sum(plane_order(shift_parts))
        scale_attn, gate_attn, scale_ffn, gate_ffn = [
            shifts[:, k * width : (k + 1) * width] for k in range(4)
        ]
        first_table = attn_gain * (1.0 + scale_attn)
        second_table = ffn_gain * (1.0 + scale_ffn)
        attn_tanh_table = jnp.tanh(gate_attn)
        ffn_tanh_table = jnp.tanh(gate_ffn)
        first_mult = by_clip(first_table, clip)
        normed = (latents_f * inverse_rms(latents_f) * first_mult).astype(LOW)
        raw = dot(qkv, normed, (0, 1))
        queries, both = project(raw, gain_q, gain_k, cosine, sine, heads)
        both, cap_part, queries, near_cot, gate_in, up_in, down_in = fence(
            (both, cap_part, queries, near_cot, gate_proj, up_proj, down_proj)
        )

        hidden_width = gate_proj.shape[1] // GROUPS
        late = []
        for t in range(GROUPS):
            at = (o ^ t) * hidden_width
            late.append(
                jnp.concatenate(
                    [
                        lax.dynamic_slice_in_dim(gate_in, at, hidden_width, 1),
                        lax.dynamic_slice_in_dim(up_in, at, hidden_width, 1),
                        lax.dynamic_slice_in_dim(down_in, at, hidden_width, 0).T,
                    ],
                    axis=1,
                )
            )
        late = hops_outer(late)
        for i in range(steps):
            far = hop_step(both, i)
            keep = cap_part.shape[0] // 2
            cap_far = hop_step(cap_part[keep:].astype(LOW), steps - 1 - i)
            if i == steps - 1:
                both, far, cap_part, cap_far, late = fence((both, far, cap_part, cap_far, late))
            else:
                both, far, cap_part, cap_far = fence((both, far, cap_part, cap_far))
            cap_part = cap_part[:keep] + cap_far.astype(FULL)
            if i < steps - 1:
                both = jnp.concatenate([both, far], axis=1)
        kvs = (both, far)
        tags = tuple(tag_columns)

        cap_sent = []
        for t in range(GROUPS):
            at = (o ^ t) * inner_width
            pair = [
                lax.dynamic_slice_in_dim(cap_part, half_at + at, inner_width, 1)
                for half_at in (0, GROUPS * inner_width)
            ]
            cap_sent.append(jnp.concatenate(pair, axis=1))
        cap_z = hops_outer([cap_sent[0]] + [x.astype(LOW) for x in cap_sent[1:]])
        late = jnp.stack(xor_order(late, o))[None]
        late_far = hop_step(late, 0)
        self_out, self_inv = attend(queries, clip_row, kvs, tags, heads)
        cap_z, self_out = fence((cap_z, self_out))

        cap_both, cap_key_raw = project_caption(cap_z, gain_c, heads)
        cap_both = [cap_both] + [hop_slot(cap_both, j) for j in range(1, inner)]
        cap_both, late, late_far = fence((cap_both, late, late_far))
        cap_both = jnp.concatenate(cap_both, axis=1)

        for i in range(1, steps):
            late = jnp.concatenate([late, late_far])
            late_far = hop_step(late, i)
        cross_out, cross_inv, mixed = attend(
            queries, clip_row, (cap_both,), (text_clip,), heads, gates, self_out
        )
        near, far = send_core(dot(mixed, out_t, (0, 1)))
        sent = fence(parts_of(near, far))

        attended_parts = hops_outer(sent)
        attended_parts, near_cot = fence((attended_parts, near_cot))

        attended = summed(attended_parts)
        attn_tanh = by_clip(attn_tanh_table, own_clip)
        hidden = inputs + attn_tanh * attended
        second_mult = by_clip(second_table, own_clip)
        ffn_own = (hidden * inverse_rms(hidden) * second_mult).astype(LOW)
        ffn_near = gather_outer(ffn_own)
        ffn_tanh = by_clip(ffn_tanh_table, own_clip)
        near_cot = jnp.concatenate(near_cot)
        group_cot = jnp.concatenate([near_cot, hop_core(near_cot)]).astype(FULL)
        d_ffn = (by_clip(ffn_tanh_table, clip) * group_cot).astype(LOW)
        late, late_far = fence((late, late_far))
        ffn_weights = assemble(late, late_far, slots)
        ffn_near, ffn_weights, d_ffn = fence((ffn_near, ffn_weights, d_ffn))

        ffn_near = jnp.concatenate(ffn_near)
        halves = (ffn_near, hop_core(ffn_near))
        activation, d_gate_up, near, far = feed_forward(halves, d_ffn, ffn_weights)
        sent, activation, d_gate_up = fence((parts_of(near, hop_core(far)), activation, d_gate_up))

        def slots_outer(parts):
            parts = parts.reshape(GROUPS, piece, -1)
            return hops_outer(
                [pick(parts, o)] + [pick(parts, o ^ t).astype(LOW) for t in range(1, GROUPS)]
            )

        d_ffn_parts = hops_outer(sent)
        plane_list = jnp.stack(planes).astype(jnp.int32)
        ffn_out_near, ffn_out_far, ffn_grads, grads_far = feed_forward_grads(
            halves, d_ffn, ffn_weights, activation, d_gate_up, plane_list, GROUPS
        )
        d_ffn_parts[1], ffn_out_near, ffn_out_far, ffn_grads, grads_far = fence(
            (d_ffn_parts[1], ffn_out_near, ffn_out_far, ffn_grads, grads_far)
        )
        ffn_grads = ffn_grads.reshape(-1, 3 * hidden_width)
        grads_far = hop_step(grads_far.reshape(ffn_grads.shape), steps - 1)
        for i in reversed(range(1, steps - 1)):
            ffn_grads = ffn_grads.astype(FULL) + grads_far.astype(FULL)
            keep = ffn_grads.shape[0] // 2
            grads_far = hop_step(ffn_grads[keep:].astype(LOW), i)
            ffn_grads = ffn_grads[:keep]
        d_ffn_parts = fence(d_ffn_parts)

        d_ffn_input = summed(d_ffn_parts)
        second_back, second_terms = norm_back(hidden, second_mult, d_ffn_input)
        d_hidden = upstream + second_back
        near, ffn_out_far = fence(((attn_tanh * d_hidden).astype(LOW), ffn_out_far))
        near = gather_outer(near)
        ffn_out_far = hop_core(ffn_out_far)
        near, ffn_grads, grads_far, ffn_out_far = fence((near, ffn_grads, grads_far, ffn_out_far))

        near = jnp.concatenate(near)
        d_attended = fence(jnp.concatenate([near, hop_core(near)]))
        d_mixed = dot(out_t, d_attended, (0, 1)).astype(LOW)
        d_mixed, ffn_out_near, ffn_out_far, ffn_grads, grads_far = fence(
            (d_mixed, ffn_out_near, ffn_out_far, ffn_grads, grads_far)
        )
        ffn_out_parts = send_outer(ffn_out_near, ffn_out_far)
        ffn_grads = ffn_grads.astype(FULL) + grads_far.astype(FULL)
        keep = ffn_grads.shape[0] // 2
        grads_far = hop_step(ffn_grads[keep:].astype(LOW), 0)
        dq_cross, cap_back, gate_terms = attend_back(
            queries,
            clip_row,
            (cap_both,),
            (text_clip,),
            heads,
            cross_inv,
            d_mixed,
            cross_out,
            FULL,
            gates,
        )
        cap_keep = cap_back.shape[1] // 2
        cap_far = hop_step(cap_back[:, cap_keep:].astype(LOW), steps - 1)
        dq_far, kv_far = attend_back(
            queries, clip_row, kvs[1:], tags[1:], heads, self_inv, d_mixed, self_out, LOW
        )
        kv_far, cap_back, cap_far, d_mixed, ffn_out_parts, ffn_grads, grads_far = fence(
            (kv_far, cap_back, cap_far, d_mixed, ffn_out_parts, ffn_grads, grads_far)
        )

        far = hop_step(kv_far, steps - 1)
        ffn_grads = ffn_grads[:keep] + grads_far.astype(FULL)
        ffn_blocks = slots_outer(ffn_grads)
        dq_near, kv_near = attend_back(
            queries, clip_row, kvs[:1], tags[:1], heads, self_inv, d_mixed, self_out, FULL
        )
        far, kv_near = fence((far, kv_near))

        cap_back = cap_back[:, :cap_keep] + cap_far.astype(FULL)
        for i in reversed(range(steps - 1)):
            kv_near = kv_near + far.astype(FULL)
            kv_keep = kv_near.shape[1] // 2
            far = hop_step(kv_near[:, kv_keep:].astype(LOW), i)
            cap_keep = cap_back.shape[1] // 2
            cap_far = hop_step(cap_back[:, cap_keep:].astype(LOW), i)
            kv_near = kv_near[:, :kv_keep]
            cap_back = cap_back[:, :cap_keep]
            if i:
                cap_back = cap_back + cap_far.astype(FULL)
        far, kv_near, cap_far, cap_back, ffn_blocks = fence((far, kv_near, cap_far, cap_back, ffn_blocks))

        d_qkv, query_terms, key_terms, attn_near, attn_far = project_back(
            raw,
            gain_q,
            gain_k,
            cosine,
            sine,
            heads,
            (dq_far, dq_near, dq_cross),
            kv_near,
            far,
            (normed, mixed, d_attended),
            plane_list,
            GROUPS,
        )
        attn_near = attn_near.reshape(-1, first_width)
        attn_far = attn_far.reshape(-1, first_width)
        near, far, first_sums = normed_back(d_qkv, first_weights, group_latents, clip_column, clips)
        near, far, attn_far, gate_terms, ffn_out_parts, first_sums, cap_back = fence(
            (near, far, attn_far, gate_terms, ffn_out_parts, first_sums, cap_back)
        )
        d_cap, cap_terms = project_caption_back(cap_key_raw, gain_c, heads, cap_back, cap_far)

        place = (core * GROUPS + o).reshape(1).astype(jnp.int32)
        output, small = small_sums(
            first_sums,
            (d_hidden, attended, second_terms),
            ffn_out_parts,
            upstream,
            hidden,
            ffn_tanh,
            own_clip_column,
            (query_terms, key_terms, cap_terms),
            gate_terms,
            gates,
            place,
            2 * GROUPS,
        )
        lanes = width // 2
        small = small.reshape(-1, 2, lanes)
        small = pick(small, core, 1) + hop_core(pick(small, 1 - core, 1))
        sent, attn_far, small, d_cap = fence((parts_of(near, hop_core(far)), attn_far, small, d_cap))

        def with_small(rows):
            return jnp.concatenate([rows, two_parts(small).reshape(-1, first_width)])

        attn_back = hop_step(with_small(attn_far), steps - 1)
        d_normed_parts = hops_outer(sent)
        d_cap_parts = gather_outer(d_cap)
        attn_near, attn_back, small, d_normed_parts, ffn_blocks = fence(
            (attn_near, attn_back, small, d_normed_parts, ffn_blocks)
        )

        count = attn_near.shape[0]
        attn_grads = attn_near + attn_back[:count].astype(FULL)
        small = two_round(small) + one_part(attn_back[count:].reshape((2,) + small.shape))
        for i in reversed(range(steps - 1)):
            keep = attn_grads.shape[0] // 2
            back = hop_step(with_small(attn_grads[keep:].astype(LOW)), i)
            attn_grads = attn_grads[:keep] + back[:keep].astype(FULL)
            small = two_round(small) + one_part(back[keep:].reshape((2,) + small.shape))
        attn_grads, small, d_cap_parts, ffn_blocks = fence(
            (attn_grads, small, d_cap_parts, ffn_blocks)
        )

        parts = attn_grads.reshape(GROUPS, piece, -1)
        attn_blocks = [pick(parts, o)]
        attn_blocks += [
            hop_outer(with_small(pick(parts, o ^ t).astype(LOW)), t) for t in range(1, GROUPS)
        ]
        smalls = [two_round(small)]
        smalls += [one_part(x[piece:].reshape((2,) + small.shape)) for x in attn_blocks[1:]]
        attn_blocks = attn_blocks[:1] + [x[:piece] for x in attn_blocks[1:]]
        small = sum(xor_order(smalls, o))
        both = jnp.stack([small, hop_core(small)])
        small = jnp.concatenate([pick(both, core), pick(both, 1 - core)], axis=1)
        d_cap = jnp.stack(xor_order(d_cap_parts, o)).reshape(GROUPS, 2, inner_width, text_group)
        d_cap = jnp.swapaxes(d_cap, 0, 1).reshape(2 * GROUPS * inner_width, text_group)
        d_cap_all = [d_cap] + [hop_slot(d_cap, j) for j in range(1, inner)]

        d_cap = jnp.concatenate(d_cap_all, axis=1)
        cap_width = caption_key.shape[1]
        grad_cap_key = dot(cap_mine, d_cap[:cap_width], (0, 1))
        grad_cap_value = dot(cap_mine, d_cap[cap_width:], (0, 1))

        grad_gate, grad_up, grad_down = place_columns(ffn_blocks, o, 3)
        grad_query, grad_key, grad_value, grad_output = place_columns(attn_blocks, o, 4)
        d_normed = summed(d_normed_parts)
        own_mult = by_clip(first_table, own_clip)
        first_back, _ = norm_back(inputs, own_mult, d_normed)
        grad_latents = (d_hidden + first_back).astype(LOW)

        first_sum, attended_sum, second_sum, out_sum = [
            small[k * clips : (k + 1) * clips] for k in range(4)
        ]
        g_query, g_key, g_cap = [small[4 * clips + k, :hd] for k in range(3)]
        g_cross = small[4 * clips + 3, : 2 * GROUPS * heads]
        g_attn = jnp.sum(first_sum * (1.0 + scale_attn), axis=0)
        g_ffn = jnp.sum(second_sum * (1.0 + scale_ffn), axis=0)
        shift_grad = jnp.concatenate(
            [
                first_sum * attn_gain,
                attended_sum * (1.0 - attn_tanh_table**2),
                second_sum * ffn_gain,
                out_sum * (1.0 - ffn_tanh_table**2),
            ],
            axis=1,
        )
        g_cross = pick(g_cross.reshape(2, -1), core)
        silu_f = silu_own.astype(FULL)
        grad_modulation = sum(silu_f[k][:, None] * shift_grad[k][None, :] for k in range(clips))

        def whole_rows(x):
            both = jnp.stack([x, hop_core(x)])
            return jnp.concatenate([pick(both, core), pick(both, 1 - core)])

        return (
            whole_rows(output),
            whole_rows(grad_latents),
            grad_query,
            grad_key,
            grad_value,
            grad_output.T,
            grad_cap_key,
            grad_cap_value,
            grad_gate,
            grad_up,
            grad_down.T,
            grad_modulation,
            g_query,
            g_key,
            g_cap,
            g_attn,
            g_ffn,
            g_cross,
        )

    return body


def solution(mesh):
    rows, cols, turned = P("seq", None), P("seq", "head"), P("head", "seq")
    one = P()
    placed = (rows, rows, one, one, one, cols, cols, cols, turned, cols, cols, cols, cols, turned)
    placed += (rows, one, one, one, one, one, P("head"), rows)
    given = (rows, rows, cols, cols, cols, turned, cols, cols, cols, cols, turned, rows)
    given += (one, one, one, one, one, P("head"))
    return jax.shard_map(
        make_body(mesh.shape["seq"]), mesh=mesh, in_specs=placed, out_specs=given, check_vma=False
    )
```

```python
import math

import jax
import jax.numpy as jnp
from jax import lax
from jax.experimental import pallas as pl
from jax.experimental.pallas import tpu as pltpu
from jax.sharding import PartitionSpec as P

TEXT = 256
FRAME = 385
GROUPS = 4
EPSILON = 1e-06
LOW = jnp.bfloat16
FULL = jnp.float32


def token_layout(clip_frames, valid_patches, ids):
    clips = clip_frames.shape[0]
    upto = jnp.arange(clips)[None, :] <= jnp.arange(clips)[:, None]
    ends = FRAME * jnp.sum(jnp.where(upto, clip_frames[None, :], 0), axis=1)
    starts = ends - FRAME * clip_frames
    clip = jnp.sum((ends[None, :] <= ids[:, None]).astype(jnp.int32), axis=1)
    chosen = (clip[:, None] == jnp.arange(clips, dtype=jnp.int32)[None, :]).astype(jnp.int32)
    position = ids - jnp.sum(chosen * starts[None, :], axis=1)
    within = position % FRAME
    limit = jnp.sum(chosen * valid_patches[None, :], axis=1)
    tag = jnp.where((within < limit) | (within == FRAME - 1), clip, -1)
    return clip, position, tag


def inverse_rms(values, axis=-1):
    return lax.rsqrt(jnp.mean(values * values, axis=axis, keepdims=True) + EPSILON)


def norm_back(raw, gain, grad, axis=-1):
    inverse = inverse_rms(raw, axis)
    unit = raw * inverse
    scaled = grad * gain
    back = inverse * (scaled - unit * jnp.mean(scaled * unit, axis=axis, keepdims=True))
    return back, grad * unit


def dot(left, right, contract=(1, 0)):
    dims = (((contract[0],), (contract[1],)), ((), ()))
    return lax.dot_general(left, right, dims, preferred_element_type=FULL)


def by_clip(table, clip):
    out = table[0][None]
    for k in range(1, table.shape[0]):
        out = jnp.where(clip[:, None] == k, table[k][None], out)
    return out


def clip_sums(values, clip, clips):
    return jnp.stack(
        [jnp.sum(jnp.where(clip[:, None] == k, values, 0.0), axis=0) for k in range(clips)]
    )


def xor_order(blocks, index):
    blocks = list(blocks)
    bit = 1
    while bit < len(blocks):
        on = (index & bit) != 0
        blocks = [jnp.where(on, blocks[j ^ bit], blocks[j]) for j in range(len(blocks))]
        bit *= 2
    return blocks


def pick(stack, index, axis=0):
    return lax.dynamic_index_in_dim(stack, index, axis, keepdims=False)


def low_round(x):
    return lax.reduce_precision(x, 8, 7)


def two_parts(x):
    upper = low_round(x)
    return jnp.stack([upper, low_round(x - upper)]).astype(LOW)


def two_round(x):
    upper = low_round(x)
    return upper + low_round(x - upper)


def one_part(x):
    return x[0].astype(FULL) + x[1].astype(FULL)


def chunk_of(keys):
    return 512 if keys % 512 == 0 else keys


def padded_bytes(shape, dtype):
    size = jnp.dtype(dtype).itemsize
    rows, lanes = (1,) * (2 - len(shape)) + tuple(shape[-2:])
    tile = 32 // size
    return math.prod(shape[:-2]) * (-(-rows // tile) * tile) * (-(-lanes // 128) * 128) * size


def kernel_call(body, ins, outs, scratch=(), scalars=-1):
    space, small = [pl.BlockSpec(memory_space=m) for m in (pltpu.VMEM, pltpu.SMEM)]
    held = sum(padded_bytes(x.shape, x.dtype) for x in (*ins, *outs))
    held += sum(padded_bytes(x.shape, x.dtype) for x in scratch)
    return pl.pallas_call(
        body,
        out_shape=outs,
        in_specs=[small if i == scalars else space for i in range(len(ins))],
        out_specs=[space] * len(outs),
        scratch_shapes=list(scratch),
        compiler_params=pltpu.CompilerParams(vmem_limit_bytes=min(held + (8 << 20), 56 << 20)),
        cost_estimate=pl.CostEstimate(flops=1000, bytes_accessed=1000, transcendentals=0),
    )(*ins)


def project(raw, gain_q, gain_k, cosine, sine, heads):
    hd = gain_q.shape[0]
    half, width, rows = hd // 2, heads * hd, raw.shape[1]
    scale = 1.0 / math.sqrt(hd)

    def body(raw_ref, gq_ref, gk_ref, cos_ref, sin_ref, q_ref, kv_ref):
        c, s = cos_ref[...], sin_ref[...]
        for part, gain_ref, out_ref in ((0, gq_ref, q_ref), (1, gk_ref, kv_ref)):
            for h in range(heads):
                u = raw_ref[pl.ds(part * width + h * hd, hd), :]
                n = u * inverse_rms(u, 0) * gain_ref[...]
                a, b = n[:half], n[half:]
                turned = jnp.concatenate([a * c - b * s, a * s + b * c], axis=0).astype(LOW)
                if part == 0:
                    turned = (turned.astype(FULL) * scale).astype(LOW)
                out_ref[pl.ds(h * hd, hd), :] = turned
        kv_ref[pl.ds(width, width), :] = raw_ref[pl.ds(2 * width, width), :].astype(LOW)

    outs = (jax.ShapeDtypeStruct((width, rows), LOW), jax.ShapeDtypeStruct((2 * width, rows), LOW))
    return kernel_call(body, (raw, gain_q, gain_k, cosine, sine), outs)


def row_sums(terms):
    wide = terms[:, :128]
    for at in range(128, terms.shape[1], 128):
        wide = wide + terms[:, at : at + 128]
    return jnp.sum(wide.T, axis=0, keepdims=True)


def project_back(raw, gain_q, gain_k, cosine, sine, heads, dqs, kv_near, kv_far, left, planes, groups):
    hd = gain_q.shape[0]
    half, width, rows = hd // 2, heads * hd, raw.shape[1]
    normed, mixed, d_attended = left
    inner, features = planes.shape[0], normed.shape[1]
    piece = features // (inner * groups)
    n = len(dqs)
    lanes = features // 4

    def body(*refs):
        raw_ref, gq_ref, gk_ref, cos_ref, sin_ref = refs[:5]
        dq_refs, rest = refs[5 : 5 + n], refs[5 + n :]
        n_ref, f_ref, x_ref, m_ref, a_ref, p_ref, out_ref, tq, tk, near_ref, far_ref, g_ref = rest
        c, s = cos_ref[...], sin_ref[...]
        for part, gain_ref, term_ref in ((0, gq_ref, tq), (1, gk_ref, tk)):
            terms = jnp.zeros((hd, rows), FULL)
            for h in range(heads):
                at = pl.ds(h * hd, hd)
                if part == 0:
                    grad = dq_refs[0][at, :]
                    for ref in dq_refs[1:]:
                        grad = grad + ref[at, :]
                else:
                    grad = n_ref[at, :] + f_ref[at, :].astype(FULL)
                x, y = grad[:half], grad[half:]
                grad = jnp.concatenate([x * c + y * s, y * c - x * s], axis=0)
                where = pl.ds(part * width + h * hd, hd)
                back, term = norm_back(raw_ref[where, :], gain_ref[...], grad, 0)
                out_ref[where, :] = back.astype(LOW)
                terms = terms + term
            term_ref[...] = row_sums(terms)
        at = pl.ds(width, width)
        out_ref[pl.ds(2 * width, width), :] = (n_ref[at, :] + f_ref[at, :].astype(FULL)).astype(LOW)
        turned = out_ref[...].T
        mix = m_ref[...].T
        for k in range(4):
            at = pl.ds(k * lanes, lanes)
            one = dot(x_ref[:, at], turned, (0, 0))
            two = dot(a_ref[:, at], mix, (0, 0))
            g_ref[at, :] = jnp.concatenate([one, two], axis=1)
        for j in range(inner):
            for g in range(groups):
                start = pl.multiple_of((g * inner + p_ref[j]) * piece, 8)
                block = g_ref[pl.ds(start, piece), :]
                if j < inner // 2:
                    near_ref[j * groups + g] = block
                else:
                    far_ref[(j - inner // 2) * groups + g] = block.astype(LOW)

    row = jax.ShapeDtypeStruct((1, hd), FULL)
    blocks = (inner * groups // 2, piece, 4 * width)
    outs = (jax.ShapeDtypeStruct((3 * width, rows), LOW), row, row)
    outs += (jax.ShapeDtypeStruct(blocks, FULL), jax.ShapeDtypeStruct(blocks, LOW))
    ins = (raw, gain_q, gain_k, cosine, sine, *dqs, kv_near, kv_far, normed, mixed, d_attended, planes)
    scratch = [pltpu.VMEM((features, 4 * width), FULL)]
    return kernel_call(body, ins, outs, scratch, len(ins) - 1)


def place_columns(blocks, index, count):
    groups = len(blocks)
    rows, w = blocks[0].shape[0], blocks[0].shape[1] // count

    def body(index_ref, *refs):
        here = index_ref[0]
        block_refs, out_refs = refs[:groups], refs[groups:]
        for g in range(groups):
            for k in range(count):
                at = pl.ds(k * w, w)
                x = block_refs[0][:, at].astype(FULL)
                for t in range(1, groups):
                    x = jnp.where(here == (g ^ t), block_refs[t][:, at].astype(FULL), x)
                out_refs[k][:, pl.ds(g * w, w)] = x

    outs = [jax.ShapeDtypeStruct((rows, groups * w), FULL)] * count
    return kernel_call(body, (index.reshape(1), *blocks), outs, (), 0)


def project_caption(parts, gain, heads):
    hd = gain.shape[0]
    width, rows = heads * hd, parts[0].shape[0]

    def body(*refs):
        part_refs, gain_ref, out_ref, raw_ref = refs[:-3], refs[-3], refs[-2], refs[-1]
        total = part_refs[0][...]
        for ref in part_refs[1:]:
            total = total + ref[...].astype(FULL)
        total = total.T
        raw_ref[...] = total[:width]
        for h in range(heads):
            u = total[h * hd : (h + 1) * hd]
            out_ref[pl.ds(h * hd, hd), :] = (u * inverse_rms(u, 0) * gain_ref[...]).astype(LOW)
        out_ref[pl.ds(width, width), :] = total[width:].astype(LOW)

    outs = (jax.ShapeDtypeStruct((2 * width, rows), LOW), jax.ShapeDtypeStruct((width, rows), FULL))
    return kernel_call(body, (*parts, gain), outs)


def project_caption_back(raw, gain, heads, near, far):
    hd = gain.shape[0]
    width, rows = raw.shape

    def body(raw_ref, gain_ref, n_ref, f_ref, out_ref, term_ref):
        total = n_ref[...] + f_ref[...].astype(FULL)
        terms = jnp.zeros((hd, rows), FULL)
        for h in range(heads):
            at = slice(h * hd, (h + 1) * hd)
            back, term = norm_back(raw_ref[at, :], gain_ref[...], total[at], 0)
            out_ref[at, :] = back.astype(LOW)
            terms = terms + term
        term_ref[...] = (row_sums(terms) if rows % 128 == 0 else jnp.sum(terms.T, axis=0, keepdims=True))
        out_ref[width:, :] = total[width:].astype(LOW)

    outs = (jax.ShapeDtypeStruct((2 * width, rows), LOW), jax.ShapeDtypeStruct((1, hd), FULL))
    return kernel_call(body, (raw, gain, near, far), outs)


def attend(query, clip, kvs, tags, heads, gates=None, other=None):
    width, rows = query.shape
    hd = width // heads
    n = len(kvs)

    def body(*refs):
        q_ref, clip_ref = refs[:2]
        kv_refs, tag_refs = refs[2 : 2 + n], refs[2 + n : 2 + 2 * n]
        rest = refs[2 + 2 * n :]
        if gates is not None:
            gate_ref, other_ref, out_ref, inv_ref, mix_ref = rest
        else:
            out_ref, inv_ref = rest
        here = clip_ref[...]
        sums = [(jnp.zeros((1, rows), FULL), jnp.zeros((hd, rows), FULL)) for _ in range(heads)]
        for kv_ref, tag_ref in zip(kv_refs, tag_refs):
            count = chunk_of(kv_ref.shape[1])

            def chunk(i, carry):
                at = pl.ds(pl.multiple_of(i * count, count), count)
                allowed = tag_ref[at, :] == here
                out = []
                for h in range(heads):
                    total, acc = carry[h]
                    key = kv_ref[pl.ds(h * hd, hd), at]
                    value = kv_ref[pl.ds(width + h * hd, hd), at]
                    scores = dot(key, q_ref[pl.ds(h * hd, hd), :], (0, 0))
                    weights = jnp.where(allowed, jnp.exp(scores), 0.0)
                    total = total + jnp.sum(weights, axis=0, keepdims=True)
                    out.append((total, acc + dot(value, weights.astype(LOW))))
                return out

            sums = lax.fori_loop(0, kv_ref.shape[1] // count, chunk, sums)
        for h in range(heads):
            total, acc = sums[h]
            inverse = 1.0 / total
            inv_ref[pl.ds(h, 1), :] = inverse
            out_ref[pl.ds(h * hd, hd), :] = acc * inverse
            if gates is not None:
                own = pl.ds(h * hd, hd)
                mix_ref[own, :] = (other_ref[own, :] + gate_ref[own, :] * (acc * inverse)).astype(LOW)

    ins = (query, clip, *kvs, *tags)
    outs = (jax.ShapeDtypeStruct((width, rows), FULL), jax.ShapeDtypeStruct((heads, rows), FULL))
    if gates is not None:
        ins += (gates, other)
        outs += (jax.ShapeDtypeStruct((width, rows), LOW),)
    return kernel_call(body, ins, outs)


def attend_back(query, clip, kvs, tags, heads, inverse, grad, out, kind, gates=None):
    width, rows = query.shape
    hd = width // heads
    n = len(kvs)
    scale = 1.0 / math.sqrt(hd)

    def body(*refs):
        q_ref, clip_ref, inv_ref, given_ref, o_ref = refs[:5]
        kv_refs, tag_refs = refs[5 : 5 + n], refs[5 + n : 5 + 2 * n]
        here = clip_ref[...]
        if gates is None:
            dq_ref, back_refs = refs[5 + 2 * n], refs[6 + 2 * n :]
            grad_ref = given_ref
        else:
            gate_ref, dq_ref, back_refs = refs[5 + 2 * n], refs[6 + 2 * n], refs[7 + 2 * n :]
            back_refs, sum_ref, grad_ref = back_refs[:n], back_refs[n], back_refs[n + 1]
        deltas = []
        for h in range(heads):
            own = pl.ds(h * hd, hd)
            if gates is not None:
                given = given_ref[own, :].astype(FULL)
                grad_ref[own, :] = (gate_ref[own, :] * given).astype(LOW)
                sum_ref[pl.ds(h, 1), :] = jnp.sum(given * o_ref[own, :], axis=0, keepdims=True)
            terms = grad_ref[own, :].astype(FULL) * o_ref[own, :]
            deltas.append(jnp.sum(terms, axis=0, keepdims=True))
        sums = [jnp.zeros((hd, rows), FULL) for _ in range(heads)]
        for kv_ref, tag_ref, back_ref in zip(kv_refs, tag_refs, back_refs):
            count = chunk_of(kv_ref.shape[1])

            def chunk(i, carry):
                at = pl.ds(pl.multiple_of(i * count, count), count)
                allowed = tag_ref[at, :] == here
                out = []
                for h in range(heads):
                    own = pl.ds(h * hd, hd)
                    key = kv_ref[own, at]
                    value = kv_ref[pl.ds(width + h * hd, hd), at]
                    scores = dot(key, q_ref[own, :], (0, 0))
                    prob = jnp.where(allowed, jnp.exp(scores), 0.0) * inv_ref[pl.ds(h, 1), :]
                    d_prob = dot(value, grad_ref[own, :], (0, 0))
                    ds = (prob * (d_prob - deltas[h])).astype(LOW)
                    back_ref[own, at] = dot(q_ref[own, :], ds, (1, 1)).astype(back_ref.dtype)
                    back_ref[pl.ds(width + h * hd, hd), at] = dot(
                        grad_ref[own, :], prob.astype(LOW), (1, 1)
                    ).astype(back_ref.dtype)
                    out.append(carry[h] + dot(key, ds))
                return out

            sums = lax.fori_loop(0, kv_ref.shape[1] // count, chunk, sums)
        for h in range(heads):
            dq_ref[pl.ds(h * hd, hd), :] = sums[h] * scale

    outs = [jax.ShapeDtypeStruct((width, rows), FULL)]
    outs += [jax.ShapeDtypeStruct(x.shape, kind) for x in kvs]
    ins = (query, clip, inverse, grad, out, *kvs, *tags)
    scratch = []
    if gates is not None:
        ins += (gates,)
        outs.append(jax.ShapeDtypeStruct((heads, rows), FULL))
        scratch = [pltpu.VMEM((width, rows), LOW)]
    return kernel_call(body, ins, outs, scratch)


def assemble(near, far, slots):
    half, groups, piece, columns = near.shape

    def body(s_ref, a_ref, b_ref, out_ref):
        for q in range(2 * half):
            at = s_ref[q]

            @pl.when(at < half)
            def _():
                for g in range(groups):
                    out_ref[g, q] = a_ref[at, g]

            @pl.when(at >= half)
            def _():
                for g in range(groups):
                    out_ref[g, q] = b_ref[at - half, g]

    shape = (groups, 2 * half, piece, columns)
    (out,) = kernel_call(body, (slots, near, far), (jax.ShapeDtypeStruct(shape, near.dtype),), (), 0)
    return out.reshape(-1, columns)


def feed_forward(halves, d_ffn, weights):
    count, width = halves[0].shape
    hidden = weights.shape[1] // 3

    def body(a_ref, b_ref, d_ref, w_ref, act_ref, dgu_ref, near_ref, far_ref):
        for k, (x_ref, out_ref) in enumerate(((a_ref, near_ref), (b_ref, far_ref))):
            at = pl.ds(k * count, count)
            gate_up = w_ref[:, pl.ds(0, 2 * hidden)]
            both = dot(x_ref[...], gate_up)
            d_act = dot(d_ref[at, :], w_ref[:, pl.ds(2 * hidden, hidden)])
            gate, up = both[:, :hidden], both[:, hidden:]
            sigma = 1.0 / (1.0 + jnp.exp(-gate))
            act_ref[at, :] = (gate * sigma * up).astype(LOW)
            d_gate = (d_act * up * sigma * (1.0 + gate * (1.0 - sigma))).astype(LOW)
            dgu_ref[at, pl.ds(0, hidden)] = d_gate
            dgu_ref[at, pl.ds(hidden, hidden)] = (d_act * gate * sigma).astype(LOW)
            out_ref[...] = dot(dgu_ref[at, :], gate_up, (1, 1)).astype(out_ref.dtype)

    outs = (
        jax.ShapeDtypeStruct((2 * count, hidden), LOW),
        jax.ShapeDtypeStruct((2 * count, 2 * hidden), LOW),
        jax.ShapeDtypeStruct((count, width), FULL),
        jax.ShapeDtypeStruct((count, width), LOW),
    )
    return kernel_call(body, (*halves, d_ffn, weights), outs)


def feed_forward_grads(halves, d_ffn, weights, activation, d_gate_up, planes, groups):
    count, width = halves[0].shape
    hidden = activation.shape[1]
    inner = planes.shape[0]
    piece = width // (inner * groups)
    lanes = width // 4

    def body(a_ref, b_ref, d_ref, w_ref, act_ref, dgu_ref, p_ref, near_ref, far_ref, gn_ref, gf_ref, g_ref):
        for k, out_ref in enumerate((near_ref, far_ref)):
            at = pl.ds(k * count, count)
            out_ref[...] = dot(
                act_ref[at, :], w_ref[:, pl.ds(2 * hidden, hidden)], (1, 1)
            ).astype(out_ref.dtype)
        for k in range(4):
            at = pl.ds(k * lanes, lanes)
            x = jnp.concatenate([a_ref[:, at], b_ref[:, at]], axis=0)
            g_ref[at, pl.ds(0, 2 * hidden)] = dot(x, dgu_ref[...], (0, 0))
            g_ref[at, pl.ds(2 * hidden, hidden)] = dot(d_ref[:, at], act_ref[...], (0, 0))
        for j in range(inner):
            for g in range(groups):
                start = pl.multiple_of((g * inner + p_ref[j]) * piece, 8)
                block = g_ref[pl.ds(start, piece), :].astype(LOW)
                if j < inner // 2:
                    gn_ref[j * groups + g] = block
                else:
                    gf_ref[(j - inner // 2) * groups + g] = block

    blocks = jax.ShapeDtypeStruct((inner * groups // 2, piece, 3 * hidden), LOW)
    outs = (
        jax.ShapeDtypeStruct((count, width), FULL),
        jax.ShapeDtypeStruct((count, width), LOW),
        blocks,
        blocks,
    )
    ins = (*halves, d_ffn, weights, activation, d_gate_up, planes)
    return kernel_call(body, ins, outs, [pltpu.VMEM((width, 3 * hidden), FULL)], len(ins) - 1)


def normed_back(d_qkv, qkv, latents, clip, clips):
    rows, width = latents.shape
    half, lanes = rows // 2, width // 4

    def body(d_ref, w_ref, x_ref, c_ref, near_ref, far_ref, sum_ref):
        x = x_ref[...].astype(FULL)
        inverse = inverse_rms(x)
        turned = d_ref[...].T
        for k in range(4):
            at = pl.ds(k * lanes, lanes)
            part = dot(turned, w_ref[at, pl.ds(0, turned.shape[1])], (1, 1))
            near_ref[:, at] = part[:half]
            far_ref[:, at] = part[half:].astype(LOW)
            terms = part * (x_ref[:, at].astype(FULL) * inverse)
            for c in range(clips):
                picked = jnp.where(c_ref[...] == c, terms, 0.0)
                sum_ref[pl.ds(c, 1), at] = jnp.sum(picked, axis=0, keepdims=True)

    outs = (
        jax.ShapeDtypeStruct((half, width), FULL),
        jax.ShapeDtypeStruct((half, width), LOW),
        jax.ShapeDtypeStruct((clips, width), FULL),
    )
    return kernel_call(body, (d_qkv, qkv, latents, clip), outs)


def small_sums(first, terms, ffn_parts, upstream, hidden, ffn_tanh, clip, gains, gate_terms, gates, place, slots):
    clips, width = first.shape
    d_hidden, attended, second = terms
    heads = gate_terms.shape[0]
    hd = gates.shape[0] // heads
    n = len(ffn_parts)
    rows = 4 * clips + len(gains) + 1
    padded = -(-rows // 8) * 8

    def body(p_ref, first_ref, dh_ref, at_ref, s_ref, *refs):
        part_refs, refs = refs[:n], refs[n:]
        up_ref, h_ref, t_ref, c_ref, *gain_refs, gt_ref, gate_ref, out_ref, sum_ref = refs
        ffn_out = part_refs[0][...]
        for ref in part_refs[1:]:
            ffn_out = ffn_out + ref[...].astype(FULL)
        out_ref[...] = (h_ref[...] + t_ref[...] * ffn_out).astype(LOW)
        sum_ref[...] = jnp.zeros_like(sum_ref)
        sum_ref[pl.ds(0, clips), :] = first_ref[...]
        for k, x in enumerate((dh_ref[...] * at_ref[...], s_ref[...], up_ref[...] * ffn_out)):
            for c in range(clips):
                picked = jnp.where(c_ref[...] == c, x, 0.0)
                sum_ref[pl.ds((k + 1) * clips + c, 1), :] = jnp.sum(picked, axis=0, keepdims=True)
        for k, ref in enumerate(gain_refs):
            sum_ref[pl.ds(4 * clips + k, 1), pl.ds(0, ref.shape[1])] = ref[...]
        lane = lax.broadcasted_iota(jnp.int32, (1, 128), 1)
        row = jnp.zeros((1, 128), FULL)
        for h in range(heads):
            total = jnp.sum(gt_ref[pl.ds(h, 1), :], axis=1, keepdims=True)
            gate = gate_ref[pl.ds(h * hd, 1), :]
            row = jnp.where(lane == p_ref[0] * heads + h, total * (1.0 - gate * gate), row)
        sum_ref[pl.ds(rows - 1, 1), pl.ds(0, 128)] = row

    ins = (place, first, d_hidden, attended, second, *ffn_parts, upstream, hidden, ffn_tanh, clip)
    ins += (*gains, gate_terms, gates)
    outs = (jax.ShapeDtypeStruct(hidden.shape, LOW), jax.ShapeDtypeStruct((padded, width), FULL))
    return kernel_call(body, ins, outs, (), 0)


def make_body(seq_size):
    inner = seq_size // GROUPS
    steps = inner.bit_length() - 1

    def turned(j):
        return sum(((j >> i) & 1) << (steps - 1 - i) for i in range(steps))

    def hop_outer(x, t):
        pairs = [(i, ((i // inner) ^ t) * inner + i % inner) for i in range(seq_size)]
        return lax.ppermute(x, "seq", pairs)

    def hop_core(x):
        return lax.ppermute(x, "head", [(0, 1), (1, 0)])

    def hop_slot(x, j):
        pairs = []
        for at in range(seq_size):
            for head in range(2):
                to = (at // inner) * inner + ((at % inner) ^ (j if head == 0 else turned(j)))
                pairs.append((at * 2 + head, to * 2 + head))
        return lax.ppermute(x, ("seq", "head"), pairs)

    def hop_step(x, i):
        return hop_slot(x, 1 << i)

    def gather_outer(x):
        return [x] + [hop_outer(x, t) for t in range(1, GROUPS)]

    def body(
        latents,
        caption,
        conditioning,
        clip_frames,
        valid_patches,
        query_proj,
        key_proj,
        value_proj,
        output_proj,
        caption_key,
        caption_value,
        gate_proj,
        up_proj,
        down_proj,
        modulation,
        query_gain,
        key_gain,
        caption_gain,
        attn_gain,
        ffn_gain,
        cross_gate,
        cotangent,
    ):
        rows, width = latents.shape
        half = rows // 2
        hd = query_gain.shape[0]
        heads = cross_gate.shape[0] // GROUPS
        inner_width = heads * hd
        clips = conditioning.shape[0]
        scale = 1.0 / math.sqrt(hd)
        seq = lax.axis_index("seq")
        core = lax.axis_index("head")
        o, p = seq // inner, seq % inner
        group_rows = GROUPS * rows
        piece = query_proj.shape[0]
        planes = [p ^ jnp.where(core == 0, j, turned(j)) for j in range(inner)]
        fence = lax.optimization_barrier
        place_of = jnp.arange(inner)
        relative = p ^ place_of
        turned_relative = sum(((relative >> i) & 1) << (steps - 1 - i) for i in range(steps))
        slots = jnp.where(core == 0, relative, turned_relative).astype(jnp.int32)


        def plane_order(blocks):
            index = jnp.where(
                core == 0, p, sum(((p >> i) & 1) << (steps - 1 - i) for i in range(steps))
            )
            blocks = xor_order(blocks, index)
            return [
                b if turned(j) == j else jnp.where(core == 0, b, blocks[turned(j)])
                for j, b in enumerate(blocks)
            ]

        def token_ids(plane):
            c_at = core ^ jnp.arange(2)[:, None, None]
            o_at = o ^ jnp.arange(GROUPS)[None, :, None]
            at = jnp.arange(half)[None, None, :]
            return ((o_at * inner + plane) * rows + c_at * half + at).reshape(-1).astype(jnp.int32)

        ids = token_ids(p)
        key_ids = jnp.concatenate([token_ids(q) for q in planes])
        clip, position, _ = token_layout(clip_frames, valid_patches, ids)
        _, _, tag = token_layout(clip_frames, valid_patches, key_ids)
        own_clip = clip[:half]
        clip_row = clip[None, :]
        rates = 10000.0 ** (-(jnp.arange(hd // 2, dtype=FULL) * 2.0 / hd))
        angle = position.astype(FULL)[None, :] * rates[:, None]
        cosine, sine = jnp.cos(angle), jnp.sin(angle)

        own = lax.dynamic_slice_in_dim(latents, core * half, half, 0)
        own_cot = lax.dynamic_slice_in_dim(cotangent, core * half, half, 0)
        inputs = own.astype(FULL)
        upstream = own_cot.astype(FULL)

        def send_core(partial):
            split = partial.shape[0] // 2
            return partial[:split], hop_core(partial[split:].astype(LOW))

        def parts_of(near, far):
            parts = (near + far.astype(FULL)).reshape(GROUPS, half, width)
            return [parts[0]] + [parts[t].astype(LOW) for t in range(1, GROUPS)]

        def send_outer(near, far):
            return hops_outer(parts_of(near, far))

        def summed(parts):
            total = parts[0]
            for x in parts[1:]:
                total = total + x.astype(FULL)
            return total

        def hops_outer(blocks):
            return [hop_outer(x, t) if t else x for t, x in enumerate(blocks)]

        def hops_slot(blocks):
            return [hop_slot(x, t) if t else x for t, x in enumerate(blocks)]

        silu_cond = jax.nn.silu(conditioning.astype(FULL)).astype(LOW)
        cond_rows = modulation.shape[0]
        silu_own = lax.dynamic_slice_in_dim(silu_cond, seq * cond_rows, cond_rows, 1)
        shift_part = dot(silu_own, modulation)
        shift_shape = (2,) + shift_part.shape
        qkv_width = 3 * inner_width
        first_width = 4 * inner_width
        sent = []
        for t in range(GROUPS):
            at = (o ^ t) * inner_width
            cols = [
                lax.dynamic_slice_in_dim(w, at, inner_width, 1)
                for w in (query_proj, key_proj, value_proj)
            ]
            cols.append(lax.dynamic_slice_in_dim(output_proj, at, inner_width, 0).T)
            sent.append(jnp.concatenate(cols, axis=1))
        text_own = caption.shape[0]
        text_group = GROUPS * text_own
        cap_cols = caption.shape[1] // seq_size
        shift_rows = two_parts(shift_part).reshape(-1, GROUPS * cap_cols)
        sent, caption, shift_rows = fence((sent, caption, shift_rows))
        got = hops_outer(sent)
        cap_split = caption.reshape(text_own, GROUPS, inner, cap_cols)
        cap = hops_slot(
            [
                jnp.concatenate([pick(cap_split, q, 2).reshape(text_own, -1), shift_rows])
                for q in planes
            ]
        )
        split = key_ids.shape[0] // 2
        p_at = jnp.stack(planes)[:, None, None]
        o_at = jnp.arange(GROUPS)[None, :, None]
        text_ids = (o_at * inner + p_at) * text_own + jnp.arange(text_own)[None, None, :]
        columns = [
            tag[:split][:, None],
            tag[split:][:, None],
            (text_ids // TEXT).reshape(-1, 1).astype(jnp.int32),
            clip[:, None],
            own_clip[:, None],
            query_gain[:, None],
            key_gain[:, None],
            caption_gain[:, None],
        ]
        gate_here = pick(cross_gate.reshape(GROUPS, heads), o)
        gates = jnp.broadcast_to(jnp.tanh(gate_here)[:, None, None], (heads, hd, 1))
        gates = gates.reshape(inner_width, 1)
        got, cap, own, columns, gates, cosine, sine = fence(
            (got, cap, own, columns, gates, cosine, sine)
        )
        tag_columns, text_clip, clip_column, own_clip_column = columns[:2], *columns[2:5]
        gain_q, gain_k, gain_c = columns[5:]

        shift_parts = plane_order([one_part(x[text_own:].reshape(shift_shape)) for x in cap])
        shift_rows = two_parts(sum(shift_parts)).reshape(-1, cap_cols)
        stack = jnp.stack(xor_order(got, o))[None]
        cap = jnp.concatenate([x[:text_own] for x in cap])
        far = hop_step(stack, 0)
        cap_blocks = [
            lax.dynamic_slice_in_dim(cap, (o ^ t) * cap_cols, cap_cols, 1) for t in range(GROUPS)
        ]
        cap = hops_outer([jnp.concatenate([x, shift_rows]) for x in cap_blocks])
        stack, far, cap, own = fence((stack, far, cap, own))

        for i in range(1, steps):
            stack = jnp.concatenate([stack, far])
            far = hop_step(stack, i)
        near_latents = gather_outer(own)
        cap = xor_order(cap, o)
        text_part = inner * text_own
        shifts = sum([one_part(x[text_part:].reshape(shift_shape)) for x in cap])
        cap = [x[:text_part].reshape(inner, text_own, cap_cols) for x in cap]
        cap_mine = jnp.stack(cap, axis=1).reshape(inner * text_group, cap_cols)
        cap_part = jnp.concatenate([dot(cap_mine, caption_key), dot(cap_mine, caption_value)], 1)
        stack, far, near_latents, cap_part, cap_mine, own_cot = fence(
            (stack, far, near_latents, cap_part, cap_mine, own_cot)
        )

        near_cot = gather_outer(own_cot)
        near_latents = jnp.concatenate(near_latents)
        group_latents = fence(jnp.concatenate([near_latents, hop_core(near_latents)]))
        latents_f = group_latents.astype(FULL)
        stack = jnp.concatenate([stack, far])
        blocks = plane_order([stack[j] for j in range(inner)])
        first_weights = jnp.stack(blocks, axis=1).reshape(seq_size * piece, -1)
        qkv, out_t = first_weights[:, :qkv_width], first_weights[:, qkv_width:]
        scale_attn, gate_attn, scale_ffn, gate_ffn = [
            shifts[:, k * width : (k + 1) * width] for k in range(4)
        ]
        first_table = attn_gain * (1.0 + scale_attn)
        second_table = ffn_gain * (1.0 + scale_ffn)
        attn_tanh_table = jnp.tanh(gate_attn)
        ffn_tanh_table = jnp.tanh(gate_ffn)
        first_mult = by_clip(first_table, clip)
        normed = (latents_f * inverse_rms(latents_f) * first_mult).astype(LOW)
        raw = dot(qkv, normed, (0, 1))
        queries, both = project(raw, gain_q, gain_k, cosine, sine, heads)
        both, cap_part, queries, near_cot, gate_in, up_in, down_in = fence(
            (both, cap_part, queries, near_cot, gate_proj, up_proj, down_proj)
        )

        hidden_width = gate_proj.shape[1] // GROUPS
        late = []
        for t in range(GROUPS):
            at = (o ^ t) * hidden_width
            late.append(
                jnp.concatenate(
                    [
                        lax.dynamic_slice_in_dim(gate_in, at, hidden_width, 1),
                        lax.dynamic_slice_in_dim(up_in, at, hidden_width, 1),
                        lax.dynamic_slice_in_dim(down_in, at, hidden_width, 0).T,
                    ],
                    axis=1,
                )
            )
        late = hops_outer(late)
        for i in range(steps):
            far = hop_step(both, i)
            keep = cap_part.shape[0] // 2
            cap_far = hop_step(cap_part[keep:].astype(LOW), steps - 1 - i)
            if i == steps - 1:
                both, far, cap_part, cap_far, late = fence((both, far, cap_part, cap_far, late))
            else:
                both, far, cap_part, cap_far = fence((both, far, cap_part, cap_far))
            cap_part = cap_part[:keep] + cap_far.astype(FULL)
            if i < steps - 1:
                both = jnp.concatenate([both, far], axis=1)
        kvs = (both, far)
        tags = tuple(tag_columns)

        cap_sent = []
        for t in range(GROUPS):
            at = (o ^ t) * inner_width
            pair = [
                lax.dynamic_slice_in_dim(cap_part, half_at + at, inner_width, 1)
                for half_at in (0, GROUPS * inner_width)
            ]
            cap_sent.append(jnp.concatenate(pair, axis=1))
        cap_z = hops_outer([cap_sent[0]] + [x.astype(LOW) for x in cap_sent[1:]])
        late = jnp.stack(xor_order(late, o))[None]
        late_far = hop_step(late, 0)
        self_out, self_inv = attend(queries, clip_row, kvs, tags, heads)
        cap_z, self_out = fence((cap_z, self_out))

        cap_both, cap_key_raw = project_caption(cap_z, gain_c, heads)
        cap_both = [cap_both] + [hop_slot(cap_both, j) for j in range(1, inner)]
        cap_both, late, late_far = fence((cap_both, late, late_far))
        cap_both = jnp.concatenate(cap_both, axis=1)

        for i in range(1, steps):
            late = jnp.concatenate([late, late_far])
            late_far = hop_step(late, i)
        cross_out, cross_inv, mixed = attend(
            queries, clip_row, (cap_both,), (text_clip,), heads, gates, self_out
        )
        near, far = send_core(dot(mixed, out_t, (0, 1)))
        sent = fence(parts_of(near, far))

        attended_parts = hops_outer(sent)
        attended_parts, near_cot = fence((attended_parts, near_cot))

        attended = summed(attended_parts)
        attn_tanh = by_clip(attn_tanh_table, own_clip)
        hidden = inputs + attn_tanh * attended
        second_mult = by_clip(second_table, own_clip)
        ffn_own = (hidden * inverse_rms(hidden) * second_mult).astype(LOW)
        ffn_near = gather_outer(ffn_own)
        ffn_tanh = by_clip(ffn_tanh_table, own_clip)
        near_cot = jnp.concatenate(near_cot)
        group_cot = jnp.concatenate([near_cot, hop_core(near_cot)]).astype(FULL)
        d_ffn = (by_clip(ffn_tanh_table, clip) * group_cot).astype(LOW)
        late, late_far = fence((late, late_far))
        ffn_weights = assemble(late, late_far, slots)
        ffn_near, ffn_weights, d_ffn = fence((ffn_near, ffn_weights, d_ffn))

        ffn_near = jnp.concatenate(ffn_near)
        halves = (ffn_near, hop_core(ffn_near))
        activation, d_gate_up, near, far = feed_forward(halves, d_ffn, ffn_weights)
        sent, activation, d_gate_up = fence((parts_of(near, hop_core(far)), activation, d_gate_up))

        def slots_outer(parts):
            parts = parts.reshape(GROUPS, piece, -1)
            return hops_outer(
                [pick(parts, o)] + [pick(parts, o ^ t).astype(LOW) for t in range(1, GROUPS)]
            )

        d_ffn_parts = hops_outer(sent)
        plane_list = jnp.stack(planes).astype(jnp.int32)
        ffn_out_near, ffn_out_far, ffn_grads, grads_far = feed_forward_grads(
            halves, d_ffn, ffn_weights, activation, d_gate_up, plane_list, GROUPS
        )
        d_ffn_parts[1], ffn_out_near, ffn_out_far, ffn_grads, grads_far = fence(
            (d_ffn_parts[1], ffn_out_near, ffn_out_far, ffn_grads, grads_far)
        )
        ffn_grads = ffn_grads.reshape(-1, 3 * hidden_width)
        grads_far = hop_step(grads_far.reshape(ffn_grads.shape), steps - 1)
        for i in reversed(range(1, steps - 1)):
            ffn_grads = ffn_grads.astype(FULL) + grads_far.astype(FULL)
            keep = ffn_grads.shape[0] // 2
            grads_far = hop_step(ffn_grads[keep:].astype(LOW), i)
            ffn_grads = ffn_grads[:keep]
        d_ffn_parts = fence(d_ffn_parts)

        d_ffn_input = summed(d_ffn_parts)
        second_back, second_terms = norm_back(hidden, second_mult, d_ffn_input)
        d_hidden = upstream + second_back
        near, ffn_out_far = fence(((attn_tanh * d_hidden).astype(LOW), ffn_out_far))
        near = gather_outer(near)
        ffn_out_far = hop_core(ffn_out_far)
        near, ffn_grads, grads_far, ffn_out_far = fence((near, ffn_grads, grads_far, ffn_out_far))

        near = jnp.concatenate(near)
        d_attended = fence(jnp.concatenate([near, hop_core(near)]))
        d_mixed = dot(out_t, d_attended, (0, 1)).astype(LOW)
        d_mixed, ffn_out_near, ffn_out_far, ffn_grads, grads_far = fence(
            (d_mixed, ffn_out_near, ffn_out_far, ffn_grads, grads_far)
        )
        ffn_out_parts = send_outer(ffn_out_near, ffn_out_far)
        ffn_grads = ffn_grads.astype(FULL) + grads_far.astype(FULL)
        keep = ffn_grads.shape[0] // 2
        grads_far = hop_step(ffn_grads[keep:].astype(LOW), 0)
        dq_cross, cap_back, gate_terms = attend_back(
            queries,
            clip_row,
            (cap_both,),
            (text_clip,),
            heads,
            cross_inv,
            d_mixed,
            cross_out,
            FULL,
            gates,
        )
        cap_keep = cap_back.shape[1] // 2
        cap_far = hop_step(cap_back[:, cap_keep:].astype(LOW), steps - 1)
        dq_far, kv_far = attend_back(
            queries, clip_row, kvs[1:], tags[1:], heads, self_inv, d_mixed, self_out, LOW
        )
        kv_far, cap_back, cap_far, d_mixed, ffn_out_parts, ffn_grads, grads_far = fence(
            (kv_far, cap_back, cap_far, d_mixed, ffn_out_parts, ffn_grads, grads_far)
        )

        far = hop_step(kv_far, steps - 1)
        ffn_grads = ffn_grads[:keep] + grads_far.astype(FULL)
        ffn_blocks = slots_outer(ffn_grads)
        dq_near, kv_near = attend_back(
            queries, clip_row, kvs[:1], tags[:1], heads, self_inv, d_mixed, self_out, FULL
        )
        far, kv_near = fence((far, kv_near))

        cap_back = cap_back[:, :cap_keep] + cap_far.astype(FULL)
        for i in reversed(range(steps - 1)):
            kv_near = kv_near + far.astype(FULL)
            kv_keep = kv_near.shape[1] // 2
            far = hop_step(kv_near[:, kv_keep:].astype(LOW), i)
            cap_keep = cap_back.shape[1] // 2
            cap_far = hop_step(cap_back[:, cap_keep:].astype(LOW), i)
            kv_near = kv_near[:, :kv_keep]
            cap_back = cap_back[:, :cap_keep]
            if i:
                cap_back = cap_back + cap_far.astype(FULL)
        far, kv_near, cap_far, cap_back, ffn_blocks = fence((far, kv_near, cap_far, cap_back, ffn_blocks))

        d_qkv, query_terms, key_terms, attn_near, attn_far = project_back(
            raw,
            gain_q,
            gain_k,
            cosine,
            sine,
            heads,
            (dq_far, dq_near, dq_cross),
            kv_near,
            far,
            (normed, mixed, d_attended),
            plane_list,
            GROUPS,
        )
        attn_near = attn_near.reshape(-1, first_width)
        attn_far = attn_far.reshape(-1, first_width)
        near, far, first_sums = normed_back(d_qkv, first_weights, group_latents, clip_column, clips)
        near, far, attn_far, gate_terms, ffn_out_parts, first_sums, cap_back = fence(
            (near, far, attn_far, gate_terms, ffn_out_parts, first_sums, cap_back)
        )
        d_cap, cap_terms = project_caption_back(cap_key_raw, gain_c, heads, cap_back, cap_far)

        place = (core * GROUPS + o).reshape(1).astype(jnp.int32)
        output, small = small_sums(
            first_sums,
            (d_hidden, attended, second_terms),
            ffn_out_parts,
            upstream,
            hidden,
            ffn_tanh,
            own_clip_column,
            (query_terms, key_terms, cap_terms),
            gate_terms,
            gates,
            place,
            2 * GROUPS,
        )
        lanes = width // 2
        small = small.reshape(-1, 2, lanes)
        small = pick(small, core, 1) + hop_core(pick(small, 1 - core, 1))
        sent, attn_far, small, d_cap = fence((parts_of(near, hop_core(far)), attn_far, small, d_cap))

        def with_small(rows):
            return jnp.concatenate([rows, two_parts(small).reshape(-1, first_width)])

        attn_back = hop_step(with_small(attn_far), steps - 1)
        d_normed_parts = hops_outer(sent)
        d_cap_parts = gather_outer(d_cap)
        attn_near, attn_back, small, d_normed_parts, ffn_blocks = fence(
            (attn_near, attn_back, small, d_normed_parts, ffn_blocks)
        )

        count = attn_near.shape[0]
        attn_grads = attn_near + attn_back[:count].astype(FULL)
        small = two_round(small) + one_part(attn_back[count:].reshape((2,) + small.shape))
        for i in reversed(range(steps - 1)):
            keep = attn_grads.shape[0] // 2
            back = hop_step(with_small(attn_grads[keep:].astype(LOW)), i)
            attn_grads = attn_grads[:keep] + back[:keep].astype(FULL)
            small = two_round(small) + one_part(back[keep:].reshape((2,) + small.shape))
        attn_grads, small, d_cap_parts, ffn_blocks = fence(
            (attn_grads, small, d_cap_parts, ffn_blocks)
        )

        parts = attn_grads.reshape(GROUPS, piece, -1)
        attn_blocks = [pick(parts, o)]
        attn_blocks += [
            hop_outer(with_small(pick(parts, o ^ t).astype(LOW)), t) for t in range(1, GROUPS)
        ]
        smalls = [two_round(small)]
        smalls += [one_part(x[piece:].reshape((2,) + small.shape)) for x in attn_blocks[1:]]
        attn_blocks = attn_blocks[:1] + [x[:piece] for x in attn_blocks[1:]]
        small = sum(xor_order(smalls, o))
        both = jnp.stack([small, hop_core(small)])
        small = jnp.concatenate([pick(both, core), pick(both, 1 - core)], axis=1)
        d_cap = jnp.stack(xor_order(d_cap_parts, o)).reshape(GROUPS, 2, inner_width, text_group)
        d_cap = jnp.swapaxes(d_cap, 0, 1).reshape(2 * GROUPS * inner_width, text_group)
        d_cap_all = [d_cap] + [hop_slot(d_cap, j) for j in range(1, inner)]

        d_cap = jnp.concatenate(d_cap_all, axis=1)
        cap_width = caption_key.shape[1]
        grad_cap_key = dot(cap_mine, d_cap[:cap_width], (0, 1))
        grad_cap_value = dot(cap_mine, d_cap[cap_width:], (0, 1))

        grad_gate, grad_up, grad_down = place_columns(ffn_blocks, o, 3)
        grad_query, grad_key, grad_value, grad_output = place_columns(attn_blocks, o, 4)
        d_normed = summed(d_normed_parts)
        own_mult = by_clip(first_table, own_clip)
        first_back, _ = norm_back(inputs, own_mult, d_normed)
        grad_latents = (d_hidden + first_back).astype(LOW)

        first_sum, attended_sum, second_sum, out_sum = [
            small[k * clips : (k + 1) * clips] for k in range(4)
        ]
        g_query, g_key, g_cap = [small[4 * clips + k, :hd] for k in range(3)]
        g_cross = small[4 * clips + 3, : 2 * GROUPS * heads]
        g_attn = jnp.sum(first_sum * (1.0 + scale_attn), axis=0)
        g_ffn = jnp.sum(second_sum * (1.0 + scale_ffn), axis=0)
        shift_grad = jnp.concatenate(
            [
                first_sum * attn_gain,
                attended_sum * (1.0 - attn_tanh_table**2),
                second_sum * ffn_gain,
                out_sum * (1.0 - ffn_tanh_table**2),
            ],
            axis=1,
        )
        g_cross = pick(g_cross.reshape(2, -1), core)
        silu_f = silu_own.astype(FULL)
        grad_modulation = sum(silu_f[k][:, None] * shift_grad[k][None, :] for k in range(clips))

        def whole_rows(x):
            both = jnp.stack([x, hop_core(x)])
            return jnp.concatenate([pick(both, core), pick(both, 1 - core)])

        return (
            whole_rows(output),
            whole_rows(grad_latents),
            grad_query,
            grad_key,
            grad_value,
            grad_output.T,
            grad_cap_key,
            grad_cap_value,
            grad_gate,
            grad_up,
            grad_down.T,
            grad_modulation,
            g_query,
            g_key,
            g_cap,
            g_attn,
            g_ffn,
            g_cross,
        )

    return body


def solution(mesh):
    rows, cols, turned = P("seq", None), P("seq", "head"), P("head", "seq")
    one = P()
    placed = (rows, rows, one, one, one, cols, cols, cols, turned, cols, cols, cols, cols, turned)
    placed += (rows, one, one, one, one, one, P("head"), rows)
    given = (rows, rows, cols, cols, cols, turned, cols, cols, cols, cols, turned, rows)
    given += (one, one, one, one, one, P("head"))
    return jax.shard_map(
        make_body(mesh.shape["seq"]), mesh=mesh, in_specs=placed, out_specs=given, check_vma=False
    )
```

```python
import math

import jax
import jax.numpy as jnp
from jax import lax
from jax.experimental import pallas as pl
from jax.experimental.pallas import tpu as pltpu
from jax.sharding import PartitionSpec as P

TEXT = 256
FRAME = 385
GROUPS = 4
EPSILON = 1e-06
LOW = jnp.bfloat16
FULL = jnp.float32


def token_layout(clip_frames, valid_patches, ids):
    clips = clip_frames.shape[0]
    upto = jnp.arange(clips)[None, :] <= jnp.arange(clips)[:, None]
    ends = FRAME * jnp.sum(jnp.where(upto, clip_frames[None, :], 0), axis=1)
    starts = ends - FRAME * clip_frames
    clip = jnp.sum((ends[None, :] <= ids[:, None]).astype(jnp.int32), axis=1)
    chosen = (clip[:, None] == jnp.arange(clips, dtype=jnp.int32)[None, :]).astype(jnp.int32)
    position = ids - jnp.sum(chosen * starts[None, :], axis=1)
    within = position % FRAME
    limit = jnp.sum(chosen * valid_patches[None, :], axis=1)
    tag = jnp.where((within < limit) | (within == FRAME - 1), clip, -1)
    return clip, position, tag


def inverse_rms(values, axis=-1):
    return lax.rsqrt(jnp.mean(values * values, axis=axis, keepdims=True) + EPSILON)


def norm_back(raw, gain, grad, axis=-1):
    inverse = inverse_rms(raw, axis)
    unit = raw * inverse
    scaled = grad * gain
    back = inverse * (scaled - unit * jnp.mean(scaled * unit, axis=axis, keepdims=True))
    return back, grad * unit


def dot(left, right, contract=(1, 0)):
    dims = (((contract[0],), (contract[1],)), ((), ()))
    return lax.dot_general(left, right, dims, preferred_element_type=FULL)


def by_clip(table, clip):
    out = table[0][None]
    for k in range(1, table.shape[0]):
        out = jnp.where(clip[:, None] == k, table[k][None], out)
    return out


def clip_sums(values, clip, clips):
    return jnp.stack(
        [jnp.sum(jnp.where(clip[:, None] == k, values, 0.0), axis=0) for k in range(clips)]
    )


def xor_order(blocks, index):
    blocks = list(blocks)
    bit = 1
    while bit < len(blocks):
        on = (index & bit) != 0
        blocks = [jnp.where(on, blocks[j ^ bit], blocks[j]) for j in range(len(blocks))]
        bit *= 2
    return blocks


def pick(stack, index, axis=0):
    return lax.dynamic_index_in_dim(stack, index, axis, keepdims=False)


def low_round(x):
    return lax.reduce_precision(x, 8, 7)


def two_parts(x):
    upper = low_round(x)
    return jnp.stack([upper, low_round(x - upper)]).astype(LOW)


def two_round(x):
    upper = low_round(x)
    return upper + low_round(x - upper)


def one_part(x):
    return x[0].astype(FULL) + x[1].astype(FULL)


def chunk_of(keys):
    return 512 if keys % 512 == 0 else keys


def padded_bytes(shape, dtype):
    size = jnp.dtype(dtype).itemsize
    rows, lanes = (1,) * (2 - len(shape)) + tuple(shape[-2:])
    tile = 32 // size
    return math.prod(shape[:-2]) * (-(-rows // tile) * tile) * (-(-lanes // 128) * 128) * size


def kernel_call(body, ins, outs, scratch=(), scalars=-1):
    space, small = [pl.BlockSpec(memory_space=m) for m in (pltpu.VMEM, pltpu.SMEM)]
    held = sum(padded_bytes(x.shape, x.dtype) for x in (*ins, *outs))
    held += sum(padded_bytes(x.shape, x.dtype) for x in scratch)
    return pl.pallas_call(
        body,
        out_shape=outs,
        in_specs=[small if i == scalars else space for i in range(len(ins))],
        out_specs=[space] * len(outs),
        scratch_shapes=list(scratch),
        compiler_params=pltpu.CompilerParams(vmem_limit_bytes=min(held + (8 << 20), 56 << 20)),
        cost_estimate=pl.CostEstimate(flops=1000, bytes_accessed=1000, transcendentals=0),
    )(*ins)


def project(raw, gain_q, gain_k, cosine, sine, heads):
    hd = gain_q.shape[0]
    half, width, rows = hd // 2, heads * hd, raw.shape[1]
    scale = 1.0 / math.sqrt(hd)

    def body(raw_ref, gq_ref, gk_ref, cos_ref, sin_ref, q_ref, kv_ref):
        c, s = cos_ref[...], sin_ref[...]
        for part, gain_ref, out_ref in ((0, gq_ref, q_ref), (1, gk_ref, kv_ref)):
            for h in range(heads):
                u = raw_ref[pl.ds(part * width + h * hd, hd), :]
                n = u * inverse_rms(u, 0) * gain_ref[...]
                a, b = n[:half], n[half:]
                turned = jnp.concatenate([a * c - b * s, a * s + b * c], axis=0).astype(LOW)
                if part == 0:
                    turned = (turned.astype(FULL) * scale).astype(LOW)
                out_ref[pl.ds(h * hd, hd), :] = turned
        kv_ref[pl.ds(width, width), :] = raw_ref[pl.ds(2 * width, width), :].astype(LOW)

    outs = (jax.ShapeDtypeStruct((width, rows), LOW), jax.ShapeDtypeStruct((2 * width, rows), LOW))
    return kernel_call(body, (raw, gain_q, gain_k, cosine, sine), outs)


def row_sums(terms):
    wide = terms[:, :128]
    for at in range(128, terms.shape[1], 128):
        wide = wide + terms[:, at : at + 128]
    return jnp.sum(wide.T, axis=0, keepdims=True)


def project_back(raw, gain_q, gain_k, cosine, sine, heads, dqs, kv_near, kv_far, left, planes, groups):
    hd = gain_q.shape[0]
    half, width, rows = hd // 2, heads * hd, raw.shape[1]
    normed, mixed, *d_attended = left
    inner, features = planes.shape[0], normed.shape[1]
    piece = features // (inner * groups)
    n = len(dqs)
    lanes = features // 4

    def body(*refs):
        raw_ref, gq_ref, gk_ref, cos_ref, sin_ref = refs[:5]
        dq_refs, rest = refs[5 : 5 + n], refs[5 + n :]
        n_ref, f_ref, x_ref, m_ref, a_ref, b_ref, p_ref, out_ref, tq, tk, near_ref, far_ref, g_ref = rest
        c, s = cos_ref[...], sin_ref[...]
        for part, gain_ref, term_ref in ((0, gq_ref, tq), (1, gk_ref, tk)):
            terms = jnp.zeros((hd, rows), FULL)
            for h in range(heads):
                at = pl.ds(h * hd, hd)
                if part == 0:
                    grad = dq_refs[0][at, :]
                    for ref in dq_refs[1:]:
                        grad = grad + ref[at, :]
                else:
                    grad = n_ref[at, :] + f_ref[at, :].astype(FULL)
                x, y = grad[:half], grad[half:]
                grad = jnp.concatenate([x * c + y * s, y * c - x * s], axis=0)
                where = pl.ds(part * width + h * hd, hd)
                back, term = norm_back(raw_ref[where, :], gain_ref[...], grad, 0)
                out_ref[where, :] = back.astype(LOW)
                terms = terms + term
            term_ref[...] = row_sums(terms)
        at = pl.ds(width, width)
        out_ref[pl.ds(2 * width, width), :] = (n_ref[at, :] + f_ref[at, :].astype(FULL)).astype(LOW)
        turned = out_ref[...].T
        mix = m_ref[...].T
        for k in range(4):
            at = pl.ds(k * lanes, lanes)
            one = dot(x_ref[:, at], turned, (0, 0))
            two = dot(jnp.concatenate([a_ref[:, at], b_ref[:, at]], axis=0), mix, (0, 0))
            g_ref[at, :] = jnp.concatenate([one, two], axis=1)
        for j in range(inner):
            for g in range(groups):
                start = pl.multiple_of((g * inner + p_ref[j]) * piece, 8)
                block = g_ref[pl.ds(start, piece), :]
                if j < inner // 2:
                    near_ref[j * groups + g] = block
                else:
                    far_ref[(j - inner // 2) * groups + g] = block.astype(LOW)

    row = jax.ShapeDtypeStruct((1, hd), FULL)
    blocks = (inner * groups // 2, piece, 4 * width)
    outs = (jax.ShapeDtypeStruct((3 * width, rows), LOW), row, row)
    outs += (jax.ShapeDtypeStruct(blocks, FULL), jax.ShapeDtypeStruct(blocks, LOW))
    ins = (raw, gain_q, gain_k, cosine, sine, *dqs, kv_near, kv_far, normed, mixed, *d_attended, planes)
    scratch = [pltpu.VMEM((features, 4 * width), FULL)]
    return kernel_call(body, ins, outs, scratch, len(ins) - 1)


def place_columns(blocks, index, count):
    groups = len(blocks)
    rows, w = blocks[0].shape[0], blocks[0].shape[1] // count

    def body(index_ref, *refs):
        here = index_ref[0]
        block_refs, out_refs = refs[:groups], refs[groups:]
        for g in range(groups):
            for k in range(count):
                at = pl.ds(k * w, w)
                x = block_refs[0][:, at].astype(FULL)
                for t in range(1, groups):
                    x = jnp.where(here == (g ^ t), block_refs[t][:, at].astype(FULL), x)
                out_refs[k][:, pl.ds(g * w, w)] = x

    outs = [jax.ShapeDtypeStruct((rows, groups * w), FULL)] * count
    return kernel_call(body, (index.reshape(1), *blocks), outs, (), 0)


def project_caption(parts, gain, heads):
    hd = gain.shape[0]
    width, rows = heads * hd, parts[0].shape[0]

    def body(*refs):
        part_refs, gain_ref, out_ref, raw_ref = refs[:-3], refs[-3], refs[-2], refs[-1]
        total = part_refs[0][...]
        for ref in part_refs[1:]:
            total = total + ref[...].astype(FULL)
        total = total.T
        raw_ref[...] = total[:width]
        for h in range(heads):
            u = total[h * hd : (h + 1) * hd]
            out_ref[pl.ds(h * hd, hd), :] = (u * inverse_rms(u, 0) * gain_ref[...]).astype(LOW)
        out_ref[pl.ds(width, width), :] = total[width:].astype(LOW)

    outs = (jax.ShapeDtypeStruct((2 * width, rows), LOW), jax.ShapeDtypeStruct((width, rows), FULL))
    return kernel_call(body, (*parts, gain), outs)


def project_caption_back(raw, gain, heads, near, far):
    hd = gain.shape[0]
    width, rows = raw.shape

    def body(raw_ref, gain_ref, n_ref, f_ref, out_ref, term_ref):
        total = n_ref[...] + f_ref[...].astype(FULL)
        terms = jnp.zeros((hd, rows), FULL)
        for h in range(heads):
            at = slice(h * hd, (h + 1) * hd)
            back, term = norm_back(raw_ref[at, :], gain_ref[...], total[at], 0)
            out_ref[at, :] = back.astype(LOW)
            terms = terms + term
        term_ref[...] = (row_sums(terms) if rows % 128 == 0 else jnp.sum(terms.T, axis=0, keepdims=True))
        out_ref[width:, :] = total[width:].astype(LOW)

    outs = (jax.ShapeDtypeStruct((2 * width, rows), LOW), jax.ShapeDtypeStruct((1, hd), FULL))
    return kernel_call(body, (raw, gain, near, far), outs)


def attend(query, clip, kvs, tags, heads, gates=None, other=None):
    width, rows = query.shape
    hd = width // heads
    n = len(kvs)

    def body(*refs):
        q_ref, clip_ref = refs[:2]
        kv_refs, tag_refs = refs[2 : 2 + n], refs[2 + n : 2 + 2 * n]
        rest = refs[2 + 2 * n :]
        if gates is not None:
            gate_ref, other_ref, out_ref, inv_ref, mix_ref = rest
        else:
            out_ref, inv_ref = rest
        here = clip_ref[...]
        sums = [(jnp.zeros((1, rows), FULL), jnp.zeros((hd, rows), FULL)) for _ in range(heads)]
        for kv_ref, tag_ref in zip(kv_refs, tag_refs):
            count = chunk_of(kv_ref.shape[1])

            def chunk(i, carry):
                at = pl.ds(pl.multiple_of(i * count, count), count)
                allowed = tag_ref[at, :] == here
                out = []
                for h in range(heads):
                    total, acc = carry[h]
                    key = kv_ref[pl.ds(h * hd, hd), at]
                    value = kv_ref[pl.ds(width + h * hd, hd), at]
                    scores = dot(key, q_ref[pl.ds(h * hd, hd), :], (0, 0))
                    weights = jnp.where(allowed, jnp.exp(scores), 0.0)
                    total = total + jnp.sum(weights, axis=0, keepdims=True)
                    out.append((total, acc + dot(value, weights.astype(LOW))))
                return out

            sums = lax.fori_loop(0, kv_ref.shape[1] // count, chunk, sums)
        for h in range(heads):
            total, acc = sums[h]
            inverse = 1.0 / total
            inv_ref[pl.ds(h, 1), :] = inverse
            out_ref[pl.ds(h * hd, hd), :] = acc * inverse
            if gates is not None:
                own = pl.ds(h * hd, hd)
                mix_ref[own, :] = (other_ref[own, :] + gate_ref[own, :] * (acc * inverse)).astype(LOW)

    ins = (query, clip, *kvs, *tags)
    outs = (jax.ShapeDtypeStruct((width, rows), FULL), jax.ShapeDtypeStruct((heads, rows), FULL))
    if gates is not None:
        ins += (gates, other)
        outs += (jax.ShapeDtypeStruct((width, rows), LOW),)
    return kernel_call(body, ins, outs)


def attend_back(query, clip, kvs, tags, heads, inverse, grad, out, kind, gates=None):
    width, rows = query.shape
    hd = width // heads
    n = len(kvs)
    scale = 1.0 / math.sqrt(hd)

    def body(*refs):
        q_ref, clip_ref, inv_ref, given_ref, o_ref = refs[:5]
        kv_refs, tag_refs = refs[5 : 5 + n], refs[5 + n : 5 + 2 * n]
        here = clip_ref[...]
        if gates is None:
            dq_ref, back_refs = refs[5 + 2 * n], refs[6 + 2 * n :]
            grad_ref = given_ref
        else:
            gate_ref, dq_ref, back_refs = refs[5 + 2 * n], refs[6 + 2 * n], refs[7 + 2 * n :]
            back_refs, sum_ref, grad_ref = back_refs[:n], back_refs[n], back_refs[n + 1]
        deltas = []
        for h in range(heads):
            own = pl.ds(h * hd, hd)
            if gates is not None:
                given = given_ref[own, :].astype(FULL)
                grad_ref[own, :] = (gate_ref[own, :] * given).astype(LOW)
                sum_ref[pl.ds(h, 1), :] = jnp.sum(given * o_ref[own, :], axis=0, keepdims=True)
            terms = grad_ref[own, :].astype(FULL) * o_ref[own, :]
            deltas.append(jnp.sum(terms, axis=0, keepdims=True))
        sums = [jnp.zeros((hd, rows), FULL) for _ in range(heads)]
        for kv_ref, tag_ref, back_ref in zip(kv_refs, tag_refs, back_refs):
            count = chunk_of(kv_ref.shape[1])

            def chunk(i, carry):
                at = pl.ds(pl.multiple_of(i * count, count), count)
                allowed = tag_ref[at, :] == here
                out = []
                for h in range(heads):
                    own = pl.ds(h * hd, hd)
                    key = kv_ref[own, at]
                    value = kv_ref[pl.ds(width + h * hd, hd), at]
                    scores = dot(key, q_ref[own, :], (0, 0))
                    prob = jnp.where(allowed, jnp.exp(scores), 0.0) * inv_ref[pl.ds(h, 1), :]
                    d_prob = dot(value, grad_ref[own, :], (0, 0))
                    ds = (prob * (d_prob - deltas[h])).astype(LOW)
                    back_ref[own, at] = dot(q_ref[own, :], ds, (1, 1)).astype(back_ref.dtype)
                    back_ref[pl.ds(width + h * hd, hd), at] = dot(
                        grad_ref[own, :], prob.astype(LOW), (1, 1)
                    ).astype(back_ref.dtype)
                    out.append(carry[h] + dot(key, ds))
                return out

            sums = lax.fori_loop(0, kv_ref.shape[1] // count, chunk, sums)
        for h in range(heads):
            dq_ref[pl.ds(h * hd, hd), :] = sums[h] * scale

    outs = [jax.ShapeDtypeStruct((width, rows), FULL)]
    outs += [jax.ShapeDtypeStruct(x.shape, kind) for x in kvs]
    ins = (query, clip, inverse, grad, out, *kvs, *tags)
    scratch = []
    if gates is not None:
        ins += (gates,)
        outs.append(jax.ShapeDtypeStruct((heads, rows), FULL))
        scratch = [pltpu.VMEM((width, rows), LOW)]
    return kernel_call(body, ins, outs, scratch)


def assemble(near, far, slots):
    half, groups, piece, columns = near.shape

    def body(s_ref, a_ref, b_ref, out_ref):
        for q in range(2 * half):
            at = s_ref[q]

            @pl.when(at < half)
            def _():
                for g in range(groups):
                    out_ref[g, q] = a_ref[at, g]

            @pl.when(at >= half)
            def _():
                for g in range(groups):
                    out_ref[g, q] = b_ref[at - half, g]

    shape = (groups, 2 * half, piece, columns)
    (out,) = kernel_call(body, (slots, near, far), (jax.ShapeDtypeStruct(shape, near.dtype),), (), 0)
    return out.reshape(-1, columns)


def feed_forward(halves, d_ffn, weights):
    count, width = halves[0].shape
    hidden = weights.shape[1] // 3

    def body(a_ref, b_ref, d_ref, w_ref, act_ref, dgu_ref, near_ref, far_ref):
        for k, (x_ref, out_ref) in enumerate(((a_ref, near_ref), (b_ref, far_ref))):
            at = pl.ds(k * count, count)
            gate_up = w_ref[:, pl.ds(0, 2 * hidden)]
            both = dot(x_ref[...], gate_up)
            d_act = dot(d_ref[at, :], w_ref[:, pl.ds(2 * hidden, hidden)])
            gate, up = both[:, :hidden], both[:, hidden:]
            sigma = 1.0 / (1.0 + jnp.exp(-gate))
            act_ref[at, :] = (gate * sigma * up).astype(LOW)
            d_gate = (d_act * up * sigma * (1.0 + gate * (1.0 - sigma))).astype(LOW)
            dgu_ref[at, pl.ds(0, hidden)] = d_gate
            dgu_ref[at, pl.ds(hidden, hidden)] = (d_act * gate * sigma).astype(LOW)
            out_ref[...] = dot(dgu_ref[at, :], gate_up, (1, 1)).astype(out_ref.dtype)

    outs = (
        jax.ShapeDtypeStruct((2 * count, hidden), LOW),
        jax.ShapeDtypeStruct((2 * count, 2 * hidden), LOW),
        jax.ShapeDtypeStruct((count, width), FULL),
        jax.ShapeDtypeStruct((count, width), LOW),
    )
    return kernel_call(body, (*halves, d_ffn, weights), outs)


def feed_forward_grads(halves, d_ffn, weights, activation, d_gate_up, planes, groups):
    count, width = halves[0].shape
    hidden = activation.shape[1]
    inner = planes.shape[0]
    piece = width // (inner * groups)
    lanes = width // 4

    def body(a_ref, b_ref, d_ref, w_ref, act_ref, dgu_ref, p_ref, near_ref, far_ref, gn_ref, gf_ref, g_ref):
        for k, out_ref in enumerate((near_ref, far_ref)):
            at = pl.ds(k * count, count)
            out_ref[...] = dot(
                act_ref[at, :], w_ref[:, pl.ds(2 * hidden, hidden)], (1, 1)
            ).astype(out_ref.dtype)
        for k in range(4):
            at = pl.ds(k * lanes, lanes)
            x = jnp.concatenate([a_ref[:, at], b_ref[:, at]], axis=0)
            g_ref[at, pl.ds(0, 2 * hidden)] = dot(x, dgu_ref[...], (0, 0))
            g_ref[at, pl.ds(2 * hidden, hidden)] = dot(d_ref[:, at], act_ref[...], (0, 0))
        for j in range(inner):
            for g in range(groups):
                start = pl.multiple_of((g * inner + p_ref[j]) * piece, 8)
                block = g_ref[pl.ds(start, piece), :].astype(LOW)
                if j < inner // 2:
                    gn_ref[j * groups + g] = block
                else:
                    gf_ref[(j - inner // 2) * groups + g] = block

    blocks = jax.ShapeDtypeStruct((inner * groups // 2, piece, 3 * hidden), LOW)
    outs = (
        jax.ShapeDtypeStruct((count, width), FULL),
        jax.ShapeDtypeStruct((count, width), LOW),
        blocks,
        blocks,
    )
    ins = (*halves, d_ffn, weights, activation, d_gate_up, planes)
    return kernel_call(body, ins, outs, [pltpu.VMEM((width, 3 * hidden), FULL)], len(ins) - 1)


def normed_back(d_qkv, qkv, latents, clip, clips):
    rows, width = latents.shape
    half, lanes = rows // 2, width // 4

    def body(d_ref, w_ref, x_ref, c_ref, near_ref, far_ref, sum_ref):
        x = x_ref[...].astype(FULL)
        inverse = inverse_rms(x)
        turned = d_ref[...].T
        for k in range(4):
            at = pl.ds(k * lanes, lanes)
            part = dot(turned, w_ref[at, pl.ds(0, turned.shape[1])], (1, 1))
            near_ref[:, at] = part[:half]
            far_ref[:, at] = part[half:].astype(LOW)
            terms = part * (x_ref[:, at].astype(FULL) * inverse)
            for c in range(clips):
                picked = jnp.where(c_ref[...] == c, terms, 0.0)
                sum_ref[pl.ds(c, 1), at] = jnp.sum(picked, axis=0, keepdims=True)

    outs = (
        jax.ShapeDtypeStruct((half, width), FULL),
        jax.ShapeDtypeStruct((half, width), LOW),
        jax.ShapeDtypeStruct((clips, width), FULL),
    )
    return kernel_call(body, (d_qkv, qkv, latents, clip), outs)


def small_sums(first, terms, ffn_parts, upstream, hidden, ffn_tanh, clip, gains, gate_terms, gates, place, slots):
    clips, width = first.shape
    d_hidden, attended, second = terms
    heads = gate_terms.shape[0]
    hd = gates.shape[0] // heads
    n = len(ffn_parts)
    rows = 4 * clips + len(gains) + 1
    padded = -(-rows // 8) * 8

    def body(p_ref, first_ref, dh_ref, at_ref, s_ref, *refs):
        part_refs, refs = refs[:n], refs[n:]
        up_ref, h_ref, t_ref, c_ref, *gain_refs, gt_ref, gate_ref, out_ref, sum_ref = refs
        ffn_out = part_refs[0][...]
        for ref in part_refs[1:]:
            ffn_out = ffn_out + ref[...].astype(FULL)
        out_ref[...] = (h_ref[...] + t_ref[...] * ffn_out).astype(LOW)
        sum_ref[...] = jnp.zeros_like(sum_ref)
        sum_ref[pl.ds(0, clips), :] = first_ref[...]
        for k, x in enumerate((dh_ref[...] * at_ref[...], s_ref[...], up_ref[...] * ffn_out)):
            for c in range(clips):
                picked = jnp.where(c_ref[...] == c, x, 0.0)
                sum_ref[pl.ds((k + 1) * clips + c, 1), :] = jnp.sum(picked, axis=0, keepdims=True)
        for k, ref in enumerate(gain_refs):
            sum_ref[pl.ds(4 * clips + k, 1), pl.ds(0, ref.shape[1])] = ref[...]
        lane = lax.broadcasted_iota(jnp.int32, (1, 128), 1)
        row = jnp.zeros((1, 128), FULL)
        for h in range(heads):
            total = jnp.sum(gt_ref[pl.ds(h, 1), :], axis=1, keepdims=True)
            gate = gate_ref[pl.ds(h * hd, 1), :]
            row = jnp.where(lane == p_ref[0] * heads + h, total * (1.0 - gate * gate), row)
        sum_ref[pl.ds(rows - 1, 1), pl.ds(0, 128)] = row

    ins = (place, first, d_hidden, attended, second, *ffn_parts, upstream, hidden, ffn_tanh, clip)
    ins += (*gains, gate_terms, gates)
    outs = (jax.ShapeDtypeStruct(hidden.shape, LOW), jax.ShapeDtypeStruct((padded, width), FULL))
    return kernel_call(body, ins, outs, (), 0)


def make_body(seq_size):
    inner = seq_size // GROUPS
    steps = inner.bit_length() - 1

    def turned(j):
        return sum(((j >> i) & 1) << (steps - 1 - i) for i in range(steps))

    def hop_outer(x, t):
        pairs = [(i, ((i // inner) ^ t) * inner + i % inner) for i in range(seq_size)]
        return lax.ppermute(x, "seq", pairs)

    def hop_core(x):
        return lax.ppermute(x, "head", [(0, 1), (1, 0)])

    def hop_slot(x, j):
        pairs = []
        for at in range(seq_size):
            for head in range(2):
                to = (at // inner) * inner + ((at % inner) ^ (j if head == 0 else turned(j)))
                pairs.append((at * 2 + head, to * 2 + head))
        return lax.ppermute(x, ("seq", "head"), pairs)

    def hop_step(x, i):
        return hop_slot(x, 1 << i)

    def gather_outer(x):
        return [x] + [hop_outer(x, t) for t in range(1, GROUPS)]

    def body(
        latents,
        caption,
        conditioning,
        clip_frames,
        valid_patches,
        query_proj,
        key_proj,
        value_proj,
        output_proj,
        caption_key,
        caption_value,
        gate_proj,
        up_proj,
        down_proj,
        modulation,
        query_gain,
        key_gain,
        caption_gain,
        attn_gain,
        ffn_gain,
        cross_gate,
        cotangent,
    ):
        rows, width = latents.shape
        half = rows // 2
        hd = query_gain.shape[0]
        heads = cross_gate.shape[0] // GROUPS
        inner_width = heads * hd
        clips = conditioning.shape[0]
        scale = 1.0 / math.sqrt(hd)
        seq = lax.axis_index("seq")
        core = lax.axis_index("head")
        o, p = seq // inner, seq % inner
        group_rows = GROUPS * rows
        piece = query_proj.shape[0]
        planes = [p ^ jnp.where(core == 0, j, turned(j)) for j in range(inner)]
        fence = lax.optimization_barrier
        place_of = jnp.arange(inner)
        relative = p ^ place_of
        turned_relative = sum(((relative >> i) & 1) << (steps - 1 - i) for i in range(steps))
        slots = jnp.where(core == 0, relative, turned_relative).astype(jnp.int32)


        def plane_order(blocks):
            index = jnp.where(
                core == 0, p, sum(((p >> i) & 1) << (steps - 1 - i) for i in range(steps))
            )
            blocks = xor_order(blocks, index)
            return [
                b if turned(j) == j else jnp.where(core == 0, b, blocks[turned(j)])
                for j, b in enumerate(blocks)
            ]

        def token_ids(plane):
            c_at = core ^ jnp.arange(2)[:, None, None]
            o_at = o ^ jnp.arange(GROUPS)[None, :, None]
            at = jnp.arange(half)[None, None, :]
            return ((o_at * inner + plane) * rows + c_at * half + at).reshape(-1).astype(jnp.int32)

        ids = token_ids(p)
        key_ids = jnp.concatenate([token_ids(q) for q in planes])
        clip, position, _ = token_layout(clip_frames, valid_patches, ids)
        _, _, tag = token_layout(clip_frames, valid_patches, key_ids)
        own_clip = clip[:half]
        clip_row = clip[None, :]
        rates = 10000.0 ** (-(jnp.arange(hd // 2, dtype=FULL) * 2.0 / hd))
        angle = position.astype(FULL)[None, :] * rates[:, None]
        cosine, sine = jnp.cos(angle), jnp.sin(angle)

        own = lax.dynamic_slice_in_dim(latents, core * half, half, 0)
        own_cot = lax.dynamic_slice_in_dim(cotangent, core * half, half, 0)
        inputs = own.astype(FULL)
        upstream = own_cot.astype(FULL)

        def send_core(partial):
            split = partial.shape[0] // 2
            return partial[:split], hop_core(partial[split:].astype(LOW))

        def parts_of(near, far):
            parts = (near + far.astype(FULL)).reshape(GROUPS, half, width)
            return [parts[0]] + [parts[t].astype(LOW) for t in range(1, GROUPS)]

        def send_outer(near, far):
            return hops_outer(parts_of(near, far))

        def summed(parts):
            total = parts[0]
            for x in parts[1:]:
                total = total + x.astype(FULL)
            return total

        def hops_outer(blocks):
            return [hop_outer(x, t) if t else x for t, x in enumerate(blocks)]

        def hops_slot(blocks):
            return [hop_slot(x, t) if t else x for t, x in enumerate(blocks)]

        silu_cond = jax.nn.silu(conditioning.astype(FULL)).astype(LOW)
        cond_rows = modulation.shape[0]
        silu_own = lax.dynamic_slice_in_dim(silu_cond, seq * cond_rows, cond_rows, 1)
        shift_part = dot(silu_own, modulation)
        shift_shape = (2,) + shift_part.shape
        qkv_width = 3 * inner_width
        first_width = 4 * inner_width
        sent = []
        for t in range(GROUPS):
            at = (o ^ t) * inner_width
            cols = [
                lax.dynamic_slice_in_dim(w, at, inner_width, 1)
                for w in (query_proj, key_proj, value_proj)
            ]
            cols.append(lax.dynamic_slice_in_dim(output_proj, at, inner_width, 0).T)
            sent.append(jnp.concatenate(cols, axis=1))
        text_own = caption.shape[0]
        text_group = GROUPS * text_own
        cap_cols = caption.shape[1] // seq_size
        shift_rows = two_parts(shift_part).reshape(-1, GROUPS * cap_cols)
        sent, caption, shift_rows = fence((sent, caption, shift_rows))
        got = hops_outer(sent)
        cap_split = caption.reshape(text_own, GROUPS, inner, cap_cols)
        cap = hops_slot(
            [
                jnp.concatenate([pick(cap_split, q, 2).reshape(text_own, -1), shift_rows])
                for q in planes
            ]
        )
        split = key_ids.shape[0] // 2
        p_at = jnp.stack(planes)[:, None, None]
        o_at = jnp.arange(GROUPS)[None, :, None]
        text_ids = (o_at * inner + p_at) * text_own + jnp.arange(text_own)[None, None, :]
        columns = [
            tag[:split][:, None],
            tag[split:][:, None],
            (text_ids // TEXT).reshape(-1, 1).astype(jnp.int32),
            clip[:, None],
            own_clip[:, None],
            query_gain[:, None],
            key_gain[:, None],
            caption_gain[:, None],
        ]
        gate_here = pick(cross_gate.reshape(GROUPS, heads), o)
        gates = jnp.broadcast_to(jnp.tanh(gate_here)[:, None, None], (heads, hd, 1))
        gates = gates.reshape(inner_width, 1)
        got, cap, own, columns, gates, cosine, sine = fence(
            (got, cap, own, columns, gates, cosine, sine)
        )
        tag_columns, text_clip, clip_column, own_clip_column = columns[:2], *columns[2:5]
        gain_q, gain_k, gain_c = columns[5:]

        shift_parts = plane_order([one_part(x[text_own:].reshape(shift_shape)) for x in cap])
        shift_rows = two_parts(sum(shift_parts)).reshape(-1, cap_cols)
        stack = jnp.stack(xor_order(got, o))[None]
        cap = jnp.concatenate([x[:text_own] for x in cap])
        far = hop_step(stack, 0)
        cap_blocks = [
            lax.dynamic_slice_in_dim(cap, (o ^ t) * cap_cols, cap_cols, 1) for t in range(GROUPS)
        ]
        cap = hops_outer([jnp.concatenate([x, shift_rows]) for x in cap_blocks])
        stack, far, cap, own = fence((stack, far, cap, own))

        for i in range(1, steps):
            stack = jnp.concatenate([stack, far])
            far = hop_step(stack, i)
        near_latents = gather_outer(own)
        cap = xor_order(cap, o)
        text_part = inner * text_own
        shifts = sum([one_part(x[text_part:].reshape(shift_shape)) for x in cap])
        cap = [x[:text_part].reshape(inner, text_own, cap_cols) for x in cap]
        cap_mine = jnp.stack(cap, axis=1).reshape(inner * text_group, cap_cols)
        cap_part = jnp.concatenate([dot(cap_mine, caption_key), dot(cap_mine, caption_value)], 1)
        stack, far, near_latents, cap_part, cap_mine, own_cot = fence(
            (stack, far, near_latents, cap_part, cap_mine, own_cot)
        )

        near_cot = gather_outer(own_cot)
        near_latents = jnp.concatenate(near_latents)
        group_latents = fence(jnp.concatenate([near_latents, hop_core(near_latents)]))
        latents_f = group_latents.astype(FULL)
        stack = jnp.concatenate([stack, far])
        blocks = plane_order([stack[j] for j in range(inner)])
        first_weights = jnp.stack(blocks, axis=1).reshape(seq_size * piece, -1)
        qkv, out_t = first_weights[:, :qkv_width], first_weights[:, qkv_width:]
        scale_attn, gate_attn, scale_ffn, gate_ffn = [
            shifts[:, k * width : (k + 1) * width] for k in range(4)
        ]
        first_table = attn_gain * (1.0 + scale_attn)
        second_table = ffn_gain * (1.0 + scale_ffn)
        attn_tanh_table = jnp.tanh(gate_attn)
        ffn_tanh_table = jnp.tanh(gate_ffn)
        first_mult = by_clip(first_table, clip)
        normed = (latents_f * inverse_rms(latents_f) * first_mult).astype(LOW)
        raw = dot(qkv, normed, (0, 1))
        queries, both = project(raw, gain_q, gain_k, cosine, sine, heads)
        both, cap_part, queries, near_cot, gate_in, up_in, down_in = fence(
            (both, cap_part, queries, near_cot, gate_proj, up_proj, down_proj)
        )

        hidden_width = gate_proj.shape[1] // GROUPS
        late = []
        for t in range(GROUPS):
            at = (o ^ t) * hidden_width
            late.append(
                jnp.concatenate(
                    [
                        lax.dynamic_slice_in_dim(gate_in, at, hidden_width, 1),
                        lax.dynamic_slice_in_dim(up_in, at, hidden_width, 1),
                        lax.dynamic_slice_in_dim(down_in, at, hidden_width, 0).T,
                    ],
                    axis=1,
                )
            )
        late = hops_outer(late)
        for i in range(steps):
            far = hop_step(both, i)
            keep = cap_part.shape[0] // 2
            cap_far = hop_step(cap_part[keep:].astype(LOW), steps - 1 - i)
            if i == steps - 1:
                both, far, cap_part, cap_far, late = fence((both, far, cap_part, cap_far, late))
            else:
                both, far, cap_part, cap_far = fence((both, far, cap_part, cap_far))
            cap_part = cap_part[:keep] + cap_far.astype(FULL)
            if i < steps - 1:
                both = jnp.concatenate([both, far], axis=1)
        kvs = (both, far)
        tags = tuple(tag_columns)

        cap_sent = []
        for t in range(GROUPS):
            at = (o ^ t) * inner_width
            pair = [
                lax.dynamic_slice_in_dim(cap_part, half_at + at, inner_width, 1)
                for half_at in (0, GROUPS * inner_width)
            ]
            cap_sent.append(jnp.concatenate(pair, axis=1))
        cap_z = hops_outer([cap_sent[0]] + [x.astype(LOW) for x in cap_sent[1:]])
        late = jnp.stack(xor_order(late, o))[None]
        late_far = hop_step(late, 0)
        self_out, self_inv = attend(queries, clip_row, kvs, tags, heads)
        cap_z, self_out = fence((cap_z, self_out))

        cap_both, cap_key_raw = project_caption(cap_z, gain_c, heads)
        cap_both = [cap_both] + [hop_slot(cap_both, j) for j in range(1, inner)]
        cap_both, late, late_far = fence((cap_both, late, late_far))
        cap_both = jnp.concatenate(cap_both, axis=1)

        for i in range(1, steps):
            late = jnp.concatenate([late, late_far])
            late_far = hop_step(late, i)
        cross_out, cross_inv, mixed = attend(
            queries, clip_row, (cap_both,), (text_clip,), heads, gates, self_out
        )
        near, far = send_core(dot(mixed, out_t, (0, 1)))
        sent = fence(parts_of(near, far))

        attended_parts = hops_outer(sent)
        attended_parts, near_cot = fence((attended_parts, near_cot))

        attended = summed(attended_parts)
        attn_tanh = by_clip(attn_tanh_table, own_clip)
        hidden = inputs + attn_tanh * attended
        second_mult = by_clip(second_table, own_clip)
        ffn_own = (hidden * inverse_rms(hidden) * second_mult).astype(LOW)
        ffn_near = gather_outer(ffn_own)
        ffn_tanh = by_clip(ffn_tanh_table, own_clip)
        near_cot = jnp.concatenate(near_cot)
        group_cot = jnp.concatenate([near_cot, hop_core(near_cot)]).astype(FULL)
        d_ffn = (by_clip(ffn_tanh_table, clip) * group_cot).astype(LOW)
        late, late_far = fence((late, late_far))
        ffn_weights = assemble(late, late_far, slots)
        ffn_near, ffn_weights, d_ffn = fence((ffn_near, ffn_weights, d_ffn))

        ffn_near = jnp.concatenate(ffn_near)
        halves = (ffn_near, hop_core(ffn_near))
        activation, d_gate_up, near, far = feed_forward(halves, d_ffn, ffn_weights)
        sent, activation, d_gate_up = fence((parts_of(near, hop_core(far)), activation, d_gate_up))

        def slots_outer(parts):
            parts = parts.reshape(GROUPS, piece, -1)
            return hops_outer(
                [pick(parts, o)] + [pick(parts, o ^ t).astype(LOW) for t in range(1, GROUPS)]
            )

        d_ffn_parts = hops_outer(sent)
        plane_list = jnp.stack(planes).astype(jnp.int32)
        ffn_out_near, ffn_out_far, ffn_grads, grads_far = feed_forward_grads(
            halves, d_ffn, ffn_weights, activation, d_gate_up, plane_list, GROUPS
        )
        d_ffn_parts[1], ffn_out_near, ffn_out_far, ffn_grads, grads_far = fence(
            (d_ffn_parts[1], ffn_out_near, ffn_out_far, ffn_grads, grads_far)
        )
        ffn_grads = ffn_grads.reshape(-1, 3 * hidden_width)
        grads_far = hop_step(grads_far.reshape(ffn_grads.shape), steps - 1)
        for i in reversed(range(1, steps - 1)):
            ffn_grads = ffn_grads.astype(FULL) + grads_far.astype(FULL)
            keep = ffn_grads.shape[0] // 2
            grads_far = hop_step(ffn_grads[keep:].astype(LOW), i)
            ffn_grads = ffn_grads[:keep]
        d_ffn_parts = fence(d_ffn_parts)

        d_ffn_input = summed(d_ffn_parts)
        second_back, second_terms = norm_back(hidden, second_mult, d_ffn_input)
        d_hidden = upstream + second_back
        near, ffn_out_far = fence(((attn_tanh * d_hidden).astype(LOW), ffn_out_far))
        near = gather_outer(near)
        ffn_out_far = hop_core(ffn_out_far)
        near, ffn_grads, grads_far, ffn_out_far = fence((near, ffn_grads, grads_far, ffn_out_far))

        near = jnp.concatenate(near)
        d_attended = (near, hop_core(near))
        d_mixed = jnp.concatenate([dot(out_t, x, (0, 1)).astype(LOW) for x in d_attended], axis=1)
        d_mixed, ffn_out_near, ffn_out_far, ffn_grads, grads_far = fence(
            (d_mixed, ffn_out_near, ffn_out_far, ffn_grads, grads_far)
        )
        ffn_out_parts = send_outer(ffn_out_near, ffn_out_far)
        ffn_grads = ffn_grads.astype(FULL) + grads_far.astype(FULL)
        keep = ffn_grads.shape[0] // 2
        grads_far = hop_step(ffn_grads[keep:].astype(LOW), 0)
        dq_cross, cap_back, gate_terms = attend_back(
            queries,
            clip_row,
            (cap_both,),
            (text_clip,),
            heads,
            cross_inv,
            d_mixed,
            cross_out,
            FULL,
            gates,
        )
        cap_keep = cap_back.shape[1] // 2
        cap_far = hop_step(cap_back[:, cap_keep:].astype(LOW), steps - 1)
        dq_far, kv_far = attend_back(
            queries, clip_row, kvs[1:], tags[1:], heads, self_inv, d_mixed, self_out, LOW
        )
        kv_far, cap_back, cap_far, d_mixed, ffn_out_parts, ffn_grads, grads_far = fence(
            (kv_far, cap_back, cap_far, d_mixed, ffn_out_parts, ffn_grads, grads_far)
        )

        far = hop_step(kv_far, steps - 1)
        ffn_grads = ffn_grads[:keep] + grads_far.astype(FULL)
        ffn_blocks = slots_outer(ffn_grads)
        dq_near, kv_near = attend_back(
            queries, clip_row, kvs[:1], tags[:1], heads, self_inv, d_mixed, self_out, FULL
        )
        far, kv_near = fence((far, kv_near))

        cap_back = cap_back[:, :cap_keep] + cap_far.astype(FULL)
        for i in reversed(range(steps - 1)):
            kv_near = kv_near + far.astype(FULL)
            kv_keep = kv_near.shape[1] // 2
            far = hop_step(kv_near[:, kv_keep:].astype(LOW), i)
            cap_keep = cap_back.shape[1] // 2
            cap_far = hop_step(cap_back[:, cap_keep:].astype(LOW), i)
            kv_near = kv_near[:, :kv_keep]
            cap_back = cap_back[:, :cap_keep]
            if i:
                cap_back = cap_back + cap_far.astype(FULL)
        far, kv_near, cap_far, cap_back = fence((far, kv_near, cap_far, cap_back))

        d_qkv, query_terms, key_terms, attn_near, attn_far = project_back(
            raw,
            gain_q,
            gain_k,
            cosine,
            sine,
            heads,
            (dq_far, dq_near, dq_cross),
            kv_near,
            far,
            (normed, mixed, *d_attended),
            plane_list,
            GROUPS,
        )
        attn_near = attn_near.reshape(-1, first_width)
        attn_far = attn_far.reshape(-1, first_width)
        near, far, first_sums = normed_back(d_qkv, first_weights, group_latents, clip_column, clips)
        near, far, attn_far, gate_terms, ffn_out_parts, first_sums, cap_back, ffn_blocks = fence(
            (near, far, attn_far, gate_terms, ffn_out_parts, first_sums, cap_back, ffn_blocks)
        )
        d_cap, cap_terms = project_caption_back(cap_key_raw, gain_c, heads, cap_back, cap_far)

        place = (core * GROUPS + o).reshape(1).astype(jnp.int32)
        output, small = small_sums(
            first_sums,
            (d_hidden, attended, second_terms),
            ffn_out_parts,
            upstream,
            hidden,
            ffn_tanh,
            own_clip_column,
            (query_terms, key_terms, cap_terms),
            gate_terms,
            gates,
            place,
            2 * GROUPS,
        )
        lanes = width // 2
        small = small.reshape(-1, 2, lanes)
        small = pick(small, core, 1) + hop_core(pick(small, 1 - core, 1))
        sent, attn_far, small, d_cap = fence((parts_of(near, hop_core(far)), attn_far, small, d_cap))

        def with_small(rows):
            return jnp.concatenate([rows, two_parts(small).reshape(-1, first_width)])

        attn_back = hop_step(with_small(attn_far), steps - 1)
        d_normed_parts = hops_outer(sent)
        d_cap_parts = gather_outer(d_cap)
        attn_near, attn_back, small, d_normed_parts, ffn_blocks = fence(
            (attn_near, attn_back, small, d_normed_parts, ffn_blocks)
        )

        count = attn_near.shape[0]
        attn_grads = attn_near + attn_back[:count].astype(FULL)
        small = two_round(small) + one_part(attn_back[count:].reshape((2,) + small.shape))
        for i in reversed(range(steps - 1)):
            keep = attn_grads.shape[0] // 2
            back = hop_step(with_small(attn_grads[keep:].astype(LOW)), i)
            attn_grads = attn_grads[:keep] + back[:keep].astype(FULL)
            small = two_round(small) + one_part(back[keep:].reshape((2,) + small.shape))
        attn_grads, small, d_cap_parts, ffn_blocks = fence(
            (attn_grads, small, d_cap_parts, ffn_blocks)
        )

        parts = attn_grads.reshape(GROUPS, piece, -1)
        attn_blocks = [pick(parts, o)]
        attn_blocks += [
            hop_outer(with_small(pick(parts, o ^ t).astype(LOW)), t) for t in range(1, GROUPS)
        ]
        smalls = [two_round(small)]
        smalls += [one_part(x[piece:].reshape((2,) + small.shape)) for x in attn_blocks[1:]]
        attn_blocks = attn_blocks[:1] + [x[:piece] for x in attn_blocks[1:]]
        small = sum(xor_order(smalls, o))
        both = jnp.stack([small, hop_core(small)])
        small = jnp.concatenate([pick(both, core), pick(both, 1 - core)], axis=1)
        d_cap = jnp.stack(xor_order(d_cap_parts, o)).reshape(GROUPS, 2, inner_width, text_group)
        d_cap = jnp.swapaxes(d_cap, 0, 1).reshape(2 * GROUPS * inner_width, text_group)
        d_cap_all = [d_cap] + [hop_slot(d_cap, j) for j in range(1, inner)]

        d_cap = jnp.concatenate(d_cap_all, axis=1)
        cap_width = caption_key.shape[1]
        grad_cap_key = dot(cap_mine, d_cap[:cap_width], (0, 1))
        grad_cap_value = dot(cap_mine, d_cap[cap_width:], (0, 1))

        grad_gate, grad_up, grad_down = place_columns(ffn_blocks, o, 3)
        grad_query, grad_key, grad_value, grad_output = place_columns(attn_blocks, o, 4)
        d_normed = summed(d_normed_parts)
        own_mult = by_clip(first_table, own_clip)
        first_back, _ = norm_back(inputs, own_mult, d_normed)
        grad_latents = (d_hidden + first_back).astype(LOW)

        first_sum, attended_sum, second_sum, out_sum = [
            small[k * clips : (k + 1) * clips] for k in range(4)
        ]
        g_query, g_key, g_cap = [small[4 * clips + k, :hd] for k in range(3)]
        g_cross = small[4 * clips + 3, : 2 * GROUPS * heads]
        g_attn = jnp.sum(first_sum * (1.0 + scale_attn), axis=0)
        g_ffn = jnp.sum(second_sum * (1.0 + scale_ffn), axis=0)
        shift_grad = jnp.concatenate(
            [
                first_sum * attn_gain,
                attended_sum * (1.0 - attn_tanh_table**2),
                second_sum * ffn_gain,
                out_sum * (1.0 - ffn_tanh_table**2),
            ],
            axis=1,
        )
        g_cross = pick(g_cross.reshape(2, -1), core)
        silu_f = silu_own.astype(FULL)
        grad_modulation = sum(silu_f[k][:, None] * shift_grad[k][None, :] for k in range(clips))

        def whole_rows(x):
            both = jnp.stack([x, hop_core(x)])
            return jnp.concatenate([pick(both, core), pick(both, 1 - core)])

        return (
            whole_rows(output),
            whole_rows(grad_latents),
            grad_query,
            grad_key,
            grad_value,
            grad_output.T,
            grad_cap_key,
            grad_cap_value,
            grad_gate,
            grad_up,
            grad_down.T,
            grad_modulation,
            g_query,
            g_key,
            g_cap,
            g_attn,
            g_ffn,
            g_cross,
        )

    return body


def solution(mesh):
    rows, cols, turned = P("seq", None), P("seq", "head"), P("head", "seq")
    one = P()
    placed = (rows, rows, one, one, one, cols, cols, cols, turned, cols, cols, cols, cols, turned)
    placed += (rows, one, one, one, one, one, P("head"), rows)
    given = (rows, rows, cols, cols, cols, turned, cols, cols, cols, cols, turned, rows)
    given += (one, one, one, one, one, P("head"))
    return jax.shard_map(
        make_body(mesh.shape["seq"]), mesh=mesh, in_specs=placed, out_specs=given, check_vma=False
    )
```

```python
import math

import jax
import jax.numpy as jnp
from jax import lax
from jax.experimental import pallas as pl
from jax.experimental.pallas import tpu as pltpu
from jax.sharding import PartitionSpec as P

TEXT = 256
FRAME = 385
GROUPS = 4
EPSILON = 1e-06
LOW = jnp.bfloat16
FULL = jnp.float32


def token_layout(clip_frames, valid_patches, ids):
    clips = clip_frames.shape[0]
    upto = jnp.arange(clips)[None, :] <= jnp.arange(clips)[:, None]
    ends = FRAME * jnp.sum(jnp.where(upto, clip_frames[None, :], 0), axis=1)
    starts = ends - FRAME * clip_frames
    clip = jnp.sum((ends[None, :] <= ids[:, None]).astype(jnp.int32), axis=1)
    chosen = (clip[:, None] == jnp.arange(clips, dtype=jnp.int32)[None, :]).astype(jnp.int32)
    position = ids - jnp.sum(chosen * starts[None, :], axis=1)
    within = position % FRAME
    limit = jnp.sum(chosen * valid_patches[None, :], axis=1)
    tag = jnp.where((within < limit) | (within == FRAME - 1), clip, -1)
    return clip, position, tag


def inverse_rms(values, axis=-1):
    return lax.rsqrt(jnp.mean(values * values, axis=axis, keepdims=True) + EPSILON)


def norm_back(raw, gain, grad, axis=-1):
    inverse = inverse_rms(raw, axis)
    unit = raw * inverse
    scaled = grad * gain
    back = inverse * (scaled - unit * jnp.mean(scaled * unit, axis=axis, keepdims=True))
    return back, grad * unit


def dot(left, right, contract=(1, 0)):
    dims = (((contract[0],), (contract[1],)), ((), ()))
    return lax.dot_general(left, right, dims, preferred_element_type=FULL)


def by_clip(table, clip):
    out = table[0][None]
    for k in range(1, table.shape[0]):
        out = jnp.where(clip[:, None] == k, table[k][None], out)
    return out


def clip_sums(values, clip, clips):
    return jnp.stack(
        [jnp.sum(jnp.where(clip[:, None] == k, values, 0.0), axis=0) for k in range(clips)]
    )


def xor_order(blocks, index):
    blocks = list(blocks)
    bit = 1
    while bit < len(blocks):
        on = (index & bit) != 0
        blocks = [jnp.where(on, blocks[j ^ bit], blocks[j]) for j in range(len(blocks))]
        bit *= 2
    return blocks


def pick(stack, index, axis=0):
    return lax.dynamic_index_in_dim(stack, index, axis, keepdims=False)


def low_round(x):
    return lax.reduce_precision(x, 8, 7)


def two_parts(x):
    upper = low_round(x)
    return jnp.stack([upper, low_round(x - upper)]).astype(LOW)


def two_round(x):
    upper = low_round(x)
    return upper + low_round(x - upper)


def one_part(x):
    return x[0].astype(FULL) + x[1].astype(FULL)


def chunk_of(keys):
    return 512 if keys % 512 == 0 else keys


def padded_bytes(shape, dtype):
    size = jnp.dtype(dtype).itemsize
    rows, lanes = (1,) * (2 - len(shape)) + tuple(shape[-2:])
    tile = 32 // size
    return math.prod(shape[:-2]) * (-(-rows // tile) * tile) * (-(-lanes // 128) * 128) * size


def kernel_call(body, ins, outs, scratch=(), scalars=-1):
    space, small = [pl.BlockSpec(memory_space=m) for m in (pltpu.VMEM, pltpu.SMEM)]
    held = sum(padded_bytes(x.shape, x.dtype) for x in (*ins, *outs))
    held += sum(padded_bytes(x.shape, x.dtype) for x in scratch)
    return pl.pallas_call(
        body,
        out_shape=outs,
        in_specs=[small if i == scalars else space for i in range(len(ins))],
        out_specs=[space] * len(outs),
        scratch_shapes=list(scratch),
        compiler_params=pltpu.CompilerParams(vmem_limit_bytes=min(held + (8 << 20), 56 << 20)),
        cost_estimate=pl.CostEstimate(flops=1000, bytes_accessed=1000, transcendentals=0),
    )(*ins)


def project(raw, gain_q, gain_k, cosine, sine, heads):
    hd = gain_q.shape[0]
    half, width, rows = hd // 2, heads * hd, raw.shape[1]
    scale = 1.0 / math.sqrt(hd)

    def body(raw_ref, gq_ref, gk_ref, cos_ref, sin_ref, q_ref, kv_ref):
        c, s = cos_ref[...], sin_ref[...]
        for part, gain_ref, out_ref in ((0, gq_ref, q_ref), (1, gk_ref, kv_ref)):
            for h in range(heads):
                u = raw_ref[pl.ds(part * width + h * hd, hd), :]
                n = u * inverse_rms(u, 0) * gain_ref[...]
                a, b = n[:half], n[half:]
                turned = jnp.concatenate([a * c - b * s, a * s + b * c], axis=0).astype(LOW)
                if part == 0:
                    turned = (turned.astype(FULL) * scale).astype(LOW)
                out_ref[pl.ds(h * hd, hd), :] = turned
        kv_ref[pl.ds(width, width), :] = raw_ref[pl.ds(2 * width, width), :].astype(LOW)

    outs = (jax.ShapeDtypeStruct((width, rows), LOW), jax.ShapeDtypeStruct((2 * width, rows), LOW))
    return kernel_call(body, (raw, gain_q, gain_k, cosine, sine), outs)


def row_sums(terms):
    wide = terms[:, :128]
    for at in range(128, terms.shape[1], 128):
        wide = wide + terms[:, at : at + 128]
    return jnp.sum(wide.T, axis=0, keepdims=True)


def project_back(raw, gain_q, gain_k, cosine, sine, heads, dqs, kv_near, kv_far, left, planes, groups):
    hd = gain_q.shape[0]
    half, width, rows = hd // 2, heads * hd, raw.shape[1]
    normed, mixed, *d_attended = left
    inner, features = planes.shape[0], normed.shape[1]
    piece = features // (inner * groups)
    n = len(dqs)
    lanes = features // 4

    def body(*refs):
        raw_ref, gq_ref, gk_ref, cos_ref, sin_ref = refs[:5]
        dq_refs, rest = refs[5 : 5 + n], refs[5 + n :]
        n_ref, f_ref, x_ref, m_ref, a_ref, b_ref, p_ref, out_ref, tq, tk, near_ref, far_ref, g_ref = rest
        c, s = cos_ref[...], sin_ref[...]
        for part, gain_ref, term_ref in ((0, gq_ref, tq), (1, gk_ref, tk)):
            terms = jnp.zeros((hd, rows), FULL)
            for h in range(heads):
                at = pl.ds(h * hd, hd)
                if part == 0:
                    grad = dq_refs[0][at, :]
                    for ref in dq_refs[1:]:
                        grad = grad + ref[at, :]
                else:
                    grad = n_ref[at, :] + f_ref[at, :].astype(FULL)
                x, y = grad[:half], grad[half:]
                grad = jnp.concatenate([x * c + y * s, y * c - x * s], axis=0)
                where = pl.ds(part * width + h * hd, hd)
                back, term = norm_back(raw_ref[where, :], gain_ref[...], grad, 0)
                out_ref[where, :] = back.astype(LOW)
                terms = terms + term
            term_ref[...] = row_sums(terms)
        at = pl.ds(width, width)
        out_ref[pl.ds(2 * width, width), :] = (n_ref[at, :] + f_ref[at, :].astype(FULL)).astype(LOW)
        turned = out_ref[...].T
        mix = m_ref[...].T
        for k in range(4):
            at = pl.ds(k * lanes, lanes)
            one = dot(x_ref[:, at], turned, (0, 0))
            two = dot(jnp.concatenate([a_ref[:, at], b_ref[:, at]], axis=0), mix, (0, 0))
            g_ref[at, :] = jnp.concatenate([one, two], axis=1)
        for j in range(inner):
            for g in range(groups):
                start = pl.multiple_of((g * inner + p_ref[j]) * piece, 8)
                block = g_ref[pl.ds(start, piece), :]
                if j < inner // 2:
                    near_ref[j * groups + g] = block
                else:
                    far_ref[(j - inner // 2) * groups + g] = block.astype(LOW)

    row = jax.ShapeDtypeStruct((1, hd), FULL)
    blocks = (inner * groups // 2, piece, 4 * width)
    outs = (jax.ShapeDtypeStruct((3 * width, rows), LOW), row, row)
    outs += (jax.ShapeDtypeStruct(blocks, FULL), jax.ShapeDtypeStruct(blocks, LOW))
    ins = (raw, gain_q, gain_k, cosine, sine, *dqs, kv_near, kv_far, normed, mixed, *d_attended, planes)
    scratch = [pltpu.VMEM((features, 4 * width), FULL)]
    return kernel_call(body, ins, outs, scratch, len(ins) - 1)


def place_columns(blocks, index, count):
    groups = len(blocks)
    rows, w = blocks[0].shape[0], blocks[0].shape[1] // count

    def body(index_ref, *refs):
        here = index_ref[0]
        block_refs, out_refs = refs[:groups], refs[groups:]
        for g in range(groups):
            for k in range(count):
                at = pl.ds(k * w, w)
                x = block_refs[0][:, at].astype(FULL)
                for t in range(1, groups):
                    x = jnp.where(here == (g ^ t), block_refs[t][:, at].astype(FULL), x)
                out_refs[k][:, pl.ds(g * w, w)] = x

    outs = [jax.ShapeDtypeStruct((rows, groups * w), FULL)] * count
    return kernel_call(body, (index.reshape(1), *blocks), outs, (), 0)


def project_caption(parts, gain, heads):
    hd = gain.shape[0]
    width, rows = heads * hd, parts[0].shape[0]

    def body(*refs):
        part_refs, gain_ref, out_ref, raw_ref = refs[:-3], refs[-3], refs[-2], refs[-1]
        total = part_refs[0][...]
        for ref in part_refs[1:]:
            total = total + ref[...].astype(FULL)
        total = total.T
        raw_ref[...] = total[:width]
        for h in range(heads):
            u = total[h * hd : (h + 1) * hd]
            out_ref[pl.ds(h * hd, hd), :] = (u * inverse_rms(u, 0) * gain_ref[...]).astype(LOW)
        out_ref[pl.ds(width, width), :] = total[width:].astype(LOW)

    outs = (jax.ShapeDtypeStruct((2 * width, rows), LOW), jax.ShapeDtypeStruct((width, rows), FULL))
    return kernel_call(body, (*parts, gain), outs)


def project_caption_back(raw, gain, heads, near, far):
    hd = gain.shape[0]
    width, rows = raw.shape

    def body(raw_ref, gain_ref, n_ref, f_ref, out_ref, term_ref):
        total = n_ref[...] + f_ref[...].astype(FULL)
        terms = jnp.zeros((hd, rows), FULL)
        for h in range(heads):
            at = slice(h * hd, (h + 1) * hd)
            back, term = norm_back(raw_ref[at, :], gain_ref[...], total[at], 0)
            out_ref[at, :] = back.astype(LOW)
            terms = terms + term
        term_ref[...] = (row_sums(terms) if rows % 128 == 0 else jnp.sum(terms.T, axis=0, keepdims=True))
        out_ref[width:, :] = total[width:].astype(LOW)

    outs = (jax.ShapeDtypeStruct((2 * width, rows), LOW), jax.ShapeDtypeStruct((1, hd), FULL))
    return kernel_call(body, (raw, gain, near, far), outs)


def attend(query, clip, kvs, tags, heads, gates=None, other=None):
    width, rows = query.shape
    hd = width // heads
    n = len(kvs)

    def body(*refs):
        q_ref, clip_ref = refs[:2]
        kv_refs, tag_refs = refs[2 : 2 + n], refs[2 + n : 2 + 2 * n]
        rest = refs[2 + 2 * n :]
        if gates is not None:
            gate_ref, other_ref, out_ref, inv_ref, mix_ref = rest
        else:
            out_ref, inv_ref = rest
        here = clip_ref[...]
        sums = [(jnp.zeros((1, rows), FULL), jnp.zeros((hd, rows), FULL)) for _ in range(heads)]
        for kv_ref, tag_ref in zip(kv_refs, tag_refs):
            count = chunk_of(kv_ref.shape[1])

            def chunk(i, carry):
                at = pl.ds(pl.multiple_of(i * count, count), count)
                allowed = tag_ref[at, :] == here
                out = []
                for h in range(heads):
                    total, acc = carry[h]
                    key = kv_ref[pl.ds(h * hd, hd), at]
                    value = kv_ref[pl.ds(width + h * hd, hd), at]
                    scores = dot(key, q_ref[pl.ds(h * hd, hd), :], (0, 0))
                    weights = jnp.where(allowed, jnp.exp(scores), 0.0)
                    total = total + jnp.sum(weights, axis=0, keepdims=True)
                    out.append((total, acc + dot(value, weights.astype(LOW))))
                return out

            sums = lax.fori_loop(0, kv_ref.shape[1] // count, chunk, sums)
        for h in range(heads):
            total, acc = sums[h]
            inverse = 1.0 / total
            inv_ref[pl.ds(h, 1), :] = inverse
            out_ref[pl.ds(h * hd, hd), :] = acc * inverse
            if gates is not None:
                own = pl.ds(h * hd, hd)
                mix_ref[own, :] = (other_ref[own, :] + gate_ref[own, :] * (acc * inverse)).astype(LOW)

    ins = (query, clip, *kvs, *tags)
    outs = (jax.ShapeDtypeStruct((width, rows), FULL), jax.ShapeDtypeStruct((heads, rows), FULL))
    if gates is not None:
        ins += (gates, other)
        outs += (jax.ShapeDtypeStruct((width, rows), LOW),)
    return kernel_call(body, ins, outs)


def attend_back(query, clip, kvs, tags, heads, inverse, grad, out, kind, gates=None):
    width, rows = query.shape
    hd = width // heads
    n = len(kvs)
    scale = 1.0 / math.sqrt(hd)

    def body(*refs):
        q_ref, clip_ref, inv_ref, given_ref, o_ref = refs[:5]
        kv_refs, tag_refs = refs[5 : 5 + n], refs[5 + n : 5 + 2 * n]
        here = clip_ref[...]
        if gates is None:
            dq_ref, back_refs = refs[5 + 2 * n], refs[6 + 2 * n :]
            grad_ref = given_ref
        else:
            gate_ref, dq_ref, back_refs = refs[5 + 2 * n], refs[6 + 2 * n], refs[7 + 2 * n :]
            back_refs, sum_ref, grad_ref = back_refs[:n], back_refs[n], back_refs[n + 1]
        deltas = []
        for h in range(heads):
            own = pl.ds(h * hd, hd)
            if gates is not None:
                given = given_ref[own, :].astype(FULL)
                grad_ref[own, :] = (gate_ref[own, :] * given).astype(LOW)
                sum_ref[pl.ds(h, 1), :] = jnp.sum(given * o_ref[own, :], axis=0, keepdims=True)
            terms = grad_ref[own, :].astype(FULL) * o_ref[own, :]
            deltas.append(jnp.sum(terms, axis=0, keepdims=True))
        sums = [jnp.zeros((hd, rows), FULL) for _ in range(heads)]
        for kv_ref, tag_ref, back_ref in zip(kv_refs, tag_refs, back_refs):
            count = chunk_of(kv_ref.shape[1])

            def chunk(i, carry):
                at = pl.ds(pl.multiple_of(i * count, count), count)
                allowed = tag_ref[at, :] == here
                out = []
                for h in range(heads):
                    own = pl.ds(h * hd, hd)
                    key = kv_ref[own, at]
                    value = kv_ref[pl.ds(width + h * hd, hd), at]
                    scores = dot(key, q_ref[own, :], (0, 0))
                    prob = jnp.where(allowed, jnp.exp(scores), 0.0) * inv_ref[pl.ds(h, 1), :]
                    d_prob = dot(value, grad_ref[own, :], (0, 0))
                    ds = (prob * (d_prob - deltas[h])).astype(LOW)
                    back_ref[own, at] = dot(q_ref[own, :], ds, (1, 1)).astype(back_ref.dtype)
                    back_ref[pl.ds(width + h * hd, hd), at] = dot(
                        grad_ref[own, :], prob.astype(LOW), (1, 1)
                    ).astype(back_ref.dtype)
                    out.append(carry[h] + dot(key, ds))
                return out

            sums = lax.fori_loop(0, kv_ref.shape[1] // count, chunk, sums)
        for h in range(heads):
            dq_ref[pl.ds(h * hd, hd), :] = sums[h] * scale

    outs = [jax.ShapeDtypeStruct((width, rows), FULL)]
    outs += [jax.ShapeDtypeStruct(x.shape, kind) for x in kvs]
    ins = (query, clip, inverse, grad, out, *kvs, *tags)
    scratch = []
    if gates is not None:
        ins += (gates,)
        outs.append(jax.ShapeDtypeStruct((heads, rows), FULL))
        scratch = [pltpu.VMEM((width, rows), LOW)]
    return kernel_call(body, ins, outs, scratch)


def assemble(near, far, slots):
    half, groups, piece, columns = near.shape

    def body(s_ref, a_ref, b_ref, out_ref):
        for q in range(2 * half):
            at = s_ref[q]

            @pl.when(at < half)
            def _():
                for g in range(groups):
                    out_ref[g, q] = a_ref[at, g]

            @pl.when(at >= half)
            def _():
                for g in range(groups):
                    out_ref[g, q] = b_ref[at - half, g]

    shape = (groups, 2 * half, piece, columns)
    (out,) = kernel_call(body, (slots, near, far), (jax.ShapeDtypeStruct(shape, near.dtype),), (), 0)
    return out.reshape(-1, columns)


def feed_forward(halves, d_ffn, weights):
    count, width = halves[0].shape
    hidden = weights.shape[1] // 3

    def body(a_ref, b_ref, d_ref, w_ref, act_ref, dgu_ref, near_ref, far_ref):
        for k, (x_ref, out_ref) in enumerate(((a_ref, near_ref), (b_ref, far_ref))):
            at = pl.ds(k * count, count)
            gate_up = w_ref[:, pl.ds(0, 2 * hidden)]
            both = dot(x_ref[...], gate_up)
            d_act = dot(d_ref[at, :], w_ref[:, pl.ds(2 * hidden, hidden)])
            gate, up = both[:, :hidden], both[:, hidden:]
            sigma = 1.0 / (1.0 + jnp.exp(-gate))
            act_ref[at, :] = (gate * sigma * up).astype(LOW)
            d_gate = (d_act * up * sigma * (1.0 + gate * (1.0 - sigma))).astype(LOW)
            dgu_ref[at, pl.ds(0, hidden)] = d_gate
            dgu_ref[at, pl.ds(hidden, hidden)] = (d_act * gate * sigma).astype(LOW)
            out_ref[...] = dot(dgu_ref[at, :], gate_up, (1, 1)).astype(out_ref.dtype)

    outs = (
        jax.ShapeDtypeStruct((2 * count, hidden), LOW),
        jax.ShapeDtypeStruct((2 * count, 2 * hidden), LOW),
        jax.ShapeDtypeStruct((count, width), FULL),
        jax.ShapeDtypeStruct((count, width), LOW),
    )
    return kernel_call(body, (*halves, d_ffn, weights), outs)


def feed_forward_grads(halves, d_ffn, weights, activation, d_gate_up, planes, groups):
    count, width = halves[0].shape
    hidden = activation.shape[1]
    inner = planes.shape[0]
    piece = width // (inner * groups)
    lanes = width // 4

    def body(a_ref, b_ref, d_ref, w_ref, act_ref, dgu_ref, p_ref, near_ref, far_ref, gn_ref, gf_ref, g_ref):
        for k, out_ref in enumerate((near_ref, far_ref)):
            at = pl.ds(k * count, count)
            out_ref[...] = dot(
                act_ref[at, :], w_ref[:, pl.ds(2 * hidden, hidden)], (1, 1)
            ).astype(out_ref.dtype)
        for k in range(4):
            at = pl.ds(k * lanes, lanes)
            x = jnp.concatenate([a_ref[:, at], b_ref[:, at]], axis=0)
            g_ref[at, pl.ds(0, 2 * hidden)] = dot(x, dgu_ref[...], (0, 0))
            g_ref[at, pl.ds(2 * hidden, hidden)] = dot(d_ref[:, at], act_ref[...], (0, 0))
        for j in range(inner):
            for g in range(groups):
                start = pl.multiple_of((g * inner + p_ref[j]) * piece, 8)
                block = g_ref[pl.ds(start, piece), :].astype(LOW)
                if j < inner // 2:
                    gn_ref[j * groups + g] = block
                else:
                    gf_ref[(j - inner // 2) * groups + g] = block

    blocks = jax.ShapeDtypeStruct((inner * groups // 2, piece, 3 * hidden), LOW)
    outs = (
        jax.ShapeDtypeStruct((count, width), FULL),
        jax.ShapeDtypeStruct((count, width), LOW),
        blocks,
        blocks,
    )
    ins = (*halves, d_ffn, weights, activation, d_gate_up, planes)
    return kernel_call(body, ins, outs, [pltpu.VMEM((width, 3 * hidden), FULL)], len(ins) - 1)


def normed_back(d_qkv, qkv, latents, clip, clips):
    rows, width = latents.shape
    half, lanes = rows // 2, width // 4

    def body(d_ref, w_ref, x_ref, c_ref, near_ref, far_ref, sum_ref):
        x = x_ref[...].astype(FULL)
        inverse = inverse_rms(x)
        turned = d_ref[...].T
        for k in range(4):
            at = pl.ds(k * lanes, lanes)
            part = dot(turned, w_ref[at, pl.ds(0, turned.shape[1])], (1, 1))
            near_ref[:, at] = part[:half]
            far_ref[:, at] = part[half:].astype(LOW)
            terms = part * (x_ref[:, at].astype(FULL) * inverse)
            for c in range(clips):
                picked = jnp.where(c_ref[...] == c, terms, 0.0)
                sum_ref[pl.ds(c, 1), at] = jnp.sum(picked, axis=0, keepdims=True)

    outs = (
        jax.ShapeDtypeStruct((half, width), FULL),
        jax.ShapeDtypeStruct((half, width), LOW),
        jax.ShapeDtypeStruct((clips, width), FULL),
    )
    return kernel_call(body, (d_qkv, qkv, latents, clip), outs)


def picked_sums(terms, column, clips, out_ref, first):
    for k, x in enumerate(terms):
        for c in range(clips):
            picked = jnp.where(column == c, x, 0.0)
            out_ref[pl.ds(first + k * clips + c, 1), :] = jnp.sum(picked, axis=0, keepdims=True)


def token_sums(d_hidden, attended, second, clip, clips):
    def body(h_ref, a_ref, s_ref, c_ref, out_ref):
        picked_sums((h_ref[...] * a_ref[...], s_ref[...]), c_ref[...], clips, out_ref, 0)

    outs = (jax.ShapeDtypeStruct((2 * clips, d_hidden.shape[1]), FULL),)
    return kernel_call(body, (d_hidden, attended, second, clip), outs)[0]


def layer_output(ffn_parts, upstream, hidden, ffn_tanh, clip, clips):
    n = len(ffn_parts)

    def body(*refs):
        up_ref, h_ref, t_ref, c_ref, out_ref, sum_ref = refs[n:]
        ffn_out = refs[0][...]
        for ref in refs[1:n]:
            ffn_out = ffn_out + ref[...].astype(FULL)
        out_ref[...] = (h_ref[...] + t_ref[...] * ffn_out).astype(LOW)
        picked_sums((up_ref[...] * ffn_out,), c_ref[...], clips, sum_ref, 0)

    outs = (
        jax.ShapeDtypeStruct(hidden.shape, LOW),
        jax.ShapeDtypeStruct((clips, hidden.shape[1]), FULL),
    )
    return kernel_call(body, (*ffn_parts, upstream, hidden, ffn_tanh, clip), outs)


def small_sums(sums, gains, gate_terms, gates, place):
    heads = gate_terms.shape[0]
    hd = gates.shape[0] // heads
    width = sums[0].shape[1]
    n = len(sums)
    rows = sum(x.shape[0] for x in sums) + len(gains) + 1
    padded = -(-rows // 8) * 8

    def body(p_ref, *refs):
        sum_refs, gain_refs, (gt_ref, gate_ref, out_ref) = refs[:n], refs[n:-3], refs[-3:]
        out_ref[...] = jnp.zeros_like(out_ref)
        at = 0
        for ref in sum_refs:
            for k in range(ref.shape[0]):
                out_ref[pl.ds(at, 1), :] = ref[pl.ds(k, 1), :]
                at += 1
        for ref in gain_refs:
            out_ref[pl.ds(at, 1), pl.ds(0, ref.shape[1])] = ref[...]
            at += 1
        lane = lax.broadcasted_iota(jnp.int32, (1, 128), 1)
        row = jnp.zeros((1, 128), FULL)
        for h in range(heads):
            total = jnp.sum(gt_ref[pl.ds(h, 1), :], axis=1, keepdims=True)
            gate = gate_ref[pl.ds(h * hd, 1), :]
            row = jnp.where(lane == p_ref[0] * heads + h, total * (1.0 - gate * gate), row)
        out_ref[pl.ds(at, 1), pl.ds(0, 128)] = row

    outs = (jax.ShapeDtypeStruct((padded, width), FULL),)
    return kernel_call(body, (place, *sums, *gains, gate_terms, gates), outs, (), 0)[0]


def make_body(seq_size):
    inner = seq_size // GROUPS
    steps = inner.bit_length() - 1

    def turned(j):
        return sum(((j >> i) & 1) << (steps - 1 - i) for i in range(steps))

    def hop_outer(x, t):
        pairs = [(i, ((i // inner) ^ t) * inner + i % inner) for i in range(seq_size)]
        return lax.ppermute(x, "seq", pairs)

    def hop_core(x):
        return lax.ppermute(x, "head", [(0, 1), (1, 0)])

    def hop_slot(x, j):
        pairs = []
        for at in range(seq_size):
            for head in range(2):
                to = (at // inner) * inner + ((at % inner) ^ (j if head == 0 else turned(j)))
                pairs.append((at * 2 + head, to * 2 + head))
        return lax.ppermute(x, ("seq", "head"), pairs)

    def hop_step(x, i):
        return hop_slot(x, 1 << i)

    def gather_outer(x):
        return [x] + [hop_outer(x, t) for t in range(1, GROUPS)]

    def body(
        latents,
        caption,
        conditioning,
        clip_frames,
        valid_patches,
        query_proj,
        key_proj,
        value_proj,
        output_proj,
        caption_key,
        caption_value,
        gate_proj,
        up_proj,
        down_proj,
        modulation,
        query_gain,
        key_gain,
        caption_gain,
        attn_gain,
        ffn_gain,
        cross_gate,
        cotangent,
    ):
        rows, width = latents.shape
        half = rows // 2
        hd = query_gain.shape[0]
        heads = cross_gate.shape[0] // GROUPS
        inner_width = heads * hd
        clips = conditioning.shape[0]
        scale = 1.0 / math.sqrt(hd)
        seq = lax.axis_index("seq")
        core = lax.axis_index("head")
        o, p = seq // inner, seq % inner
        group_rows = GROUPS * rows
        piece = query_proj.shape[0]
        planes = [p ^ jnp.where(core == 0, j, turned(j)) for j in range(inner)]
        fence = lax.optimization_barrier
        place_of = jnp.arange(inner)
        relative = p ^ place_of
        turned_relative = sum(((relative >> i) & 1) << (steps - 1 - i) for i in range(steps))
        slots = jnp.where(core == 0, relative, turned_relative).astype(jnp.int32)


        def plane_order(blocks):
            index = jnp.where(
                core == 0, p, sum(((p >> i) & 1) << (steps - 1 - i) for i in range(steps))
            )
            blocks = xor_order(blocks, index)
            return [
                b if turned(j) == j else jnp.where(core == 0, b, blocks[turned(j)])
                for j, b in enumerate(blocks)
            ]

        def token_ids(plane):
            c_at = core ^ jnp.arange(2)[:, None, None]
            o_at = o ^ jnp.arange(GROUPS)[None, :, None]
            at = jnp.arange(half)[None, None, :]
            return ((o_at * inner + plane) * rows + c_at * half + at).reshape(-1).astype(jnp.int32)

        ids = token_ids(p)
        key_ids = jnp.concatenate([token_ids(q) for q in planes])
        clip, position, _ = token_layout(clip_frames, valid_patches, ids)
        _, _, tag = token_layout(clip_frames, valid_patches, key_ids)
        own_clip = clip[:half]
        clip_row = clip[None, :]
        rates = 10000.0 ** (-(jnp.arange(hd // 2, dtype=FULL) * 2.0 / hd))
        angle = position.astype(FULL)[None, :] * rates[:, None]
        cosine, sine = jnp.cos(angle), jnp.sin(angle)

        own = lax.dynamic_slice_in_dim(latents, core * half, half, 0)
        own_cot = lax.dynamic_slice_in_dim(cotangent, core * half, half, 0)
        inputs = own.astype(FULL)
        upstream = own_cot.astype(FULL)

        def send_core(partial):
            split = partial.shape[0] // 2
            return partial[:split], hop_core(partial[split:].astype(LOW))

        def parts_of(near, far):
            parts = (near + far.astype(FULL)).reshape(GROUPS, half, width)
            return [parts[0]] + [parts[t].astype(LOW) for t in range(1, GROUPS)]

        def send_outer(near, far):
            return hops_outer(parts_of(near, far))

        def summed(parts):
            total = parts[0]
            for x in parts[1:]:
                total = total + x.astype(FULL)
            return total

        def hops_outer(blocks):
            return [hop_outer(x, t) if t else x for t, x in enumerate(blocks)]

        def hops_slot(blocks):
            return [hop_slot(x, t) if t else x for t, x in enumerate(blocks)]

        silu_cond = jax.nn.silu(conditioning.astype(FULL)).astype(LOW)
        cond_rows = modulation.shape[0]
        silu_own = lax.dynamic_slice_in_dim(silu_cond, seq * cond_rows, cond_rows, 1)
        shift_part = dot(silu_own, modulation)
        shift_shape = (2,) + shift_part.shape
        qkv_width = 3 * inner_width
        first_width = 4 * inner_width
        sent = []
        for t in range(GROUPS):
            at = (o ^ t) * inner_width
            cols = [
                lax.dynamic_slice_in_dim(w, at, inner_width, 1)
                for w in (query_proj, key_proj, value_proj)
            ]
            cols.append(lax.dynamic_slice_in_dim(output_proj, at, inner_width, 0).T)
            sent.append(jnp.concatenate(cols, axis=1))
        text_own = caption.shape[0]
        text_group = GROUPS * text_own
        cap_cols = caption.shape[1] // seq_size
        shift_rows = two_parts(shift_part).reshape(-1, GROUPS * cap_cols)
        sent, caption, shift_rows = fence((sent, caption, shift_rows))
        got = hops_outer(sent)
        cap_split = caption.reshape(text_own, GROUPS, inner, cap_cols)
        cap = hops_slot(
            [
                jnp.concatenate([pick(cap_split, q, 2).reshape(text_own, -1), shift_rows])
                for q in planes
            ]
        )
        split = key_ids.shape[0] // 2
        p_at = jnp.stack(planes)[:, None, None]
        o_at = jnp.arange(GROUPS)[None, :, None]
        text_ids = (o_at * inner + p_at) * text_own + jnp.arange(text_own)[None, None, :]
        columns = [
            tag[:split][:, None],
            tag[split:][:, None],
            (text_ids // TEXT).reshape(-1, 1).astype(jnp.int32),
            clip[:, None],
            own_clip[:, None],
            query_gain[:, None],
            key_gain[:, None],
            caption_gain[:, None],
        ]
        gate_here = pick(cross_gate.reshape(GROUPS, heads), o)
        gates = jnp.broadcast_to(jnp.tanh(gate_here)[:, None, None], (heads, hd, 1))
        gates = gates.reshape(inner_width, 1)
        got, cap, own, columns, gates, cosine, sine = fence(
            (got, cap, own, columns, gates, cosine, sine)
        )
        tag_columns, text_clip, clip_column, own_clip_column = columns[:2], *columns[2:5]
        gain_q, gain_k, gain_c = columns[5:]

        shift_parts = plane_order([one_part(x[text_own:].reshape(shift_shape)) for x in cap])
        shift_rows = two_parts(sum(shift_parts)).reshape(-1, cap_cols)
        stack = jnp.stack(xor_order(got, o))[None]
        cap = jnp.concatenate([x[:text_own] for x in cap])
        far = hop_step(stack, 0)
        cap_blocks = [
            lax.dynamic_slice_in_dim(cap, (o ^ t) * cap_cols, cap_cols, 1) for t in range(GROUPS)
        ]
        cap = hops_outer([jnp.concatenate([x, shift_rows]) for x in cap_blocks])
        stack, far, cap, own = fence((stack, far, cap, own))

        for i in range(1, steps):
            stack = jnp.concatenate([stack, far])
            far = hop_step(stack, i)
        near_latents = gather_outer(own)
        cap = xor_order(cap, o)
        text_part = inner * text_own
        shifts = sum([one_part(x[text_part:].reshape(shift_shape)) for x in cap])
        cap = [x[:text_part].reshape(inner, text_own, cap_cols) for x in cap]
        cap_mine = jnp.stack(cap, axis=1).reshape(inner * text_group, cap_cols)
        cap_part = jnp.concatenate([dot(cap_mine, caption_key), dot(cap_mine, caption_value)], 1)
        stack, far, near_latents, cap_part, cap_mine, own_cot = fence(
            (stack, far, near_latents, cap_part, cap_mine, own_cot)
        )

        near_cot = gather_outer(own_cot)
        near_latents = jnp.concatenate(near_latents)
        group_latents = fence(jnp.concatenate([near_latents, hop_core(near_latents)]))
        latents_f = group_latents.astype(FULL)
        stack = jnp.concatenate([stack, far])
        blocks = plane_order([stack[j] for j in range(inner)])
        first_weights = jnp.stack(blocks, axis=1).reshape(seq_size * piece, -1)
        qkv, out_t = first_weights[:, :qkv_width], first_weights[:, qkv_width:]
        scale_attn, gate_attn, scale_ffn, gate_ffn = [
            shifts[:, k * width : (k + 1) * width] for k in range(4)
        ]
        first_table = attn_gain * (1.0 + scale_attn)
        second_table = ffn_gain * (1.0 + scale_ffn)
        attn_tanh_table = jnp.tanh(gate_attn)
        ffn_tanh_table = jnp.tanh(gate_ffn)
        first_mult = by_clip(first_table, clip)
        normed = (latents_f * inverse_rms(latents_f) * first_mult).astype(LOW)
        raw = dot(qkv, normed, (0, 1))
        queries, both = project(raw, gain_q, gain_k, cosine, sine, heads)
        both, cap_part, queries, near_cot, gate_in, up_in, down_in = fence(
            (both, cap_part, queries, near_cot, gate_proj, up_proj, down_proj)
        )

        hidden_width = gate_proj.shape[1] // GROUPS
        late = []
        for t in range(GROUPS):
            at = (o ^ t) * hidden_width
            late.append(
                jnp.concatenate(
                    [
                        lax.dynamic_slice_in_dim(gate_in, at, hidden_width, 1),
                        lax.dynamic_slice_in_dim(up_in, at, hidden_width, 1),
                        lax.dynamic_slice_in_dim(down_in, at, hidden_width, 0).T,
                    ],
                    axis=1,
                )
            )
        late = hops_outer(late)
        for i in range(steps):
            far = hop_step(both, i)
            keep = cap_part.shape[0] // 2
            cap_far = hop_step(cap_part[keep:].astype(LOW), steps - 1 - i)
            if i == steps - 1:
                both, far, cap_part, cap_far, late = fence((both, far, cap_part, cap_far, late))
            else:
                both, far, cap_part, cap_far = fence((both, far, cap_part, cap_far))
            cap_part = cap_part[:keep] + cap_far.astype(FULL)
            if i < steps - 1:
                both = jnp.concatenate([both, far], axis=1)
        kvs = (both, far)
        tags = tuple(tag_columns)

        cap_sent = []
        for t in range(GROUPS):
            at = (o ^ t) * inner_width
            pair = [
                lax.dynamic_slice_in_dim(cap_part, half_at + at, inner_width, 1)
                for half_at in (0, GROUPS * inner_width)
            ]
            cap_sent.append(jnp.concatenate(pair, axis=1))
        cap_z = hops_outer([cap_sent[0]] + [x.astype(LOW) for x in cap_sent[1:]])
        late = jnp.stack(xor_order(late, o))[None]
        late_far = hop_step(late, 0)
        self_out, self_inv = attend(queries, clip_row, kvs, tags, heads)
        cap_z, self_out = fence((cap_z, self_out))

        cap_both, cap_key_raw = project_caption(cap_z, gain_c, heads)
        cap_both = [cap_both] + [hop_slot(cap_both, j) for j in range(1, inner)]
        cap_both, late, late_far = fence((cap_both, late, late_far))
        cap_both = jnp.concatenate(cap_both, axis=1)

        for i in range(1, steps):
            late = jnp.concatenate([late, late_far])
            late_far = hop_step(late, i)
        cross_out, cross_inv, mixed = attend(
            queries, clip_row, (cap_both,), (text_clip,), heads, gates, self_out
        )
        near, far = send_core(dot(mixed, out_t, (0, 1)))
        sent = fence(parts_of(near, far))

        attended_parts = hops_outer(sent)
        attended_parts, near_cot = fence((attended_parts, near_cot))

        attended = summed(attended_parts)
        attn_tanh = by_clip(attn_tanh_table, own_clip)
        hidden = inputs + attn_tanh * attended
        second_mult = by_clip(second_table, own_clip)
        ffn_own = (hidden * inverse_rms(hidden) * second_mult).astype(LOW)
        ffn_near = gather_outer(ffn_own)
        ffn_tanh = by_clip(ffn_tanh_table, own_clip)
        near_cot = jnp.concatenate(near_cot)
        group_cot = jnp.concatenate([near_cot, hop_core(near_cot)]).astype(FULL)
        d_ffn = (by_clip(ffn_tanh_table, clip) * group_cot).astype(LOW)
        late, late_far = fence((late, late_far))
        ffn_weights = assemble(late, late_far, slots)
        ffn_near, ffn_weights, d_ffn = fence((ffn_near, ffn_weights, d_ffn))

        ffn_near = jnp.concatenate(ffn_near)
        halves = (ffn_near, hop_core(ffn_near))
        activation, d_gate_up, near, far = feed_forward(halves, d_ffn, ffn_weights)
        sent, activation, d_gate_up = fence((parts_of(near, hop_core(far)), activation, d_gate_up))

        def slots_outer(parts):
            parts = parts.reshape(GROUPS, piece, -1)
            return hops_outer(
                [pick(parts, o)] + [pick(parts, o ^ t).astype(LOW) for t in range(1, GROUPS)]
            )

        d_ffn_parts = hops_outer(sent)
        plane_list = jnp.stack(planes).astype(jnp.int32)
        ffn_out_near, ffn_out_far, ffn_grads, grads_far = feed_forward_grads(
            halves, d_ffn, ffn_weights, activation, d_gate_up, plane_list, GROUPS
        )
        d_ffn_parts[1], ffn_out_near, ffn_out_far, ffn_grads, grads_far = fence(
            (d_ffn_parts[1], ffn_out_near, ffn_out_far, ffn_grads, grads_far)
        )
        ffn_grads = ffn_grads.reshape(-1, 3 * hidden_width)
        grads_far = hop_step(grads_far.reshape(ffn_grads.shape), steps - 1)
        for i in reversed(range(1, steps - 1)):
            ffn_grads = ffn_grads.astype(FULL) + grads_far.astype(FULL)
            keep = ffn_grads.shape[0] // 2
            grads_far = hop_step(ffn_grads[keep:].astype(LOW), i)
            ffn_grads = ffn_grads[:keep]
        d_ffn_parts = fence(d_ffn_parts)

        d_ffn_input = summed(d_ffn_parts)
        second_back, second_terms = norm_back(hidden, second_mult, d_ffn_input)
        d_hidden = upstream + second_back
        near, ffn_out_far = fence(((attn_tanh * d_hidden).astype(LOW), ffn_out_far))
        near = gather_outer(near)
        ffn_out_far = hop_core(ffn_out_far)
        near, ffn_grads, grads_far, ffn_out_far = fence((near, ffn_grads, grads_far, ffn_out_far))

        near = jnp.concatenate(near)
        d_attended = (near, hop_core(near))
        d_mixed = jnp.concatenate([dot(out_t, x, (0, 1)).astype(LOW) for x in d_attended], axis=1)
        d_mixed, ffn_out_near, ffn_out_far, ffn_grads, grads_far = fence(
            (d_mixed, ffn_out_near, ffn_out_far, ffn_grads, grads_far)
        )
        ffn_out_parts = send_outer(ffn_out_near, ffn_out_far)
        ffn_grads = ffn_grads.astype(FULL) + grads_far.astype(FULL)
        keep = ffn_grads.shape[0] // 2
        grads_far = hop_step(ffn_grads[keep:].astype(LOW), 0)
        dq_cross, cap_back, gate_terms = attend_back(
            queries,
            clip_row,
            (cap_both,),
            (text_clip,),
            heads,
            cross_inv,
            d_mixed,
            cross_out,
            FULL,
            gates,
        )
        cap_keep = cap_back.shape[1] // 2
        cap_far = hop_step(cap_back[:, cap_keep:].astype(LOW), steps - 1)
        dq_far, kv_far = attend_back(
            queries, clip_row, kvs[1:], tags[1:], heads, self_inv, d_mixed, self_out, LOW
        )
        kv_far, cap_back, cap_far, d_mixed, ffn_out_parts, ffn_grads, grads_far = fence(
            (kv_far, cap_back, cap_far, d_mixed, ffn_out_parts, ffn_grads, grads_far)
        )

        far = hop_step(kv_far, steps - 1)
        ffn_grads = ffn_grads[:keep] + grads_far.astype(FULL)
        ffn_blocks = slots_outer(ffn_grads)
        dq_near, kv_near = attend_back(
            queries, clip_row, kvs[:1], tags[:1], heads, self_inv, d_mixed, self_out, FULL
        )
        far, kv_near = fence((far, kv_near))

        ffn_out_parts, kv_near, second_terms = fence((ffn_out_parts, kv_near, second_terms))
        early_sums = token_sums(d_hidden, attended, second_terms, own_clip_column, clips)
        output, out_sums = layer_output(ffn_out_parts, upstream, hidden, ffn_tanh, own_clip_column, clips)
        cap_back = cap_back[:, :cap_keep] + cap_far.astype(FULL)
        for i in reversed(range(steps - 1)):
            kv_near = kv_near + far.astype(FULL)
            kv_keep = kv_near.shape[1] // 2
            far = hop_step(kv_near[:, kv_keep:].astype(LOW), i)
            cap_keep = cap_back.shape[1] // 2
            cap_far = hop_step(cap_back[:, cap_keep:].astype(LOW), i)
            kv_near = kv_near[:, :kv_keep]
            cap_back = cap_back[:, :cap_keep]
            if i:
                cap_back = cap_back + cap_far.astype(FULL)
        far, kv_near, cap_far, cap_back, out_sums, output, early_sums = fence(
            (far, kv_near, cap_far, cap_back, out_sums, output, early_sums)
        )

        d_qkv, query_terms, key_terms, attn_near, attn_far = project_back(
            raw,
            gain_q,
            gain_k,
            cosine,
            sine,
            heads,
            (dq_far, dq_near, dq_cross),
            kv_near,
            far,
            (normed, mixed, *d_attended),
            plane_list,
            GROUPS,
        )
        attn_near = attn_near.reshape(-1, first_width)
        attn_far = attn_far.reshape(-1, first_width)
        near, far, first_sums = normed_back(d_qkv, first_weights, group_latents, clip_column, clips)
        near, far, attn_far, gate_terms, first_sums, cap_back, ffn_blocks = fence(
            (near, far, attn_far, gate_terms, first_sums, cap_back, ffn_blocks)
        )
        d_cap, cap_terms = project_caption_back(cap_key_raw, gain_c, heads, cap_back, cap_far)

        place = (core * GROUPS + o).reshape(1).astype(jnp.int32)
        small = small_sums(
            (first_sums, early_sums, out_sums),
            (query_terms, key_terms, cap_terms),
            gate_terms,
            gates,
            place,
        )
        lanes = width // 2
        small = small.reshape(-1, 2, lanes)
        small = pick(small, core, 1) + hop_core(pick(small, 1 - core, 1))
        sent, attn_far, small, d_cap = fence((parts_of(near, hop_core(far)), attn_far, small, d_cap))

        def with_small(rows):
            return jnp.concatenate([rows, two_parts(small).reshape(-1, first_width)])

        attn_back = hop_step(with_small(attn_far), steps - 1)
        d_normed_parts = hops_outer(sent)
        d_cap_parts = gather_outer(d_cap)
        attn_near, attn_back, small, d_normed_parts, ffn_blocks = fence(
            (attn_near, attn_back, small, d_normed_parts, ffn_blocks)
        )

        count = attn_near.shape[0]
        attn_grads = attn_near + attn_back[:count].astype(FULL)
        small = two_round(small) + one_part(attn_back[count:].reshape((2,) + small.shape))
        for i in reversed(range(steps - 1)):
            keep = attn_grads.shape[0] // 2
            back = hop_step(with_small(attn_grads[keep:].astype(LOW)), i)
            attn_grads = attn_grads[:keep] + back[:keep].astype(FULL)
            small = two_round(small) + one_part(back[keep:].reshape((2,) + small.shape))
        attn_grads, small, d_cap_parts, ffn_blocks = fence(
            (attn_grads, small, d_cap_parts, ffn_blocks)
        )

        parts = attn_grads.reshape(GROUPS, piece, -1)
        attn_blocks = [pick(parts, o)]
        attn_blocks += [
            hop_outer(with_small(pick(parts, o ^ t).astype(LOW)), t) for t in range(1, GROUPS)
        ]
        smalls = [two_round(small)]
        smalls += [one_part(x[piece:].reshape((2,) + small.shape)) for x in attn_blocks[1:]]
        attn_blocks = attn_blocks[:1] + [x[:piece] for x in attn_blocks[1:]]
        small = sum(xor_order(smalls, o))
        both = jnp.stack([small, hop_core(small)])
        small = jnp.concatenate([pick(both, core), pick(both, 1 - core)], axis=1)
        d_cap = jnp.stack(xor_order(d_cap_parts, o)).reshape(GROUPS, 2, inner_width, text_group)
        d_cap = jnp.swapaxes(d_cap, 0, 1).reshape(2 * GROUPS * inner_width, text_group)
        d_cap_all = [d_cap] + [hop_slot(d_cap, j) for j in range(1, inner)]

        d_cap = jnp.concatenate(d_cap_all, axis=1)
        cap_width = caption_key.shape[1]
        grad_cap_key = dot(cap_mine, d_cap[:cap_width], (0, 1))
        grad_cap_value = dot(cap_mine, d_cap[cap_width:], (0, 1))

        grad_gate, grad_up, grad_down = place_columns(ffn_blocks, o, 3)
        grad_query, grad_key, grad_value, grad_output = place_columns(attn_blocks, o, 4)
        d_normed = summed(d_normed_parts)
        own_mult = by_clip(first_table, own_clip)
        first_back, _ = norm_back(inputs, own_mult, d_normed)
        grad_latents = (d_hidden + first_back).astype(LOW)

        first_sum, attended_sum, second_sum, out_sum = [
            small[k * clips : (k + 1) * clips] for k in range(4)
        ]
        g_query, g_key, g_cap = [small[4 * clips + k, :hd] for k in range(3)]
        g_cross = small[4 * clips + 3, : 2 * GROUPS * heads]
        g_attn = jnp.sum(first_sum * (1.0 + scale_attn), axis=0)
        g_ffn = jnp.sum(second_sum * (1.0 + scale_ffn), axis=0)
        shift_grad = jnp.concatenate(
            [
                first_sum * attn_gain,
                attended_sum * (1.0 - attn_tanh_table**2),
                second_sum * ffn_gain,
                out_sum * (1.0 - ffn_tanh_table**2),
            ],
            axis=1,
        )
        g_cross = pick(g_cross.reshape(2, -1), core)
        silu_f = silu_own.astype(FULL)
        grad_modulation = sum(silu_f[k][:, None] * shift_grad[k][None, :] for k in range(clips))

        def whole_rows(x):
            both = jnp.stack([x, hop_core(x)])
            return jnp.concatenate([pick(both, core), pick(both, 1 - core)])

        return (
            whole_rows(output),
            whole_rows(grad_latents),
            grad_query,
            grad_key,
            grad_value,
            grad_output.T,
            grad_cap_key,
            grad_cap_value,
            grad_gate,
            grad_up,
            grad_down.T,
            grad_modulation,
            g_query,
            g_key,
            g_cap,
            g_attn,
            g_ffn,
            g_cross,
        )

    return body


def solution(mesh):
    rows, cols, turned = P("seq", None), P("seq", "head"), P("head", "seq")
    one = P()
    placed = (rows, rows, one, one, one, cols, cols, cols, turned, cols, cols, cols, cols, turned)
    placed += (rows, one, one, one, one, one, P("head"), rows)
    given = (rows, rows, cols, cols, cols, turned, cols, cols, cols, cols, turned, rows)
    given += (one, one, one, one, one, P("head"))
    return jax.shard_map(
        make_body(mesh.shape["seq"]), mesh=mesh, in_specs=placed, out_specs=given, check_vma=False
    )
```
